32 devices in a mesh: section: 2 (over x), dp: 4 (over y, core), tensor: 4 (over z).
Axes of the slice: x: 2, y: 2, z: 4, core: 2. Of those that a mesh axis runs over, the one named last changes fastest.
Arguments:
- block_input: bfloat16 [4, 1024, 1024], P('dp'), may hold values from -6 to 6
- doc_ids: int32 [4, 1536], P('dp'), may hold values from 0 to 5, never falling along the last dimension, each value on 1 to 768 neighbouring positions
- memory: bfloat16 [2, 4, 512, 1024], P('section', 'dp'), may hold values from -6 to 6
- compressed: bfloat16 [2, 4, 512, 1024], P('section', 'dp'), may hold values from -6 to 6
- gain_attn: float32 [2, 1024], P('section'), may hold values from 0.1 to 1.9
- w_query: bfloat16 [2, 1024, 1024], P('section', None, 'tensor'), may hold values from -0.1875 to 0.1875
- w_key: bfloat16 [2, 1024, 1024], P('section', None, 'tensor'), may hold values from -0.1875 to 0.1875
- w_value: bfloat16 [2, 1024, 1024], P('section', None, 'tensor'), may hold values from -0.1875 to 0.1875
- w_out: bfloat16 [2, 1024, 1024], P('section', 'tensor'), may hold values from -1.5 to 1.5
- gain_ffn: float32 [2, 1024], P('section'), may hold values from 0.1 to 1.9
- w_up: bfloat16 [2, 1024, 4096], P('section', None, 'tensor'), may hold values from -0.1875 to 0.1875
- w_down: bfloat16 [2, 4096, 1024], P('section', 'tensor'), may hold values from -0.125 to 0.125
- w_compress: bfloat16 [2, 3, 1024, 1024], P('section', None, None, 'tensor'), may hold values from -0.109375 to 0.109375
- cotangent: bfloat16 [4, 1024, 1024], P('dp'), may hold values from -6 to 6
Outputs:
- layer_outputs: bfloat16 [2, 4, 1024, 1024], P('section', 'dp')
- input_grads: bfloat16 [2, 4, 1024, 1024], P('section', 'dp')
- grad_gain_attn: float32 [2, 1024], P('section', 'dp')
- grad_query: float32 [2, 1024, 1024], P('section', 'dp', 'tensor')
- grad_key: float32 [2, 1024, 1024], P('section', 'dp', 'tensor')
- grad_value: float32 [2, 1024, 1024], P('section', 'dp', 'tensor')
- grad_out: float32 [2, 1024, 1024], P('section', 'tensor', 'dp')
- grad_gain_ffn: float32 [2, 1024], P('section', 'dp')
- grad_up: float32 [2, 1024, 4096], P('section', 'dp', 'tensor')
- grad_down: float32 [2, 4096, 1024], P('section', 'tensor', 'dp')
- grad_compress: float32 [2, 3, 1024, 1024], P('section', None, 'dp', 'tensor')
The draws below stay inside these ranges and needn't reach their ends.
Inputs may be any that keep to these rules, and one draw needn't show every extreme that they name: `doc_ids`: along a sequence's history the ids never fall; each document covers 1 to 768 positions, one exactly 768.
All inputs are finite; a program needn't handle non-finite values.
Results may differ from the reference program's by a relative error of at most 0.03.
Values may be sent and summed in bfloat16 or wider, within the bound.
A program may use at most 192 MiB of HBM per device.

```python
import math
import jax
import jax.numpy as jnp
import numpy as np
from jax import lax

D = 1024
HEADS = 8
HD = 128
FF = 4096
SEG = 512
MEM = 512
CMEM = 512
RATE = 3
DOCS = 6
DOC_MOST = 768
LAYERS = 2
SEQ_TOKENS = 1024
TOTAL_SEQS = 4
COMP_ROWS = 171
PAD = 1
HISTORY = 1536


def shard_levels(own_key, extent, cuts, least, largest):
    level = 1.0
    for position, shards_of in cuts:
        heights = jax.random.uniform(jax.random.fold_in(jax.random.fold_in(own_key, 6), position), (shards_of,), jnp.float32, least / len(cuts), largest / len(cuts))
        level = level * jnp.repeat(jnp.exp(heights), extent[position] // shards_of).reshape((-1,) + (1,) * (len(extent) - 1 - position))
    return level


def length_profile(count, total, most, slope):
    weights = [(1 << 20) // math.isqrt(standing ** slope) + 1 for standing in range(2, count + 1)]
    surplus, given = total - most - (count - 1), [1] * (count - 1)
    while surplus > 0:
        candidates = [i for i in range(count - 1) if given[i] < most]
        whole, left = sum([weights[i] for i in candidates]), surplus
        for i in candidates:
            addition = min(most - given[i], max(1, left * weights[i] // whole), surplus)
            given[i] = given[i] + addition
            surplus = surplus - addition
    return np.array([most] + given)


def ragged_sizes(stream_key, number_of, total, reach, lean):
    if number_of == 2:
        one = jax.random.randint(stream_key, (), max(1, total - reach), min(reach, total - 1) + 1)
        return jnp.stack([one, total - one])
    lengths = jnp.asarray(length_profile(number_of, total, reach, lean), jnp.int32)
    couples = (number_of - 1) // 2
    giver, taker = lengths[1:1 + 2 * couples:2], lengths[2:2 + 2 * couples:2]
    room = jnp.minimum(giver - 1, reach - taker)
    passed = jax.random.randint(jax.random.fold_in(stream_key, 1), (couples,), 0, 1 << 20) % (room + 1)
    lengths = lengths.at[1:1 + 2 * couples:2].set(giver - passed).at[2:2 + 2 * couples:2].set(taker + passed)
    return lengths[jax.random.permutation(jax.random.fold_in(stream_key, 2), number_of)]


def noise(rng, extent, deviation, bound, cuts=(), held_as=jnp.bfloat16):
    result = deviation * jax.random.normal(rng, extent, jnp.float32)
    if cuts:
        result = result * shard_levels(rng, extent, cuts, -0.22, 0.18)
    return jnp.clip(result, -bound, bound).astype(held_as)


def setup_inputs(seed: int = 0) -> dict:
    arg_keys = jax.random.split(jax.random.key(seed), 15)
    return {
        "block_input": noise(arg_keys[0], (TOTAL_SEQS, SEQ_TOKENS, D), 1.0, 6.0, ((0, 4),)),
        "doc_ids": jax.vmap(lambda own: jnp.searchsorted(jnp.cumsum(ragged_sizes(own, DOCS, HISTORY, DOC_MOST, 2)), jnp.arange(HISTORY), side="right"))(jax.random.split(arg_keys[1], TOTAL_SEQS)).reshape((TOTAL_SEQS, HISTORY)).astype(jnp.int32),
        "memory": noise(arg_keys[2], (LAYERS, TOTAL_SEQS, MEM, D), 1.0, 6.0, ((0, 2), (1, 4))),
        "compressed": noise(arg_keys[3], (LAYERS, TOTAL_SEQS, CMEM, D), 1.0, 6.0, ((0, 2), (1, 4))),
        "gain_attn": jnp.clip(1.0 + 0.18 * jax.random.normal(arg_keys[4], (LAYERS, D), jnp.float32), 0.1, 1.9),
        "w_query": noise(arg_keys[5], (LAYERS, D, HEADS * HD), D ** -0.5, 0.1875, ((0, 2), (2, 4))),
        "w_key": noise(arg_keys[6], (LAYERS, D, HEADS * HD), D ** -0.5, 0.1875, ((0, 2), (2, 4))),
        "w_value": noise(arg_keys[7], (LAYERS, D, HEADS * HD), D ** -0.5, 0.1875, ((0, 2), (2, 4))),
        "w_out": noise(arg_keys[8], (LAYERS, HEADS * HD, D), 16 ** -0.5, 1.5, ((0, 2), (1, 4))),
        "gain_ffn": jnp.clip(1.0 + 0.18 * jax.random.normal(arg_keys[9], (LAYERS, D), jnp.float32), 0.1, 1.9),
        "w_up": noise(arg_keys[10], (LAYERS, D, FF), D ** -0.5, 0.1875, ((0, 2), (2, 4))),
        "w_down": noise(arg_keys[11], (LAYERS, FF, D), (FF // 2) ** -0.5, 0.125, ((0, 2), (1, 4))),
        "w_compress": noise(arg_keys[12], (LAYERS, RATE, D, D), (RATE * D) ** -0.5, 0.109375, ((0, 2), (3, 4))),
        "cotangent": noise(arg_keys[13], (TOTAL_SEQS, SEQ_TOKENS, D), 1.0, 6.0, ((0, 4),)),
    }


@jax.custom_vjp
def low(v):
    return lax.optimization_barrier(v.astype(jnp.bfloat16)).astype(jnp.float32)

@jax.custom_vjp
def low_back(v):
    return v

def low_keep(v):
    return (low(v), None)

def low_pass(kept, grad):
    return (grad,)

def back_keep(v):
    return (v, None)

def back_low(kept, grad):
    return (low(grad),)
low.defvjp(low_keep, low_pass)
low_back.defvjp(back_keep, back_low)
epsilon = 1e-06
masked_value = -1000000000.0

def matmul(left_side, right_side):
    return jnp.dot(left_side, right_side, precision=lax.Precision.HIGHEST, preferred_element_type=jnp.float32)

def normalize(row_block, gain_row):
    return row_block * lax.rsqrt(lax.optimization_barrier(jnp.mean(row_block * row_block, axis=-1, keepdims=True)) + epsilon) * gain_row

def attention_mask(key_docs, query_docs):
    key_place = jnp.concatenate([jnp.full((MEM,), -1, jnp.int32), jnp.arange(SEG, dtype=jnp.int32)])
    query_place = jnp.arange(SEG, dtype=jnp.int32)
    same_doc = key_docs[None, :] == query_docs[:, None]
    limited = same_doc & (key_place[None, :] <= query_place[:, None])
    return jnp.concatenate([jnp.ones((SEG, CMEM), bool), limited], axis=1)

def layer_segment(params, inputs, compressed_rows, memory_rows, key_docs, query_docs):
    gain_attn, w_query, w_key, w_value, w_out, gain_ffn, w_up, w_down = params
    inputs = low_back(inputs)
    stacked = jnp.concatenate([compressed_rows, memory_rows, inputs], axis=0)
    row_count = stacked.shape[0]
    normed = low(normalize(stacked, gain_attn))
    queries = low_back(low(matmul(normed[row_count - SEG:], w_query))).reshape(SEG, HEADS, HD)
    keys_proj = low_back(low(matmul(normed, w_key))).reshape(row_count, HEADS, HD)
    values_proj = low_back(low(matmul(normed, w_value))).reshape(row_count, HEADS, HD)
    scores = jnp.einsum('qhd,khd->hqk', queries, keys_proj, precision=lax.Precision.HIGHEST) * HD ** (-0.5)
    scores = low_back(scores)
    allowed = attention_mask(key_docs, query_docs)
    scores = jnp.where(allowed[None], scores, masked_value)
    attn_probs = jax.nn.softmax(scores, axis=-1)
    attended = jnp.einsum('hqk,khd->qhd', low(attn_probs), values_proj, precision=lax.Precision.HIGHEST)
    attended = low_back(low(attended))
    branch = low_back(matmul(attended.reshape(SEG, HEADS * HD), w_out))
    residual = inputs + branch
    normed_two = low(normalize(residual, gain_ffn))
    hidden_pre = low_back(matmul(normed_two, w_up))
    active = low(jax.nn.gelu(hidden_pre, approximate=True))
    feed_out = low_back(matmul(active, w_down))
    return low(residual + feed_out)

def layer_sequence(params, compress_weight, seq_input, seq_memory, seq_compressed, history, first_inputs):
    padded = jnp.concatenate([jnp.zeros((PAD, D), jnp.float32), seq_memory]).reshape(COMP_ROWS, RATE * D)
    fresh_rows = low_back(low(matmul(padded, compress_weight.reshape(RATE * D, D))))
    early = layer_segment(params, seq_input[:SEG], seq_compressed, seq_memory, history[:MEM + SEG], history[MEM:MEM + SEG])
    later_compressed = jnp.concatenate([seq_compressed[COMP_ROWS:], fresh_rows])
    later = layer_segment(params, seq_input[SEG:], later_compressed, first_inputs, history[MEM:MEM + 2 * SEG], history[MEM + SEG:MEM + 2 * SEG])
    return jnp.concatenate([early, later])

def run_layer(weights, layer_input, extras):
    seq_step = jax.checkpoint(lambda pieces: layer_sequence(weights[0], weights[1], *pieces))
    return lax.map(seq_step, (layer_input,) + extras)

def reference(block_input, doc_ids, memory, compressed, gain_attn, w_query, w_key, w_value, w_out, gain_ffn, w_up, w_down, w_compress, cotangent):
    current = block_input.astype(jnp.float32)
    pullbacks = []
    produced_all = []
    for layer_index in range(LAYERS):
        params = tuple((weight[layer_index].astype(jnp.float32) for weight in (gain_attn, w_query, w_key, w_value, w_out, gain_ffn, w_up, w_down)))
        compress_weight = w_compress[layer_index].astype(jnp.float32)
        extras = (memory[layer_index].astype(jnp.float32), compressed[layer_index].astype(jnp.float32), doc_ids, current[:, :SEG])
        produced, pullback = jax.vjp(lambda weights, layer_input: run_layer(weights, layer_input, extras), (params, compress_weight), current)
        pullbacks.append(pullback)
        produced_all.append(produced)
        current = produced
    grad_now = cotangent.astype(jnp.float32)
    input_grads = []
    weight_grads = []
    for layer_index in reversed(range(LAYERS)):
        weight_grad, grad_now = pullbacks[layer_index](grad_now)
        input_grads.insert(0, grad_now)
        weight_grads.insert(0, weight_grad)
    param_grads = [jnp.stack([grads[0][member] for grads in weight_grads]) for member in range(8)]
    compress_grad = jnp.stack([grads[1] for grads in weight_grads])
    return (jnp.stack(produced_all).astype(jnp.bfloat16), jnp.stack(input_grads).astype(jnp.bfloat16), param_grads[0], param_grads[1], param_grads[2], param_grads[3], param_grads[4], param_grads[5], param_grads[6], param_grads[7], compress_grad)
```

```python
import functools

import jax
import jax.numpy as jnp
from jax import lax
from jax.experimental import pallas as pl
from jax.experimental.pallas import tpu as pltpu
from jax.sharding import PartitionSpec as P

HD = 128
SEG = 512
MEM = 512
CMEM = 512
RATE = 3
COMP_ROWS = 171
PAD = 1
OLD_ROWS = CMEM - COMP_ROWS
CHUNKS = 4
ROWS = SEG // CHUNKS
FRESH_START = OLD_ROWS // 16 * 16

epsilon = 1e-06
masked_value = -1000000000.0
MESH = pl.DeviceIdType.MESH
f32 = jnp.float32
bf16 = jnp.bfloat16
GELU_A = 0.7978845608028654
GELU_B = 0.044715


def inverse_rms(rows):
    return lax.rsqrt(jnp.mean(rows * rows, axis=-1, keepdims=True) + epsilon)


def rms_pull(grad, rows, gain):
    scale = inverse_rms(rows)
    scaled_grad = grad * gain
    inner = jnp.mean(scaled_grad * rows, axis=-1, keepdims=True)
    return scale * (scaled_grad - rows * (scale * scale * inner))


def gelu(x):
    return 0.5 * x * (1.0 + jnp.tanh(GELU_A * (x + GELU_B * x * x * x)))


def gelu_slope(x):
    square = x * x
    bend = jnp.tanh(GELU_A * (x + GELU_B * x * square))
    return 0.5 * (1.0 + bend) + 0.5 * x * (1.0 - bend * bend) * GELU_A * (
        1.0 + 3.0 * GELU_B * square
    )


def dot_nn(a, b):
    return lax.dot_general(a, b, (((1,), (0,)), ((), ())), preferred_element_type=f32)


def dot_nt(a, b):
    return lax.dot_general(a, b, (((1,), (1,)), ((), ())), preferred_element_type=f32)


def dot_tn(a, b):
    return lax.dot_general(a, b, (((0,), (0,)), ((), ())), preferred_element_type=f32)


def greet(n, with_peer):
    me = lax.axis_index("tensor")
    barrier = pltpu.get_barrier_semaphore()
    for step in (-1, 1):
        other = me + step

        @pl.when((other >= 0) & (other < n))
        def _():
            pl.semaphore_signal(barrier, inc=1, device_id={"tensor": other}, device_id_type=MESH)

    if with_peer:
        peer = 1 - lax.axis_index("section")
        pl.semaphore_signal(barrier, inc=1, device_id={"section": peer}, device_id_type=MESH)
    extra = 1 if with_peer else 0
    pl.semaphore_wait(barrier, jnp.where((me > 0) & (me < n - 1), 2 + extra, 1 + extra))
    return me


class LineSum:
    def __init__(self, n, me, middle, part, out, held, sems):
        self.n, self.me, self.middle, self.part, self.out = n, me, middle, part, out
        self.from_left, self.from_right, self.to_right, self.to_left = held
        self.rs_send, self.rs_recv, self.ag_send, self.ag_recv = sems
        self.stages = 2 * n - 1

    def reduce_copy(self, src, landing, side, chunk, block, target):
        return pltpu.make_async_remote_copy(
            src_ref=src,
            dst_ref=landing.at[chunk, block],
            send_sem=self.rs_send.at[side, chunk, block],
            recv_sem=self.rs_recv.at[side, chunk, block],
            device_id={"tensor": target},
            device_id_type=MESH,
        )

    def gather_copy(self, side, chunk, block, target):
        return pltpu.make_async_remote_copy(
            src_ref=self.out.at[chunk, block],
            dst_ref=self.out.at[chunk, block],
            send_sem=self.ag_send.at[side, chunk, block],
            recv_sem=self.ag_recv.at[chunk, block],
            device_id={"tensor": target},
            device_id_type=MESH,
        )

    def put(self, chunk, rows):
        self.part[chunk] = rows.astype(bf16).reshape(self.part.shape[1:])

    def rows(self, chunk):
        whole = self.out[chunk]
        return whole.reshape(-1, whole.shape[-1])

    def stage(self, chunk, stage):
        n = self.n
        if stage == 0:
            self.first_sends(chunk)
        elif stage <= n - 2:
            self.hop(chunk, stage)
        elif stage == n - 1:
            self.own_rows(chunk)
        else:
            self.forward(chunk, stage - n + 1)

    def first_sends(self, chunk):
        n, part = self.n, self.part

        @pl.when(self.me == 0)
        def _():
            for block in range(n - 1, 0, -1):
                self.reduce_copy(
                    part.at[chunk, block], self.from_left, 0, chunk, block, 1
                ).start()

        @pl.when(self.me == n - 1)
        def _():
            for block in range(n - 1):
                self.reduce_copy(
                    part.at[chunk, block], self.from_right, 1, chunk, block, n - 2
                ).start()

    def hop(self, chunk, step):
        n, part = self.n, self.part

        @pl.when(self.me == step)
        def _():
            landing, sent = self.from_left, self.to_right
            for block in range(n - 1, step, -1):
                self.reduce_copy(
                    part.at[chunk, block], landing, 0, chunk, block, step
                ).wait_recv()
                sent[chunk, block] = (
                    landing[chunk, block].astype(f32) + part[chunk, block].astype(f32)
                ).astype(bf16)
                self.reduce_copy(
                    sent.at[chunk, block], landing, 0, chunk, block, step + 1
                ).start()

        @pl.when(self.me == n - 1 - step)
        def _():
            landing, sent = self.from_right, self.to_left
            mine = n - 1 - step
            for block in range(mine):
                self.reduce_copy(
                    part.at[chunk, block], landing, 1, chunk, block, mine
                ).wait_recv()
                sent[chunk, block] = (
                    landing[chunk, block].astype(f32) + part[chunk, block].astype(f32)
                ).astype(bf16)
                self.reduce_copy(
                    sent.at[chunk, block], landing, 1, chunk, block, mine - 1
                ).start()

    def own_rows(self, chunk):
        n, me, part = self.n, self.me, self.part

        @pl.when(me > 0)
        def _():
            self.reduce_copy(part.at[chunk, me], self.from_left, 0, chunk, me, me).wait_recv()

        @pl.when(me < n - 1)
        def _():
            self.reduce_copy(part.at[chunk, me], self.from_right, 1, chunk, me, me).wait_recv()

        total = part[chunk, me].astype(f32)
        total = total + jnp.where(me > 0, self.from_left[chunk, me].astype(f32), 0.0)
        total = total + jnp.where(me < n - 1, self.from_right[chunk, me].astype(f32), 0.0)
        self.out[chunk, me] = self.middle(chunk, me, total).astype(bf16)

        @pl.when(me < n - 1)
        def _():
            self.gather_copy(0, chunk, me, me + 1).start()

        @pl.when(me > 0)
        def _():
            self.gather_copy(1, chunk, me, me - 1).start()

    def forward(self, chunk, step):
        n, me = self.n, self.me
        left_block = me - step

        @pl.when(left_block >= 0)
        def _():
            self.gather_copy(0, chunk, left_block, me).wait_recv()

            @pl.when(me < n - 1)
            def _():
                self.gather_copy(0, chunk, left_block, me + 1).start()

        right_block = me + step

        @pl.when(right_block < n)
        def _():
            self.gather_copy(1, chunk, right_block, me).wait_recv()

            @pl.when(me > 0)
            def _():
                self.gather_copy(1, chunk, right_block, me - 1).start()

    def finish(self):
        n, me, part = self.n, self.me, self.part
        for chunk in range(part.shape[0]):
            for block in range(n):

                @pl.when((me < n - 1) & (block > me))
                def _():
                    self.reduce_copy(
                        part.at[chunk, block], self.from_left, 0, chunk, block, me
                    ).wait_send()

                @pl.when((me > 0) & (block < me))
                def _():
                    self.reduce_copy(
                        part.at[chunk, block], self.from_right, 1, chunk, block, me
                    ).wait_send()

                @pl.when((me < n - 1) & (block <= me))
                def _():
                    self.gather_copy(0, chunk, block, me).wait_send()

                @pl.when((me > 0) & (block >= me))
                def _():
                    self.gather_copy(1, chunk, block, me).wait_send()


def line_scratch(chunks, n, block, width):
    return [pltpu.VMEM((chunks, n, block, width), bf16)] * 5 + [
        pltpu.SemaphoreType.DMA((2, chunks, n)),
        pltpu.SemaphoreType.DMA((2, chunks, n)),
        pltpu.SemaphoreType.DMA((2, chunks, n)),
        pltpu.SemaphoreType.DMA((chunks, n)),
    ]


def make_line(n, me, middle, out, scratch):
    return LineSum(n, me, middle, scratch[0], out, scratch[1:5], scratch[5:9])


def run_two(order, first, second, produce, between, finished, extra):
    lag = first.stages - 1
    last = len(order) - 1
    for slot in range(2 * lag + last + 1):
        if slot <= last:
            produce(order[slot])
        for place, chunk in enumerate(order):
            stage = slot - lag - place
            if 1 <= stage <= lag:
                second.stage(chunk, stage)
            if stage == lag:
                finished(chunk)
        if slot > lag + last:
            extra(slot - lag - last)
        for place, chunk in enumerate(order):
            stage = slot - place
            if 0 <= stage <= lag:
                first.stage(chunk, stage)
        if 0 <= slot - lag <= last:
            chunk = order[slot - lag]
            between(chunk)
            second.stage(chunk, 0)


def score_columns(head, chunk, q_ref, kv_ref, docs, keys_docs):
    lanes = slice(head * HD, (head + 1) * HD)
    width = CMEM + MEM + (chunk + 1) * ROWS
    query = q_ref[chunk * ROWS : (chunk + 1) * ROWS, lanes]
    scores = dot_nt(kv_ref[:width, lanes], query) * HD ** (-0.5)
    own = docs[:, chunk * ROWS : (chunk + 1) * ROWS]
    same = keys_docs[: MEM + chunk * ROWS, :] == own
    tail_docs = keys_docs[MEM + chunk * ROWS : MEM + (chunk + 1) * ROWS, :]
    key_place = lax.broadcasted_iota(jnp.int32, (ROWS, ROWS), 0)
    query_place = lax.broadcasted_iota(jnp.int32, (ROWS, ROWS), 1)
    tail_same = (tail_docs == own) & (key_place <= query_place)
    middle_end = CMEM + MEM + chunk * ROWS
    return jnp.concatenate(
        [
            scores[:CMEM],
            jnp.where(same, scores[CMEM:middle_end], masked_value),
            jnp.where(tail_same, scores[middle_end:], masked_value),
        ],
        axis=0,
    )


def forward_kernel(n, ship, *refs):
    (c_ref, m_ref, x_ref, wq, wkv, wo, wup, wdown, gains, docs, key_docs) = refs[:11]
    (normed, q_ref, kv_ref, log_sum, attended, residual, two, hidden, active) = refs[11:20]
    out = refs[20]
    rest = refs[21:]
    if ship:
        shipped, rest = rest[0], rest[1:]
    keys_docs, values_t = rest[:2]
    first_scratch, second_scratch = rest[2:11], rest[11:20]
    if ship:
        ship_send, ship_recv = rest[20:22]
    me = greet(n, ship)
    section = lax.axis_index("section")
    heads = wq.shape[1] // HD
    local = wq.shape[1]

    keys_docs[...] = jnp.broadcast_to(key_docs[...], keys_docs.shape)
    gain_a = gains[0:1, :]
    gain_f = gains[1:2, :]

    def project_block(source, place):
        def body(step, carry):
            rows = pl.ds(pl.multiple_of(step * 256, 256), 256)
            at = pl.ds(pl.multiple_of(place * SEG + step * 256, 256), 256)
            wide = source[rows, :].astype(f32)
            block = (wide * inverse_rms(wide) * gain_a).astype(bf16)
            normed[at, :] = block
            both = dot_nn(block, wkv[...]).astype(bf16)
            kv_ref[at, :] = both
            if place == 2:
                q_ref[rows, :] = dot_nn(block, wq[...]).astype(bf16)
            return carry

        lax.fori_loop(0, SEG // 256, body, 0)

    project_block(c_ref, 0)
    project_block(m_ref, 1)
    x_rows = x_ref.reshape(SEG, x_ref.shape[-1])
    project_block(x_rows, 2)
    for head in range(heads):
        lanes = slice(local + head * HD, local + (head + 1) * HD)
        values_t[head] = kv_ref[:, lanes].astype(f32).T.astype(bf16)

    def attention_middle(chunk, me, total):
        rows = x_ref[chunk, me].astype(f32) + total
        residual[chunk] = rows
        return rows * inverse_rms(rows) * gain_f

    def output_middle(chunk, me, total):
        return residual[chunk] + total

    first = make_line(n, me, attention_middle, two, first_scratch)
    second = make_line(n, me, output_middle, out, second_scratch)

    def attend(chunk):
        rows = slice(chunk * ROWS, (chunk + 1) * ROWS)
        for head in range(heads):
            lanes = slice(head * HD, (head + 1) * HD)
            scores = score_columns(head, chunk, q_ref, kv_ref, docs, keys_docs)
            top = jnp.max(scores, axis=0, keepdims=True)
            powers = jnp.exp(scores - top)
            total = jnp.sum(powers, axis=0, keepdims=True)
            log_sum[head : head + 1, rows] = top + jnp.log(total)
            weights = (powers * (1.0 / total)).astype(bf16)
            mixed = dot_nn(values_t[head, :, : weights.shape[0]], weights)
            attended[rows, lanes] = mixed.T.astype(bf16)
        first.put(chunk, dot_nn(attended[rows, :], wo[...]))

    def feed(chunk):
        rows = slice(chunk * ROWS, (chunk + 1) * ROWS)
        before = dot_nn(first.rows(chunk), wup[...])
        hidden[rows, :] = before
        after = gelu(before).astype(bf16)
        active[rows, :] = after
        second.put(chunk, dot_nn(after, wdown[...]))

    def ship_copy(chunk):
        return pltpu.make_async_remote_copy(
            src_ref=out.at[chunk],
            dst_ref=shipped.at[chunk],
            send_sem=ship_send.at[chunk],
            recv_sem=ship_recv.at[chunk],
            device_id={"section": 1 - section},
            device_id_type=MESH,
        )

    def finished(chunk):
        if ship:

            @pl.when(section == 0)
            def _():
                ship_copy(chunk).start()

    run_two(list(range(CHUNKS)), first, second, attend, feed, finished, lambda step: None)
    first.finish()
    second.finish()
    if ship:
        for chunk in range(CHUNKS):

            @pl.when(section == 0)
            def _():
                ship_copy(chunk).wait_send()

            @pl.when(section == 1)
            def _():
                ship_copy(chunk).wait_recv()


def vmem_specs(count):
    return [pl.BlockSpec(memory_space=pltpu.VMEM)] * count


def forward_layer(collective, n, ship, c_rows, m_rows, x_rows, weights, gains, docs, key_docs):
    wq, wkv, wo, wup, wdown = weights
    width = x_rows.shape[1]
    local = wq.shape[1]
    hidden = wup.shape[1]
    block = ROWS // n
    shape = jax.ShapeDtypeStruct
    rows = shape((CHUNKS, n, block, width), bf16)
    outs = [
        shape((CMEM + MEM + SEG, width), bf16),
        shape((SEG, local), bf16),
        shape((CMEM + MEM + SEG, 2 * local), bf16),
        shape((8, SEG), f32),
        shape((SEG, local), bf16),
        shape((CHUNKS, block, width), f32),
        rows,
        shape((SEG, hidden), f32),
        shape((SEG, hidden), bf16),
        rows,
    ] + ([rows] if ship else [])
    result = pl.pallas_call(
        functools.partial(forward_kernel, n, ship),
        name="forward_ship" if ship else "forward_last",
        out_shape=outs,
        in_specs=vmem_specs(11),
        out_specs=vmem_specs(len(outs)),
        scratch_shapes=[
            pltpu.VMEM((MEM + SEG, HD), jnp.int32),
            pltpu.VMEM((local // HD, HD, CMEM + MEM + SEG), bf16),
        ]
        + line_scratch(CHUNKS, n, block, width)
        + line_scratch(CHUNKS, n, block, width)
        + ([pltpu.SemaphoreType.DMA((CHUNKS,))] * 2 if ship else []),
        compiler_params=pltpu.CompilerParams(
            collective_id=collective, has_side_effects=True, vmem_limit_bytes=60000 * 1024
        ),
    )(c_rows, m_rows, x_rows.reshape(CHUNKS, n, block, width), wq, wkv, wo, wup, wdown, gains,
      docs, key_docs)
    return result


def backward_kernel(n, *refs):
    (g_ref, x_ref, residual, hidden, fresh, wq, wkv, wo, wup, wdown, gains, q_ref, kv_ref,
     log_sum, docs, key_docs) = refs[:16]
    d_hidden, d_branch, dq_ref, dkv_ref, dx_ref, d_fresh = refs[16:22]
    d_residual, keys_docs, keys_t, sums = refs[22:26]
    first_scratch, second_scratch, fresh_scratch = refs[26:35], refs[35:44], refs[44:53]
    me = greet(n, False)
    late = lax.axis_index("section") == 1
    local = wq.shape[1]
    heads = local // HD
    gain_a = gains[0:1, :]
    gain_f = gains[1:2, :]
    scale = HD ** (-0.5)

    keys_docs[...] = jnp.broadcast_to(key_docs[...], keys_docs.shape)
    for head in range(heads):
        lanes = slice(head * HD, (head + 1) * HD)
        keys_t[head] = kv_ref[:, lanes].astype(f32).T.astype(bf16)

    def branch_middle(chunk, me, total):
        rows = g_ref[chunk, me].astype(f32) + rms_pull(total, residual[chunk], gain_f)
        d_residual[chunk] = rows
        return rows

    def input_middle(chunk, me, total):
        return d_residual[chunk] + rms_pull(total, x_ref[chunk, me].astype(f32), gain_a)

    def fresh_middle(chunk, me, total):
        return rms_pull(total, fresh[chunk, me].astype(f32), gain_a)

    first = make_line(n, me, branch_middle, d_branch, first_scratch)
    second = make_line(n, me, input_middle, dx_ref, second_scratch)
    third = make_line(n, me, fresh_middle, d_fresh, fresh_scratch)

    def produce(chunk):
        rows = slice(chunk * ROWS, (chunk + 1) * ROWS)
        grad = g_ref[chunk]
        d_active = dot_nt(grad.reshape(ROWS, grad.shape[-1]), wdown[...])
        block = (gelu_slope(hidden[rows, :]) * d_active).astype(bf16)
        d_hidden[rows, :] = block
        first.put(chunk, dot_nt(block, wup[...]))

    def attend_back(chunk):
        rows = slice(chunk * ROWS, (chunk + 1) * ROWS)
        d_attended = dot_nt(first.rows(chunk), wo[...]).astype(bf16)
        fresh_sum = chunk == CHUNKS - 1
        for head in range(heads):
            lanes = slice(head * HD, (head + 1) * HD)
            value_lanes = slice(local + head * HD, local + (head + 1) * HD)
            scores = score_columns(head, chunk, q_ref, kv_ref, docs, keys_docs)
            size = scores.shape[0]
            probs = jnp.exp(scores - log_sum[head : head + 1, rows])
            d_mixed = d_attended[:, lanes]
            d_values = dot_nn(probs.astype(bf16), d_mixed)
            d_probs = dot_nt(kv_ref[:size, value_lanes], d_mixed)
            inner = jnp.sum(d_probs * probs, axis=0, keepdims=True)
            d_scores = (probs * (d_probs - inner)).astype(bf16)
            d_keys = dot_nn(d_scores, q_ref[rows, lanes])
            d_queries = dot_nn(keys_t[head, :, :size], d_scores) * scale
            dq_ref[rows, lanes] = d_queries.T.astype(bf16)
            if fresh_sum:
                sums[:size, lanes] = d_keys
                sums[:size, value_lanes] = d_values
            else:
                sums[:size, lanes] += d_keys
                sums[:size, value_lanes] += d_values
        own = slice(CMEM + MEM + chunk * ROWS, CMEM + MEM + (chunk + 1) * ROWS)
        close_rows(own)
        second.put(
            chunk, dot_nt(dq_ref[rows, :], wq[...]) + dot_nt(dkv_ref[own, :], wkv[...])
        )
        if chunk == 0:
            close_rows(slice(0, CMEM + MEM))

            @pl.when(late)
            def _():
                count = third.part.shape[1] * third.part.shape[2]
                third.put(0, dot_nt(dkv_ref[FRESH_START : FRESH_START + count, :], wkv[...]))
                third.stage(0, 0)

    def close_rows(rows):
        dkv_ref[rows, :local] = (sums[rows, :local] * scale).astype(bf16)
        dkv_ref[rows, local:] = sums[rows, local:].astype(bf16)

    def extra(step):
        if step < third.stages:

            @pl.when(late)
            def _():
                third.stage(0, step)

    run_two(
        list(range(CHUNKS - 1, -1, -1)), first, second, produce, attend_back,
        lambda chunk: None, extra,
    )
    first.finish()
    second.finish()

    @pl.when(late)
    def _():
        third.finish()


def fresh_block(n):
    return -(-(CMEM - FRESH_START) // (16 * n)) * 16


def backward_layer(collective, n, grad, x_rows, residual, hidden, fresh, weights, gains, q, kv,
                   log_sum, docs, key_docs):
    wq, wkv, wo, wup, wdown = weights
    width = wo.shape[1]
    local = wq.shape[1]
    block = ROWS // n
    shape = jax.ShapeDtypeStruct
    rows = shape((CHUNKS, n, block, width), bf16)
    outs = [
        shape((SEG, wup.shape[1]), bf16),
        rows,
        shape((SEG, local), bf16),
        shape((CMEM + MEM + SEG, 2 * local), bf16),
        rows,
        shape((1, n, fresh_block(n), width), bf16),
    ]
    return pl.pallas_call(
        functools.partial(backward_kernel, n),
        name="backward",
        out_shape=outs,
        in_specs=vmem_specs(16),
        out_specs=vmem_specs(len(outs)),
        scratch_shapes=[
            pltpu.VMEM((CHUNKS, block, width), f32),
            pltpu.VMEM((MEM + SEG, HD), jnp.int32),
            pltpu.VMEM((local // HD, HD, CMEM + MEM + SEG), bf16),
            pltpu.VMEM((CMEM + MEM + SEG, 2 * local), f32),
        ]
        + line_scratch(CHUNKS, n, block, width)
        + line_scratch(CHUNKS, n, block, width)
        + line_scratch(1, n, fresh_block(n), width),
        compiler_params=pltpu.CompilerParams(
            collective_id=collective, has_side_effects=True, vmem_limit_bytes=60000 * 1024
        ),
    )(grad.reshape(rows.shape), x_rows.reshape(rows.shape), residual, hidden, fresh,
      wq, wkv, wo, wup, wdown, gains, q, kv, log_sum, docs, key_docs)


def gather_kernel(n, x_ref, out, send, recv):
    me = greet(n, False)

    def copy(side, block, target):
        return pltpu.make_async_remote_copy(
            src_ref=out.at[block],
            dst_ref=out.at[block],
            send_sem=send.at[side, block],
            recv_sem=recv.at[block],
            device_id={"tensor": target},
            device_id_type=MESH,
        )

    out[me] = x_ref[...]

    @pl.when(me < n - 1)
    def _():
        copy(0, me, me + 1).start()

    @pl.when(me > 0)
    def _():
        copy(1, me, me - 1).start()

    for step in range(1, n):
        left_block = me - step

        @pl.when(left_block >= 0)
        def _():
            copy(0, left_block, me).wait_recv()

            @pl.when(me < n - 1)
            def _():
                copy(0, left_block, me + 1).start()

        right_block = me + step

        @pl.when(right_block < n)
        def _():
            copy(1, right_block, me).wait_recv()

            @pl.when(me > 0)
            def _():
                copy(1, right_block, me - 1).start()

    for block in range(n):

        @pl.when((me < n - 1) & (block <= me))
        def _():
            copy(0, block, me).wait_send()

        @pl.when((me > 0) & (block >= me))
        def _():
            copy(1, block, me).wait_send()


def gather_line(name, collective, n, x):
    return pl.pallas_call(
        functools.partial(gather_kernel, n),
        name=name,
        out_shape=jax.ShapeDtypeStruct((n,) + x.shape, x.dtype),
        in_specs=vmem_specs(1),
        out_specs=pl.BlockSpec(memory_space=pltpu.VMEM),
        scratch_shapes=[pltpu.SemaphoreType.DMA((2, n)), pltpu.SemaphoreType.DMA((n,))],
        compiler_params=pltpu.CompilerParams(collective_id=collective, has_side_effects=True),
    )(x)


def project(rows, weight):
    return jnp.dot(rows, weight, preferred_element_type=f32).astype(bf16)


def shards(
    block_input,
    doc_ids,
    memory,
    compressed,
    gain_attn,
    w_query,
    w_key,
    w_value,
    w_out,
    gain_ffn,
    w_up,
    w_down,
    w_compress,
    cotangent,
):
    section = lax.axis_index("section")
    first = section == 0
    n = lax.axis_size("tensor")
    groups = lax.axis_size("dp")
    tensor_index = lax.axis_index("tensor")
    dp_index = lax.axis_index("dp")
    width = block_input.shape[2]
    local = w_query.shape[2]
    both = [(0, 1), (1, 0)]
    forth, back = [(0, 1)], [(1, 0)]

    core = dp_index % 2
    row = dp_index // 2
    rows_y = groups // 2
    core_pairs = [(i, i ^ 1) for i in range(groups)]

    def row_pairs(step):
        return [(i, (i + 2 * step) % groups) for i in range(groups)]

    def swap_weight(weight):
        rows = weight.shape[0] // groups
        piece = lax.dynamic_slice_in_dim(weight, dp_index * rows, rows, 0)
        piece = lax.ppermute(piece, "section", both)
        partner = lax.ppermute(piece, "dp", core_pairs)
        pair = jnp.where(
            core == 0,
            jnp.concatenate([piece, partner]),
            jnp.concatenate([partner, piece]),
        )
        whole = jnp.zeros(weight.shape, weight.dtype)
        whole = lax.dynamic_update_slice_in_dim(whole, pair, row * 2 * rows, 0)
        for step in range(1, rows_y):
            other = lax.ppermute(pair, "dp", row_pairs(step))
            place = (row - step) % rows_y
            whole = lax.dynamic_update_slice_in_dim(whole, other, place * 2 * rows, 0)
        return whole

    def scatter_rows(array):
        blocks = array.reshape(rows_y, 2, width // groups, array.shape[1])
        kept = lax.dynamic_index_in_dim(blocks, core, 1, keepdims=False)
        sent = lax.dynamic_index_in_dim(blocks, 1 - core, 1, keepdims=False)
        kept = (kept.astype(f32) + lax.ppermute(sent, "dp", core_pairs).astype(f32)).astype(bf16)
        total = lax.dynamic_index_in_dim(kept, row, 0, keepdims=False).astype(f32)
        for step in range(1, rows_y):
            sent = lax.dynamic_index_in_dim(kept, (row + step) % rows_y, 0, keepdims=False)
            total = total + lax.ppermute(sent, "dp", row_pairs(step)).astype(f32)
        return total

    def by_layer(own, other):
        return [jnp.where(first, own, other), jnp.where(first, other, own)]

    gains = jnp.stack([gain_attn[0], gain_ffn[0]])
    gains_other = lax.ppermute(gains, "section", both)
    gains_by_layer = by_layer(gains, gains_other)

    own_weights = (
        w_query[0], jnp.concatenate([w_key[0], w_value[0]], axis=1), w_out[0], w_up[0], w_down[0],
    )
    weight_layers = list(
        zip(*[by_layer(weight, swap_weight(weight)) for weight in own_weights])
    )

    history = doc_ids[0]
    memory_docs = lax.dynamic_slice_in_dim(history, section * SEG, MEM, 0)
    token_docs = lax.dynamic_slice_in_dim(history, MEM + section * SEG, SEG, 0)
    docs = token_docs[None]
    key_docs = jnp.concatenate([memory_docs, token_docs])[:, None]
    early, later = block_input[0, :SEG], block_input[0, SEG:]
    grad_now = lax.dynamic_slice_in_dim(cotangent[0], section * SEG, SEG, 0)

    padded = jnp.concatenate([jnp.zeros((PAD, width), bf16), memory[0, 0]]).reshape(
        COMP_ROWS, RATE * width
    )
    fresh_piece = project(padded, w_compress[0].reshape(RATE * width, local))
    fresh = gather_line("gather_fresh", 8, n, fresh_piece)
    fresh = fresh.transpose(1, 0, 2).reshape(COMP_ROWS, width)
    late_rows = jnp.concatenate([compressed[0, 0, COMP_ROWS:], fresh])
    sent_rows = lax.ppermute(jnp.where(first, late_rows, compressed[0, 0]), "section", both)
    sent_memory = lax.ppermute(memory[0, 0], "section", back)
    c_rows = [
        jnp.where(first, compressed[0, 0], sent_rows), jnp.where(first, sent_rows, late_rows),
    ]

    saved = []
    outputs = []
    tokens = jnp.where(first, early, later)
    m_rows = jnp.where(first, memory[0, 0], early)
    for layer in range(2):
        result = forward_layer(
            1 + layer, n, layer == 0, c_rows[layer], m_rows, tokens, weight_layers[layer],
            gains_by_layer[layer], docs, key_docs,
        )
        normed, queries, kv, log_total, attended, residual, two, hidden, active, out = result[:10]
        saved.append((tokens, m_rows, normed, queries, kv, log_total, attended, residual,
                      two.reshape(SEG, width), hidden, active))
        tokens = out.reshape(SEG, width)
        outputs.append(tokens)
        if layer == 0:
            m_rows = jnp.where(first, sent_memory, result[10].reshape(SEG, width))

    grads = [None, None]
    input_grads = [None, None]
    fresh_grads = [None, None]
    for layer in (1, 0):
        (tokens, m_rows, normed, queries, kv, log_total, attended, residual, two, hidden,
         active) = saved[layer]
        block = fresh_block(n)
        fresh_rows = jnp.concatenate(
            [c_rows[layer][FRESH_START:], m_rows[: n * block - (CMEM - FRESH_START)]]
        ).reshape(1, n, block, width)
        d_hidden, d_branch, dq, dkv, dx, d_fresh = backward_layer(
            4, n, grad_now, tokens, residual, hidden, fresh_rows, weight_layers[layer],
            gains_by_layer[layer], queries, kv, log_total, docs, key_docs,
        )
        d_branch = d_branch.reshape(SEG, width)
        grad = jnp.concatenate(
            [
                dot_tn(normed[CMEM + MEM :], dq).astype(bf16),
                dot_tn(normed, dkv).astype(bf16),
                dot_tn(d_branch, attended).astype(bf16),
                dot_tn(two, d_hidden).astype(bf16),
                dot_tn(grad_now, active).astype(bf16),
            ],
            axis=1,
        )
        grad_now = dx.reshape(SEG, width)
        input_grads[layer] = grad_now
        share = scatter_rows(grad)
        grads[layer] = (
            share, lax.ppermute(share.astype(bf16), "section", forth if layer == 1 else back)
        )
        skip = OLD_ROWS - FRESH_START
        d_fresh = d_fresh.reshape(n * block, width)[skip : skip + COMP_ROWS]
        fresh_grads[layer] = lax.dynamic_slice_in_dim(d_fresh, tensor_index * local, local, 1)

    d_fresh = jnp.where(
        first, lax.ppermute(fresh_grads[0], "section", back), fresh_grads[1]
    )
    grad_compress = dot_tn(padded, d_fresh).astype(bf16)
    compress_share = scatter_rows(
        jnp.concatenate(
            [grad_compress[place * width : (place + 1) * width] for place in range(RATE)], axis=1
        )
    )
    share = jnp.where(first, grads[0][0], grads[1][0]) + jnp.where(
        first, grads[0][1], grads[1][1]
    ).astype(f32)
    rows = width // groups
    up_local = w_up.shape[2]
    qkv_share = share[:, : 3 * local]
    out_share = share[:, 3 * local : 4 * local]
    up_share = share[:, 4 * local : 4 * local + up_local]
    down_share = share[:, 4 * local + up_local :]
    compress_share = compress_share.reshape(rows, RATE, local)

    def my_rows(weight):
        return lax.dynamic_slice_in_dim(weight, dp_index * rows, rows, 0).astype(f32)

    my_qkv = jnp.concatenate([my_rows(w_query[0]), my_rows(w_key[0]), my_rows(w_value[0])], axis=1)
    sums = jnp.stack(
        [jnp.sum(my_qkv * qkv_share, axis=1), jnp.sum(my_rows(w_up[0]) * up_share, axis=1)]
    )
    my_gains = lax.dynamic_slice_in_dim(gains, dp_index * rows, rows, 1)
    sums = gather_line("gather_sums", 9, n, jnp.pad(sums, ((0, 6), (0, 0))))
    gain_grads = jnp.sum(sums, axis=0)[:2] / my_gains

    return (
        assemble(outputs, first),
        assemble(input_grads, first),
        gain_grads[:1],
        qkv_share[None, :, :local],
        qkv_share[None, :, local : 2 * local],
        qkv_share[None, :, 2 * local :],
        out_share.T[None],
        gain_grads[1:],
        up_share[None],
        down_share.T[None],
        compress_share.transpose(1, 0, 2)[None],
    )


def assemble(pieces, first):
    own = jnp.where(first, pieces[0], pieces[1])
    other = lax.ppermute(
        jnp.where(first, pieces[1], pieces[0]), "section", [(0, 1), (1, 0)]
    )
    return jnp.concatenate(
        [jnp.where(first, own, other), jnp.where(first, other, own)]
    )[None, None]


def solution(mesh):
    return jax.shard_map(
        shards,
        mesh=mesh,
        in_specs=(
            P("dp", None, None),
            P("dp", None),
            P("section", "dp", None, None),
            P("section", "dp", None, None),
            P("section", None),
            P("section", None, "tensor"),
            P("section", None, "tensor"),
            P("section", None, "tensor"),
            P("section", "tensor", None),
            P("section", None),
            P("section", None, "tensor"),
            P("section", "tensor", None),
            P("section", None, None, "tensor"),
            P("dp", None, None),
        ),
        out_specs=(
            P("section", "dp", None, None),
            P("section", "dp", None, None),
            P("section", "dp"),
            P("section", "dp", "tensor"),
            P("section", "dp", "tensor"),
            P("section", "dp", "tensor"),
            P("section", "tensor", "dp"),
            P("section", "dp"),
            P("section", "dp", "tensor"),
            P("section", "tensor", "dp"),
            P("section", None, "dp", "tensor"),
        ),
        check_vma=False,
    )
```

```python
import functools

import jax
import jax.numpy as jnp
from jax import lax
from jax.experimental import pallas as pl
from jax.experimental.pallas import tpu as pltpu
from jax.sharding import PartitionSpec as P

HD = 128
SEG = 512
MEM = 512
CMEM = 512
RATE = 3
COMP_ROWS = 171
PAD = 1
OLD_ROWS = CMEM - COMP_ROWS
CHUNKS = 4
ROWS = SEG // CHUNKS
FRESH_START = OLD_ROWS // 16 * 16

epsilon = 1e-06
masked_value = -1000000000.0
MESH = pl.DeviceIdType.MESH
f32 = jnp.float32
bf16 = jnp.bfloat16
GELU_A = 0.7978845608028654
GELU_B = 0.044715


def inverse_rms(rows):
    return lax.rsqrt(jnp.mean(rows * rows, axis=-1, keepdims=True) + epsilon)


def rms_pull(grad, rows, gain):
    scale = inverse_rms(rows)
    scaled_grad = grad * gain
    inner = jnp.mean(scaled_grad * rows, axis=-1, keepdims=True)
    return scale * (scaled_grad - rows * (scale * scale * inner))


def gelu(x):
    return 0.5 * x * (1.0 + jnp.tanh(GELU_A * (x + GELU_B * x * x * x)))


def gelu_slope(x):
    square = x * x
    bend = jnp.tanh(GELU_A * (x + GELU_B * x * square))
    return 0.5 * (1.0 + bend) + 0.5 * x * (1.0 - bend * bend) * GELU_A * (
        1.0 + 3.0 * GELU_B * square
    )


def dot_nn(a, b):
    return lax.dot_general(a, b, (((1,), (0,)), ((), ())), preferred_element_type=f32)


def dot_nt(a, b):
    return lax.dot_general(a, b, (((1,), (1,)), ((), ())), preferred_element_type=f32)


def dot_tn(a, b):
    return lax.dot_general(a, b, (((0,), (0,)), ((), ())), preferred_element_type=f32)


def greet(n, with_peer=False, groups=0):
    me = lax.axis_index("tensor")
    barrier = pltpu.get_barrier_semaphore()
    for step in (-1, 1):
        other = me + step

        @pl.when((other >= 0) & (other < n))
        def _():
            pl.semaphore_signal(barrier, inc=1, device_id={"tensor": other}, device_id_type=MESH)

    extra = 0
    if with_peer:
        extra += 1
        peer = 1 - lax.axis_index("section")
        pl.semaphore_signal(barrier, inc=1, device_id={"section": peer}, device_id_type=MESH)
    if groups:
        mine = lax.axis_index("dp")
        others = [mine + 1 - 2 * (mine % 2)]
        others += [(mine + 2 * step) % groups for step in range(1, groups // 2)]
        for other in others:
            pl.semaphore_signal(barrier, inc=1, device_id={"dp": other}, device_id_type=MESH)
        extra += len(others)
    pl.semaphore_wait(barrier, jnp.where((me > 0) & (me < n - 1), 2 + extra, 1 + extra))
    return me


class GridSum:
    def __init__(self, groups, home, tiles, landings, sems, parts):
        self.groups, self.home, self.tiles, self.parts = groups, home, tiles, parts
        self.from_core, self.from_row, self.from_section = landings
        self.core_sems, self.row_sems, self.section_sems = sems
        self.dp = lax.axis_index("dp")
        self.section = lax.axis_index("section")
        self.core = self.dp % 2
        self.row = self.dp // 2
        self.rows = groups // 2

    def span(self, part):
        start, stop = self.parts[part]
        return pl.ds(start, stop - start)

    def core_copy(self, part, row):
        return pltpu.make_async_remote_copy(
            src_ref=self.tiles.at[row * 2 + 1 - self.core, self.span(part)],
            dst_ref=self.from_core.at[row, self.span(part)],
            send_sem=self.core_sems.at[0, part, row],
            recv_sem=self.core_sems.at[1, part, row],
            device_id={"dp": self.dp + 1 - 2 * self.core},
            device_id_type=MESH,
        )

    def row_copy(self, part, step):
        target = (self.row + step) % self.rows
        return pltpu.make_async_remote_copy(
            src_ref=self.tiles.at[target * 2 + self.core, self.span(part)],
            dst_ref=self.from_row.at[step - 1, self.span(part)],
            send_sem=self.row_sems.at[0, part, step - 1],
            recv_sem=self.row_sems.at[1, part, step - 1],
            device_id={"dp": target * 2 + self.core},
            device_id_type=MESH,
        )

    def section_copy(self, part):
        return pltpu.make_async_remote_copy(
            src_ref=self.tiles.at[self.dp, self.span(part)],
            dst_ref=self.from_section.at[self.span(part)],
            send_sem=self.section_sems.at[0, part],
            recv_sem=self.section_sems.at[1, part],
            device_id={"section": 1 - self.section},
            device_id_type=MESH,
        )

    def add(self, place, landing, part):
        start, stop = self.parts[part]

        def body(tile, carry):
            self.tiles[place, tile] = (
                self.tiles[place, tile].astype(f32) + landing[tile].astype(f32)
            ).astype(bf16)
            return carry

        lax.fori_loop(start, stop, body, 0)

    def send_core(self, part):
        for row in range(self.rows):
            self.core_copy(part, row).start()

    def send_rows(self, part):
        for row in range(self.rows):
            self.core_copy(part, row).wait_recv()
            self.add(row * 2 + self.core, self.from_core.at[row], part)
        for step in range(1, self.rows):
            self.row_copy(part, step).start()

    def send_section(self, part):
        for step in range(1, self.rows):
            self.row_copy(part, step).wait_recv()
            self.add(self.dp, self.from_row.at[step - 1], part)

        @pl.when(self.section != self.home)
        def _():
            self.section_copy(part).start()

    def close(self, part, write):
        @pl.when(self.section == self.home)
        def _():
            self.section_copy(part).wait_recv()
            for tile in range(*self.parts[part]):
                write(
                    tile,
                    self.tiles[self.dp, tile].astype(f32) + self.from_section[tile].astype(f32),
                )

    def close_rows(self, part, write):
        for step in range(1, self.rows):
            self.row_copy(part, step).wait_recv()
        for tile in range(*self.parts[part]):
            total = self.tiles[self.dp, tile].astype(f32)
            for step in range(1, self.rows):
                total = total + self.from_row[step - 1, tile].astype(f32)
            write(tile, total)

    def finish(self, shared):
        for part in range(len(self.parts)):
            for row in range(self.rows):
                self.core_copy(part, row).wait_send()
            for step in range(1, self.rows):
                self.row_copy(part, step).wait_send()
            if part < shared:

                @pl.when(self.section != self.home)
                def _():
                    self.section_copy(part).wait_send()


def grid_scratch(groups, tiles, size, parts):
    rows = groups // 2
    return [
        pltpu.VMEM((groups, tiles, size, size), bf16),
        pltpu.VMEM((rows, tiles, size, size), bf16),
        pltpu.VMEM((rows - 1, tiles, size, size), bf16),
        pltpu.VMEM((tiles, size, size), bf16),
        pltpu.SemaphoreType.DMA((2, parts, rows)),
        pltpu.SemaphoreType.DMA((2, parts, rows - 1)),
        pltpu.SemaphoreType.DMA((2, parts)),
    ]


class LineSum:
    def __init__(self, n, me, middle, part, out, held, sems):
        self.n, self.me, self.middle, self.part, self.out = n, me, middle, part, out
        self.from_left, self.from_right = held
        self.rs_send, self.rs_recv, self.ag_send, self.ag_recv = sems
        self.stages = 2 * n - 1

    def reduce_copy(self, src, landing, side, chunk, block, target):
        return pltpu.make_async_remote_copy(
            src_ref=src,
            dst_ref=landing.at[chunk, block],
            send_sem=self.rs_send.at[side, chunk, block],
            recv_sem=self.rs_recv.at[side, chunk, block],
            device_id={"tensor": target},
            device_id_type=MESH,
        )

    def gather_copy(self, side, chunk, block, target):
        return pltpu.make_async_remote_copy(
            src_ref=self.out.at[chunk, block],
            dst_ref=self.out.at[chunk, block],
            send_sem=self.ag_send.at[side, chunk, block],
            recv_sem=self.ag_recv.at[chunk, block],
            device_id={"tensor": target},
            device_id_type=MESH,
        )

    def put(self, chunk, rows):
        self.part[chunk] = rows.astype(bf16).reshape(self.part.shape[1:])

    def rows(self, chunk):
        whole = self.out[chunk]
        return whole.reshape(-1, whole.shape[-1])

    def stage(self, chunk, stage):
        n = self.n
        if stage == 0:
            self.first_sends(chunk)
        elif stage <= n - 2:
            self.hop(chunk, stage)
        elif stage == n - 1:
            self.own_rows(chunk)
        else:
            self.forward(chunk, stage - n + 1)

    def first_sends(self, chunk):
        n, part = self.n, self.part

        @pl.when(self.me == 0)
        def _():
            for block in range(n - 1, 0, -1):
                self.reduce_copy(
                    part.at[chunk, block], self.from_left, 0, chunk, block, 1
                ).start()

        @pl.when(self.me == n - 1)
        def _():
            for block in range(n - 1):
                self.reduce_copy(
                    part.at[chunk, block], self.from_right, 1, chunk, block, n - 2
                ).start()

    def hop(self, chunk, step):
        n, part = self.n, self.part

        @pl.when(self.me == step)
        def _():
            landing = self.from_left
            for block in range(n - 1, step, -1):
                self.reduce_copy(
                    part.at[chunk, block], landing, 0, chunk, block, step
                ).wait_recv()
                part[chunk, block] = (
                    landing[chunk, block].astype(f32) + part[chunk, block].astype(f32)
                ).astype(bf16)
                self.reduce_copy(
                    part.at[chunk, block], landing, 0, chunk, block, step + 1
                ).start()

        @pl.when(self.me == n - 1 - step)
        def _():
            landing = self.from_right
            mine = n - 1 - step
            for block in range(mine):
                self.reduce_copy(
                    part.at[chunk, block], landing, 1, chunk, block, mine
                ).wait_recv()
                part[chunk, block] = (
                    landing[chunk, block].astype(f32) + part[chunk, block].astype(f32)
                ).astype(bf16)
                self.reduce_copy(
                    part.at[chunk, block], landing, 1, chunk, block, mine - 1
                ).start()

    def own_rows(self, chunk):
        n, me, part = self.n, self.me, self.part

        @pl.when(me > 0)
        def _():
            self.reduce_copy(part.at[chunk, me], self.from_left, 0, chunk, me, me).wait_recv()

        @pl.when(me < n - 1)
        def _():
            self.reduce_copy(part.at[chunk, me], self.from_right, 1, chunk, me, me).wait_recv()

        total = part[chunk, me].astype(f32)
        total = total + jnp.where(me > 0, self.from_left[chunk, me].astype(f32), 0.0)
        total = total + jnp.where(me < n - 1, self.from_right[chunk, me].astype(f32), 0.0)
        self.out[chunk, me] = self.middle(chunk, me, total).astype(bf16)

        @pl.when(me < n - 1)
        def _():
            self.gather_copy(0, chunk, me, me + 1).start()

        @pl.when(me > 0)
        def _():
            self.gather_copy(1, chunk, me, me - 1).start()

    def forward(self, chunk, step):
        n, me = self.n, self.me
        left_block = me - step

        @pl.when(left_block >= 0)
        def _():
            self.gather_copy(0, chunk, left_block, me).wait_recv()

            @pl.when(me < n - 1)
            def _():
                self.gather_copy(0, chunk, left_block, me + 1).start()

        right_block = me + step

        @pl.when(right_block < n)
        def _():
            self.gather_copy(1, chunk, right_block, me).wait_recv()

            @pl.when(me > 0)
            def _():
                self.gather_copy(1, chunk, right_block, me - 1).start()

    def finish(self):
        n, me, part = self.n, self.me, self.part
        for chunk in range(part.shape[0]):
            for block in range(n):

                @pl.when((me < n - 1) & (block > me))
                def _():
                    self.reduce_copy(
                        part.at[chunk, block], self.from_left, 0, chunk, block, me
                    ).wait_send()

                @pl.when((me > 0) & (block < me))
                def _():
                    self.reduce_copy(
                        part.at[chunk, block], self.from_right, 1, chunk, block, me
                    ).wait_send()

                @pl.when((me < n - 1) & (block <= me))
                def _():
                    self.gather_copy(0, chunk, block, me).wait_send()

                @pl.when((me > 0) & (block >= me))
                def _():
                    self.gather_copy(1, chunk, block, me).wait_send()


def line_scratch(chunks, n, block, width):
    return [pltpu.VMEM((chunks, n, block, width), bf16)] * 3 + [
        pltpu.SemaphoreType.DMA((2, chunks, n)),
        pltpu.SemaphoreType.DMA((2, chunks, n)),
        pltpu.SemaphoreType.DMA((2, chunks, n)),
        pltpu.SemaphoreType.DMA((chunks, n)),
    ]


def make_line(n, me, middle, out, scratch):
    return LineSum(n, me, middle, scratch[0], out, scratch[1:3], scratch[3:7])


def run_two(order, first, second, produce, between, finished, extra):
    lag = first.stages - 1
    last = len(order) - 1
    for slot in range(2 * lag + last + 1):
        if slot <= last:
            produce(order[slot])
        extra(slot)
        for place, chunk in enumerate(order):
            stage = slot - lag - place
            if 1 <= stage <= lag:
                second.stage(chunk, stage)
            if stage == lag:
                finished(chunk)
        for place, chunk in enumerate(order):
            stage = slot - place
            if 0 <= stage <= lag:
                first.stage(chunk, stage)
        if 0 <= slot - lag <= last:
            chunk = order[slot - lag]
            between(chunk)
            second.stage(chunk, 0)


class WeightSwap:
    def __init__(self, groups, own, layers, sems):
        self.groups, self.own, self.layers = groups, own, layers
        self.x_sems, self.row_sems, self.core_sems, self.local_sems = sems
        self.dp = lax.axis_index("dp")
        self.section = lax.axis_index("section")
        self.core = self.dp % 2
        self.row = self.dp // 2
        self.rows = groups // 2

    def share(self, array, piece):
        rows = self.own[array][0].shape[0] // self.groups
        return pl.ds(pl.multiple_of(piece * rows, rows), rows)

    def block(self, layer, array, piece):
        ref, lanes = self.layers[layer][array]
        return ref.at[self.share(array, piece), lanes]

    def section_copy(self, layer, array):
        ref, lanes = self.own[array]
        return pltpu.make_async_remote_copy(
            src_ref=ref.at[self.share(array, self.dp), lanes],
            dst_ref=self.block(layer, array, self.dp),
            send_sem=self.x_sems.at[0, array],
            recv_sem=self.x_sems.at[1, array],
            device_id={"section": 1 - self.section},
            device_id_type=MESH,
        )

    def row_copy(self, layer, array, step, source, target):
        piece = source * 2 + self.core
        return pltpu.make_async_remote_copy(
            src_ref=self.block(layer, array, piece),
            dst_ref=self.block(layer, array, piece),
            send_sem=self.row_sems.at[0, array, step - 1],
            recv_sem=self.row_sems.at[1, array, step - 1],
            device_id={"dp": target * 2 + self.core},
            device_id_type=MESH,
        )

    def core_copy(self, layer, array, step, core):
        piece = (self.row - step) % self.rows * 2 + core
        return pltpu.make_async_remote_copy(
            src_ref=self.block(layer, array, piece),
            dst_ref=self.block(layer, array, piece),
            send_sem=self.core_sems.at[0, array, step],
            recv_sem=self.core_sems.at[1, array, step],
            device_id={"dp": self.dp + 1 - 2 * self.core},
            device_id_type=MESH,
        )

    def local_copy(self, layer, array):
        ref, lanes = self.own[array]
        to, to_lanes = self.layers[layer][array]
        return pltpu.make_async_copy(
            ref.at[:, lanes], to.at[:, to_lanes], self.local_sems.at[array]
        )

    def take(self, layer, arrays):
        for array in arrays:
            self.section_copy(layer, array).wait_recv()
            for step in range(1, self.rows):
                target = (self.row + step) % self.rows
                self.row_copy(layer, array, step, self.row, target).start()
            self.core_copy(layer, array, 0, self.core).start()

    def spread(self, layer, arrays):
        for array in arrays:
            for step in range(1, self.rows):
                source = (self.row - step) % self.rows
                self.row_copy(layer, array, step, source, self.row).wait_recv()
                self.core_copy(layer, array, step, self.core).start()

    def settle(self, layer, arrays):
        for array in arrays:
            for step in range(self.rows):
                self.core_copy(layer, array, step, 1 - self.core).wait_recv()

    def on_arrival(self, work, arrays):
        for layer in range(2):

            @pl.when(self.section != layer)
            def _():
                work(layer, arrays)

    def finish(self):
        for layer in range(2):
            for array in range(len(self.own)):

                @pl.when(self.section == layer)
                def _():
                    self.section_copy(layer, array).wait_send()

                @pl.when(self.section != layer)
                def _():
                    for step in range(1, self.rows):
                        target = (self.row + step) % self.rows
                        self.row_copy(layer, array, step, self.row, target).wait_send()
                    for step in range(self.rows):
                        self.core_copy(layer, array, step, self.core).wait_send()


class LineGather:
    def __init__(self, n, me, place, sems):
        self.n, self.me, self.place = n, me, place
        self.send, self.recv = sems

    def copy(self, side, block, target):
        return pltpu.make_async_remote_copy(
            src_ref=self.place(block),
            dst_ref=self.place(block),
            send_sem=self.send.at[side, block],
            recv_sem=self.recv.at[block],
            device_id={"tensor": target},
            device_id_type=MESH,
        )

    def start(self):
        n, me = self.n, self.me

        @pl.when(me < n - 1)
        def _():
            self.copy(0, me, me + 1).start()

        @pl.when(me > 0)
        def _():
            self.copy(1, me, me - 1).start()

    def forward(self, step):
        n, me = self.n, self.me
        left_block = me - step

        @pl.when(left_block >= 0)
        def _():
            self.copy(0, left_block, me).wait_recv()

            @pl.when(me < n - 1)
            def _():
                self.copy(0, left_block, me + 1).start()

        right_block = me + step

        @pl.when(right_block < n)
        def _():
            self.copy(1, right_block, me).wait_recv()

            @pl.when(me > 0)
            def _():
                self.copy(1, right_block, me - 1).start()

    def finish(self):
        n, me = self.n, self.me
        for block in range(n):

            @pl.when((me < n - 1) & (block <= me))
            def _():
                self.copy(0, block, me).wait_send()

            @pl.when((me > 0) & (block >= me))
            def _():
                self.copy(1, block, me).wait_send()


def columns_of(ref, lanes):
    def place(block):
        at = pl.ds(pl.multiple_of(block * lanes, lanes), lanes)
        return ref.at[FRESH_START:CMEM, at]

    return place


def score_columns(head, chunk, q_ref, kv_ref, docs, keys_docs):
    lanes = slice(head * HD, (head + 1) * HD)
    width = CMEM + MEM + (chunk + 1) * ROWS
    query = q_ref[chunk * ROWS : (chunk + 1) * ROWS, lanes]
    scores = dot_nt(kv_ref[:width, lanes], query) * HD ** (-0.5)
    own = docs[:, chunk * ROWS : (chunk + 1) * ROWS]
    same = keys_docs[: MEM + chunk * ROWS, :] == own
    tail_docs = keys_docs[MEM + chunk * ROWS : MEM + (chunk + 1) * ROWS, :]
    key_place = lax.broadcasted_iota(jnp.int32, (ROWS, ROWS), 0)
    query_place = lax.broadcasted_iota(jnp.int32, (ROWS, ROWS), 1)
    tail_same = (tail_docs == own) & (key_place <= query_place)
    middle_end = CMEM + MEM + chunk * ROWS
    return jnp.concatenate(
        [
            scores[:CMEM],
            jnp.where(same, scores[CMEM:middle_end], masked_value),
            jnp.where(tail_same, scores[middle_end:], masked_value),
        ],
        axis=0,
    )


def forward_kernel(n, groups, ship, *refs):
    if ship:
        m_ref, x_ref, own_gains, docs, key_docs = refs[:5]
        own_refs, (old, piece, compressed, memory) = refs[5:11], refs[11:15]
        (normed, q_ref, kv_ref, log_sum, attended, residual, two, hidden, active) = refs[15:24]
        out, shipped = refs[24:26]
        layer_refs = [refs[26:33], refs[33:40]]
        wq, wkv, wo, wup, wdown, gains, c_ref = layer_refs[0]
        rest = refs[40:]
    else:
        (c_ref, m_ref, x_ref, wq, wkv, wo, wup, wdown, gains, docs, key_docs) = refs[:11]
        (normed, q_ref, kv_ref, log_sum, attended, residual, two, hidden, active) = refs[11:20]
        out, outputs = refs[20:22]
        rest = refs[22:]
    keys_docs, values_t = rest[:2]
    first_scratch, second_scratch = rest[2:9], rest[9:16]
    ship_send, ship_recv = rest[16:18]
    me = greet(n, True, groups)
    section = lax.axis_index("section")
    heads = wq.shape[1] // HD
    local = wq.shape[1]
    if ship:
        swap_sems, item_sems, local_sems, gather_sems = rest[18:22], rest[22], rest[23], rest[24:28]
        inner = wup.shape[1]
        half = inner // 2
        all_lanes = slice(None)
        front, back = slice(0, half), slice(half, inner)
        width = wup.shape[0]
        lead, trail = slice(0, width // 2), slice(width // 2, width)
        q_own, k_own, v_own, o_own, up_own, down_own = own_refs
        own = [(q_own, all_lanes), (k_own, all_lanes), (v_own, all_lanes), (o_own, all_lanes),
               (up_own, front), (up_own, back), (down_own, lead), (down_own, trail)]
        layers = [
            [(w[0], all_lanes), (w[1], slice(0, local)), (w[1], slice(local, 2 * local)),
             (w[2], all_lanes), (w[3], front), (w[3], back), (w[4], lead), (w[4], trail)]
            for w in layer_refs
        ]
        swap = WeightSwap(groups, own, layers, swap_sems)
        gathers = [
            LineGather(n, me, columns_of(layer_refs[layer][6], local),
                       gather_sems[2 * layer : 2 * layer + 2])
            for layer in range(2)
        ]
        items = [
            [(own_gains, layer_refs[0][5]), (piece, gathers[0].place(me)),
             (old, layer_refs[0][6].at[:FRESH_START, :])],
            [(own_gains, layer_refs[1][5]), (compressed, layer_refs[1][6]), (memory, shipped)],
        ]

        def item_copy(layer, index):
            src, dst = items[layer][index]
            return pltpu.make_async_remote_copy(
                src_ref=src,
                dst_ref=dst,
                send_sem=item_sems.at[0, index],
                recv_sem=item_sems.at[1, index],
                device_id={"section": 1 - section},
                device_id_type=MESH,
            )

        local_rows = [
            pltpu.make_async_copy(compressed, layer_refs[0][6], local_sems.at[0]),
            pltpu.make_async_copy(old, layer_refs[1][6].at[:FRESH_START, :], local_sems.at[0]),
            pltpu.make_async_copy(piece, gathers[1].place(me), local_sems.at[1]),
        ]

        @pl.when(section == 0)
        def _():
            item_copy(0, 0).start()
            item_copy(0, 1).start()
            for array in range(4):
                swap.section_copy(0, array).start()
            item_copy(0, 2).start()
            for array in range(4, 8):
                swap.section_copy(0, array).start()
            for array in range(3):
                swap.local_copy(0, array).start()
            local_rows[0].start()
            for array in range(3, 8):
                swap.local_copy(0, array).start()
            layer_refs[0][5][...] = own_gains[...]
            local_rows[0].wait()
            for array in range(8):
                swap.local_copy(0, array).wait()

        @pl.when(section == 1)
        def _():
            item_copy(1, 0).start()
            for array in range(8):
                swap.section_copy(1, array).start()
            item_copy(1, 1).start()
            item_copy(1, 2).start()
            local_rows[1].start()
            local_rows[2].start()
            for array in range(8):
                swap.local_copy(1, array).start()
            layer_refs[1][5][...] = own_gains[...]
            item_copy(0, 0).wait_recv()
            item_copy(0, 1).wait_recv()
            gathers[0].start()
            swap.take(0, range(3))
            gathers[0].forward(1)
            swap.spread(0, range(3))
            for step in range(2, n):
                gathers[0].forward(step)
            swap.settle(0, range(3))

    keys_docs[...] = jnp.broadcast_to(key_docs[...], keys_docs.shape)
    gain_a = gains[0:1, :]
    gain_f = gains[1:2, :]

    def project_block(source, place):
        def body(step, carry):
            rows = pl.ds(pl.multiple_of(step * 256, 256), 256)
            at = pl.ds(pl.multiple_of(place * SEG + step * 256, 256), 256)
            wide = source[rows, :].astype(f32)
            block = (wide * inverse_rms(wide) * gain_a).astype(bf16)
            normed[at, :] = block
            both = dot_nn(block, wkv[...]).astype(bf16)
            kv_ref[at, :] = both
            if place == 2:
                q_ref[rows, :] = dot_nn(block, wq[...]).astype(bf16)
            return carry

        lax.fori_loop(0, SEG // 256, body, 0)

    project_block(m_ref, 1)
    x_rows = x_ref.reshape(SEG, x_ref.shape[-1])
    project_block(x_rows, 2)
    if ship:

        @pl.when(section == 1)
        def _():
            swap.take(0, [3])
            swap.spread(0, [3])
            item_copy(0, 2).wait_recv()
            swap.settle(0, [3])

    project_block(c_ref, 0)
    for head in range(heads):
        lanes = slice(local + head * HD, local + (head + 1) * HD)
        values_t[head] = kv_ref[:, lanes].astype(f32).T.astype(bf16)

    def attention_middle(chunk, me, total):
        rows = x_ref[chunk, me].astype(f32) + total
        residual[chunk] = rows
        return rows * inverse_rms(rows) * gain_f

    def output_middle(chunk, me, total):
        return residual[chunk] + total

    first = make_line(n, me, attention_middle, two, first_scratch)
    second = make_line(n, me, output_middle, out, second_scratch)

    def attend(chunk):
        rows = slice(chunk * ROWS, (chunk + 1) * ROWS)
        for head in range(heads):
            lanes = slice(head * HD, (head + 1) * HD)
            scores = score_columns(head, chunk, q_ref, kv_ref, docs, keys_docs)
            top = jnp.max(scores, axis=0, keepdims=True)
            powers = jnp.exp(scores - top)
            total = jnp.sum(powers, axis=0, keepdims=True)
            log_sum[head : head + 1, rows] = top + jnp.log(total)
            weights = (powers * (1.0 / total)).astype(bf16)
            mixed = dot_nn(values_t[head, :, : weights.shape[0]], weights)
            attended[rows, lanes] = mixed.T.astype(bf16)
        first.put(chunk, dot_nn(attended[rows, :], wo[...]))

    def feed(chunk):
        rows = slice(chunk * ROWS, (chunk + 1) * ROWS)
        before = dot_nn(first.rows(chunk), wup[...])
        hidden[rows, :] = before
        after = gelu(before).astype(bf16)
        active[rows, :] = after
        second.put(chunk, dot_nn(after, wdown[...]))

    def ship_copy(chunk):
        return pltpu.make_async_remote_copy(
            src_ref=out.at[chunk],
            dst_ref=shipped.at[chunk] if ship else outputs.at[0, chunk],
            send_sem=ship_send.at[chunk],
            recv_sem=ship_recv.at[chunk],
            device_id={"section": 1 - section},
            device_id_type=MESH,
        )

    def finished(chunk):
        @pl.when(section == 0)
        def _():
            ship_copy(chunk).start()

        if not ship:

            @pl.when(section == 1)
            def _():
                keep_out(chunk).start()

    if not ship:
        out_send, out_recv, keep = rest[18:21]

        def keep_out(chunk):
            return pltpu.make_async_copy(out.at[chunk], outputs.at[1, chunk], keep.at[chunk])

        keep_input = pltpu.make_async_copy(x_ref, outputs.at[0], keep.at[0])
        send_input = pltpu.make_async_remote_copy(
            src_ref=x_ref,
            dst_ref=outputs.at[1],
            send_sem=out_send.at[0],
            recv_sem=out_recv.at[0],
            device_id={"section": 1 - section},
            device_id_type=MESH,
        )

        @pl.when(section == 0)
        def _():
            keep_input.start()

        @pl.when(section == 1)
        def _():
            send_input.start()

    def early(work, arrays):
        @pl.when(section == 0)
        def _():
            work(1, arrays)

    def extra(slot):
        if not ship:
            return
        if slot < 3:
            early((swap.take, swap.spread, swap.settle)[slot], range(4))
        plan = {
            2: [(swap.take, [4])],
            3: [(swap.take, [5]), (swap.spread, [4])],
            4: [(swap.spread, [5]), (swap.take, [6])],
            5: [(swap.take, [7]), (swap.spread, [6]), (swap.settle, [4, 5])],
            6: [(swap.spread, [7]), (swap.settle, [6, 7])],
        }
        for work, arrays in plan.get(slot, ()):
            swap.on_arrival(work, arrays)
        if slot < n:

            @pl.when(section == 1)
            def _():
                if slot == 0:
                    local_rows[2].wait()
                    gathers[1].start()
                else:
                    gathers[1].forward(slot)

    run_two(list(range(CHUNKS)), first, second, attend, feed, finished, extra)
    first.finish()
    second.finish()
    if not ship:

        @pl.when(section == 0)
        def _():
            keep_input.wait()
            send_input.wait_recv()
            for chunk in range(CHUNKS):
                ship_copy(chunk).wait_send()

        @pl.when(section == 1)
        def _():
            send_input.wait_send()
            for chunk in range(CHUNKS):
                keep_out(chunk).wait()
                ship_copy(chunk).wait_recv()

    if ship:
        swap.finish()

        @pl.when(section == 0)
        def _():
            for chunk in range(CHUNKS):
                ship_copy(chunk).wait_send()
            for index in range(3):
                item_copy(0, index).wait_send()
                item_copy(1, index).wait_recv()

        @pl.when(section == 1)
        def _():
            for chunk in range(CHUNKS):
                ship_copy(chunk).wait_recv()
            for index in range(3):
                item_copy(1, index).wait_send()
            local_rows[1].wait()
            for array in range(8):
                swap.local_copy(1, array).wait()
            for gather in gathers:
                gather.finish()


def vmem_specs(count):
    return [pl.BlockSpec(memory_space=pltpu.VMEM)] * count


def forward_outs(n, width, local, inner):
    block = ROWS // n
    shape = jax.ShapeDtypeStruct
    rows = shape((CHUNKS, n, block, width), bf16)
    outs = [
        shape((CMEM + MEM + SEG, width), bf16),
        shape((SEG, local), bf16),
        shape((CMEM + MEM + SEG, 2 * local), bf16),
        shape((8, SEG), f32),
        shape((SEG, local), bf16),
        shape((CHUNKS, block, width), f32),
        rows,
        shape((SEG, inner), f32),
        shape((SEG, inner), bf16),
        rows,
    ]
    scratch = (
        [
            pltpu.VMEM((MEM + SEG, HD), jnp.int32),
            pltpu.VMEM((local // HD, HD, CMEM + MEM + SEG), bf16),
        ]
        + line_scratch(CHUNKS, n, block, width)
        + line_scratch(CHUNKS, n, block, width)
    )
    return rows, outs, scratch


def forward_last(collective, n, c_rows, m_rows, x_rows, weights, gains, docs, key_docs):
    wq, wkv, wo, wup, wdown = weights
    rows, outs, scratch = forward_outs(n, x_rows.shape[1], wq.shape[1], wup.shape[1])
    return pl.pallas_call(
        functools.partial(forward_kernel, n, 0, False),
        name="forward_last",
        out_shape=outs + [jax.ShapeDtypeStruct((2,) + rows.shape, bf16)],
        in_specs=vmem_specs(11),
        out_specs=vmem_specs(len(outs) + 1),
        scratch_shapes=scratch
        + [
            pltpu.SemaphoreType.DMA((CHUNKS,)),
            pltpu.SemaphoreType.DMA((CHUNKS,)),
            pltpu.SemaphoreType.DMA((1,)),
            pltpu.SemaphoreType.DMA((1,)),
            pltpu.SemaphoreType.DMA((CHUNKS,)),
        ],
        compiler_params=pltpu.CompilerParams(
            collective_id=collective, has_side_effects=True, vmem_limit_bytes=60000 * 1024
        ),
    )(c_rows, m_rows, x_rows.reshape(rows.shape), wq, wkv, wo, wup, wdown, gains, docs, key_docs)


def forward_first(collective, n, groups, m_rows, x_rows, gains, docs, key_docs, own, old, piece,
                  compressed, memory):
    width, local, inner = x_rows.shape[1], own[0].shape[1], own[4].shape[1]
    rows, outs, scratch = forward_outs(n, width, local, inner)
    shape = jax.ShapeDtypeStruct
    layer = [
        shape((width, local), bf16),
        shape((width, 2 * local), bf16),
        shape((local, width), bf16),
        shape((width, inner), bf16),
        shape((inner, width), bf16),
        shape(gains.shape, f32),
        shape((CMEM, width), bf16),
    ]
    outs = outs + [rows] + layer + layer
    arrays, rows_y = 8, groups // 2
    dma = pltpu.SemaphoreType.DMA
    scratch = scratch + [
        dma((CHUNKS,)),
        dma((CHUNKS,)),
        dma((2, arrays)),
        dma((2, arrays, rows_y - 1)),
        dma((2, arrays, rows_y)),
        dma((arrays,)),
        dma((2, 3)),
        dma((2,)),
        dma((2, n)),
        dma((n,)),
        dma((2, n)),
        dma((n,)),
    ]
    result = pl.pallas_call(
        functools.partial(forward_kernel, n, groups, True),
        name="forward_ship",
        out_shape=outs,
        in_specs=vmem_specs(5) + [pl.BlockSpec(memory_space=pl.ANY)] * 10,
        out_specs=vmem_specs(len(outs)),
        scratch_shapes=scratch,
        compiler_params=pltpu.CompilerParams(
            collective_id=collective, has_side_effects=True, vmem_limit_bytes=60000 * 1024
        ),
    )(m_rows, x_rows.reshape(rows.shape), gains, docs, key_docs, *own, old, piece, compressed,
      memory.reshape(rows.shape))
    return result[:11], result[11:18], result[18:25]


def backward_kernel(n, groups, home, *refs):
    (g_ref, x_ref, residual, hidden, fresh, wq, wkv, wo, wup, wdown, gains, q_ref, kv_ref,
     log_sum, docs, key_docs, normed, two, active, attended) = refs[:20]
    last = home == 0
    rest = refs[20:]
    if last:
        earlier_gains, padded, earlier, rest = rest[:2], rest[2], rest[3:11], rest[11:]
    dx_ref, shipped, d_fresh = rest[:3]
    results, gain_results, rest = rest[3:9], rest[9:11], rest[11:]
    grad_query, grad_key, grad_value, grad_out, grad_up, grad_down = results
    if last:
        grad_compress, rest = rest[0], rest[1:]
    d_hidden, d_branch, dq_ref, dkv_ref, d_residual, keys_docs, keys_t, sums = rest[:8]
    rest = rest[8:]
    first_scratch, second_scratch, fresh_scratch = rest[:7], rest[7:14], rest[14:21]
    tiles, grid_rest = rest[21], rest[22:28]
    ship_send, ship_recv = rest[28:30]
    gain_sums, gain_blocks, gain_send, gain_recv = rest[30:34]
    if last:
        fresh_columns, keep, keep_rows, fresh_sems = rest[34:38]
    me = greet(n, True, groups)
    section = lax.axis_index("section")
    late = section == 1
    local = wq.shape[1]
    heads = local // HD
    gain_a = gains[0:1, :]
    gain_f = gains[1:2, :]
    scale = HD ** (-0.5)

    keys_docs[...] = jnp.broadcast_to(key_docs[...], keys_docs.shape)
    for head in range(heads):
        lanes = slice(head * HD, (head + 1) * HD)
        keys_t[head] = kv_ref[:, lanes].astype(f32).T.astype(bf16)

    def branch_middle(chunk, me, total):
        rows = g_ref[chunk, me].astype(f32) + rms_pull(total, residual[chunk], gain_f)
        d_residual[chunk] = rows
        return rows

    def input_middle(chunk, me, total):
        return d_residual[chunk] + rms_pull(total, x_ref[chunk, me].astype(f32), gain_a)

    def fresh_middle(chunk, me, total):
        return rms_pull(total, fresh[chunk, me].astype(f32), gain_a)

    first = make_line(n, me, branch_middle, d_branch, first_scratch)
    second = make_line(n, me, input_middle, dx_ref, second_scratch)
    third = make_line(n, me, fresh_middle, d_fresh, fresh_scratch)

    def produce(chunk):
        rows = slice(chunk * ROWS, (chunk + 1) * ROWS)
        grad = g_ref[chunk]
        d_active = dot_nt(grad.reshape(ROWS, grad.shape[-1]), wdown[...])
        block = (gelu_slope(hidden[rows, :]) * d_active).astype(bf16)
        d_hidden[rows, :] = block
        first.put(chunk, dot_nt(block, wup[...]))

    def attend_back(chunk):
        rows = slice(chunk * ROWS, (chunk + 1) * ROWS)
        d_attended = dot_nt(first.rows(chunk), wo[...]).astype(bf16)
        fresh_sum = chunk == CHUNKS - 1
        for head in range(heads):
            lanes = slice(head * HD, (head + 1) * HD)
            value_lanes = slice(local + head * HD, local + (head + 1) * HD)
            scores = score_columns(head, chunk, q_ref, kv_ref, docs, keys_docs)
            size = scores.shape[0]
            probs = jnp.exp(scores - log_sum[head : head + 1, rows])
            d_mixed = d_attended[:, lanes]
            d_values = dot_nn(probs.astype(bf16), d_mixed)
            d_probs = dot_nt(kv_ref[:size, value_lanes], d_mixed)
            inner = jnp.sum(d_probs * probs, axis=0, keepdims=True)
            d_scores = (probs * (d_probs - inner)).astype(bf16)
            d_keys = dot_nn(d_scores, q_ref[rows, lanes])
            d_queries = dot_nn(keys_t[head, :, :size], d_scores) * scale
            dq_ref[rows, lanes] = d_queries.T.astype(bf16)
            if fresh_sum:
                sums[:size, lanes] = d_keys
                sums[:size, value_lanes] = d_values
            else:
                sums[:size, lanes] += d_keys
                sums[:size, value_lanes] += d_values
        own = slice(CMEM + MEM + chunk * ROWS, CMEM + MEM + (chunk + 1) * ROWS)
        close_rows(own)
        second.put(
            chunk, dot_nt(dq_ref[rows, :], wq[...]) + dot_nt(dkv_ref[own, :], wkv[...])
        )
        if chunk == 0:
            close_rows(slice(0, CMEM + MEM))

            @pl.when(late)
            def _():
                count = third.part.shape[1] * third.part.shape[2]
                third.put(0, dot_nt(dkv_ref[FRESH_START : FRESH_START + count, :], wkv[...]))
                third.stage(0, 0)

    def close_rows(rows):
        dkv_ref[rows, :local] = (sums[rows, :local] * scale).astype(bf16)
        dkv_ref[rows, local:] = sums[rows, local:].astype(bf16)

    size = wq.shape[0] // groups
    wide = hidden.shape[1] // size
    up_at, down_at, fresh_at = 4, 4 + wide, 4 + 2 * wide
    parts = [(down_at, fresh_at), (up_at, down_at), (0, 2), (2, 4)]
    shared = len(parts)
    if last:
        parts.append((fresh_at, fresh_at + RATE))
    grid = GridSum(groups, home, tiles, grid_rest[:3], grid_rest[3:6], parts)
    half = groups // 2
    g_rows = g_ref.reshape(SEG, g_ref.shape[-1])
    two_rows = two.reshape(SEG, two.shape[-1])
    branch_rows = d_branch.reshape(SEG, d_branch.shape[-1])

    def each_block(start, stop, work):
        def body(block, carry):
            work(block, pl.ds(pl.multiple_of(block * size, size), size))
            return carry

        lax.fori_loop(start, stop, body, 0)

    def put_tiles(block, at, value):
        for tile in range(value.shape[1] // size):
            tiles[block, at + tile] = value[:, tile * size : (tile + 1) * size].astype(bf16)

    def down_block(block, lanes):
        put_tiles(block, down_at, dot_tn(g_rows[:, lanes], active[...]))

    def up_block(block, lanes):
        put_tiles(block, up_at, dot_tn(two_rows[:, lanes], d_hidden[...]))

    def small_block(block, lanes):
        put_tiles(block, 0, dot_tn(normed[CMEM + MEM :, lanes], dq_ref[...]))
        put_tiles(block, 1, dot_tn(branch_rows[:, lanes], attended[...]))

    def kv_block(block, lanes):
        put_tiles(block, 2, dot_tn(normed[:, lanes], dkv_ref[...]))

    share = pl.ds(pl.multiple_of(grid.dp * size, size), size)
    gain_sums[...] = jnp.zeros(gain_sums.shape, f32)

    def write(tile, value):
        if tile >= down_at:
            grad_down[(tile - down_at) * size : (tile - down_at + 1) * size, :] = value.T
        elif tile >= up_at:
            lanes = slice((tile - up_at) * size, (tile - up_at + 1) * size)
            grad_up[:, lanes] = value
            gain_sums[1] += wup[share, lanes].astype(f32) * value
        elif tile == 1:
            grad_out[...] = value.T
        elif tile == 0:
            grad_query[...] = value
            gain_sums[0] += wq[share, :].astype(f32) * value
        else:
            (grad_key, grad_value)[tile - 2][...] = value
            lanes = slice((tile - 2) * local, (tile - 1) * local)
            gain_sums[0] += wkv[share, lanes].astype(f32) * value

    gain_gather = LineGather(
        n, me, lambda block: gain_blocks.at[block], (gain_send, gain_recv)
    )

    first_slot = 2 * n - 2
    plan = {
        1: [lambda: each_block(0, half, down_block)],
        2: [lambda: each_block(half, groups, down_block), lambda: grid.send_core(0)],
        4: [lambda: each_block(0, half, up_block), lambda: grid.send_rows(0)],
        5: [lambda: each_block(half, groups, up_block), lambda: grid.send_core(1)],
        first_slot: [lambda: grid.send_rows(1)],
        first_slot + 1: [lambda: grid.send_section(0)],
        first_slot + 2: [lambda: grid.send_section(1)],
        first_slot + 3: [lambda: grid.close(0, write)],
        first_slot + 4: [
            lambda: each_block(0, groups, small_block), lambda: grid.send_core(2),
        ],
        first_slot + 5: [lambda: each_block(0, half, kv_block), lambda: grid.send_rows(2)],
        first_slot + 6: [
            lambda: each_block(half, groups, kv_block), lambda: grid.send_core(3),
            lambda: grid.send_section(2), lambda: grid.close(1, write),
        ],
        first_slot + 7: [lambda: grid.send_rows(3)],
        first_slot + 8: [lambda: grid.close(2, write)],
        first_slot + 9: [lambda: grid.send_section(3)],
    }

    def ship_copy(chunk):
        return pltpu.make_async_remote_copy(
            src_ref=dx_ref.at[chunk],
            dst_ref=shipped.at[1, chunk] if last else shipped.at[chunk],
            send_sem=ship_send.at[chunk],
            recv_sem=ship_recv.at[chunk],
            device_id={"section": 1 - section},
            device_id_type=MESH,
        )

    def finished(chunk):
        @pl.when(section != home)
        def _():
            ship_copy(chunk).start()

        if last:

            @pl.when(section == home)
            def _():
                keep_row(chunk).start()

    if last:
        earlier_shipped, earlier_fresh = earlier[6:]
        columns = pl.ds(pl.multiple_of(me * local, local), local)

        def keep_row(chunk):
            return pltpu.make_async_copy(
                dx_ref.at[chunk], shipped.at[0, chunk], keep_rows.at[chunk]
            )

        kept = [
            pltpu.make_async_copy(src, dst, keep.at[index])
            for index, (src, dst) in enumerate(zip(earlier[:6], results))
        ] + [
            pltpu.make_async_copy(earlier_shipped, shipped.at[0], keep.at[6]),
            pltpu.make_async_copy(g_ref, shipped.at[1], keep.at[7]),
            pltpu.make_async_copy(
                earlier_fresh.at[0, :, :, columns], fresh_columns, keep.at[8]
            ),
        ]
        fresh_copy = pltpu.make_async_remote_copy(
            src_ref=d_fresh.at[0, :, :, columns],
            dst_ref=fresh_columns,
            send_sem=fresh_sems.at[0],
            recv_sem=fresh_sems.at[1],
            device_id={"section": 1 - section},
            device_id_type=MESH,
        )

        @pl.when(late)
        def _():
            for copy in kept:
                copy.start()
            for index in range(2):
                gain_results[index][...] = earlier_gains[index][...]

    def compress_block(block, lanes):
        rows = fresh_columns.reshape(padded.shape[0], local)[...]
        for place in range(RATE):
            at = pl.ds(pl.multiple_of(place * wo.shape[1] + block * size, size), size)
            put_tiles(block, fresh_at + place, dot_tn(padded[:, at], rows))

    def write_compress(tile, value):
        grad_compress[tile - fresh_at] = value

    def extra(slot):
        for action in plan.get(slot, ()):
            action()
        step = slot - (first_slot + CHUNKS - 1)
        if 0 < step < third.stages:

            @pl.when(late)
            def _():
                third.stage(0, step)

    run_two(
        list(range(CHUNKS - 1, -1, -1)), first, second, produce, attend_back, finished, extra,
    )
    if last:

        @pl.when(late)
        def _():
            fresh_copy.start()
            for copy in kept:
                copy.wait()

        @pl.when(section == home)
        def _():
            fresh_copy.wait_recv()

        each_block(0, groups, compress_block)
        grid.send_core(4)
    grid.close(3, write)

    @pl.when(section == home)
    def _():
        gain_blocks[me] = jnp.zeros(gain_blocks.shape[1:], f32)
        for index in range(2):
            gain_blocks[me, index : index + 1, :] = jnp.sum(
                gain_sums[index].T, axis=0, keepdims=True
            )
        gain_gather.start()

    if last:
        grid.send_rows(4)

    @pl.when(section == home)
    def _():
        for step in range(1, n):
            gain_gather.forward(step)
        total = gain_blocks[0]
        for block in range(1, n):
            total = total + gain_blocks[block]
        for index in range(2):
            gain_results[index][...] = (
                total[index : index + 1, :] / gains[index : index + 1, share]
            )
        gain_gather.finish()

    first.finish()
    second.finish()
    if last:
        grid.close_rows(4, write_compress)
    grid.finish(shared)
    for chunk in range(CHUNKS):

        @pl.when(section != home)
        def _():
            ship_copy(chunk).wait_send()

        @pl.when(section == home)
        def _():
            ship_copy(chunk).wait_recv()
            if last:
                keep_row(chunk).wait()

    @pl.when(late)
    def _():
        third.finish()
        if last:
            fresh_copy.wait_send()


def fresh_block(n):
    return -(-(CMEM - FRESH_START) // (16 * n)) * 16


def backward_layer(collective, n, groups, home, grad, x_rows, residual, hidden, fresh, weights,
                   gains, q, kv, log_sum, docs, key_docs, normed, two, active, attended,
                   earlier_gains=(), padded=(), earlier=()):
    wq, wkv, wo, wup, wdown = weights
    width = wo.shape[1]
    local = wq.shape[1]
    block = ROWS // n
    size = width // groups
    inner = wup.shape[1]
    last = home == 0
    shape = jax.ShapeDtypeStruct
    any_space = pl.BlockSpec(memory_space=pl.ANY)
    rows = shape((CHUNKS, n, block, width), bf16)
    ship = shape((2,) + rows.shape, bf16) if last else rows
    fresh_shape = (n, fresh_block(n), width)
    outs = [rows, ship, shape((1,) + fresh_shape, bf16)]
    outs += [shape((size, local), f32)] * 3
    outs += [shape((local, size), f32), shape((size, inner), f32), shape((inner, size), f32)]
    outs += [shape((1, size), f32)] * 2
    out_specs = vmem_specs(1) + [any_space] + vmem_specs(9)
    tile_count = 4 + 2 * inner // size
    dma = pltpu.SemaphoreType.DMA
    if last:
        outs.append(shape((RATE, size, local), f32))
        out_specs += vmem_specs(1)
        tile_count += RATE
    return pl.pallas_call(
        functools.partial(backward_kernel, n, groups, home),
        name="backward_%d" % home,
        out_shape=outs,
        in_specs=vmem_specs(20 + (3 if last else 0)) + [any_space] * len(earlier),
        out_specs=out_specs,
        scratch_shapes=[
            pltpu.VMEM((SEG, inner), bf16),
            pltpu.VMEM(rows.shape, bf16),
            pltpu.VMEM((SEG, local), bf16),
            pltpu.VMEM((CMEM + MEM + SEG, 2 * local), bf16),
            pltpu.VMEM((CHUNKS, block, width), f32),
            pltpu.VMEM((MEM + SEG, HD), jnp.int32),
            pltpu.VMEM((local // HD, HD, CMEM + MEM + SEG), bf16),
            pltpu.VMEM((CMEM + MEM + SEG, 2 * local), f32),
        ]
        + line_scratch(CHUNKS, n, block, width)
        + line_scratch(CHUNKS, n, block, width)
        + line_scratch(1, n, fresh_block(n), width)
        + grid_scratch(groups, tile_count, size, 5 if last else 4)
        + [dma((CHUNKS,))] * 2
        + [pltpu.VMEM((2, size, size), f32), pltpu.VMEM((n, 8, size), f32), dma((2, n)), dma((n,))]
        + (
            [
                pltpu.VMEM((n, fresh_block(n), local), bf16),
                dma((9,)),
                dma((CHUNKS,)),
                dma((2,)),
            ]
            if last
            else []
        ),
        compiler_params=pltpu.CompilerParams(
            collective_id=collective, has_side_effects=True, vmem_limit_bytes=65000 * 1024
        ),
    )(grad.reshape(rows.shape), x_rows.reshape(rows.shape), residual, hidden, fresh,
      wq, wkv, wo, wup, wdown, gains, q, kv, log_sum, docs, key_docs, normed, two, active,
      attended, *earlier_gains, *padded, *earlier)


def project(rows, weight):
    return jnp.dot(rows, weight, preferred_element_type=f32).astype(bf16)


def shards(
    block_input,
    doc_ids,
    memory,
    compressed,
    gain_attn,
    w_query,
    w_key,
    w_value,
    w_out,
    gain_ffn,
    w_up,
    w_down,
    w_compress,
    cotangent,
):
    section = lax.axis_index("section")
    first = section == 0
    n = lax.axis_size("tensor")
    groups = lax.axis_size("dp")
    tensor_index = lax.axis_index("tensor")
    width = block_input.shape[2]
    local = w_query.shape[2]
    gains = jnp.stack([gain_attn[0], gain_ffn[0]])

    history = doc_ids[0]
    memory_docs = lax.dynamic_slice_in_dim(history, section * SEG, MEM, 0)
    token_docs = lax.dynamic_slice_in_dim(history, MEM + section * SEG, SEG, 0)
    docs = token_docs[None]
    key_docs = jnp.concatenate([memory_docs, token_docs])[:, None]
    tokens = lax.dynamic_slice_in_dim(block_input[0], section * SEG, SEG, 0)
    grad_now = lax.dynamic_slice_in_dim(cotangent[0], section * SEG, SEG, 0)

    fresh_count = n * fresh_block(n)
    lead = OLD_ROWS - FRESH_START
    trail = fresh_count - lead - COMP_ROWS
    padded = jnp.concatenate(
        [
            jnp.zeros((RATE * lead + PAD, width), bf16),
            memory[0, 0],
            jnp.zeros((RATE * trail, width), bf16),
        ]
    ).reshape(fresh_count, RATE * width)
    fresh_piece = project(padded, w_compress[0].reshape(RATE * width, local))
    fresh_piece = fresh_piece[lead : lead + COMP_ROWS]
    kept = compressed[0, 0, COMP_ROWS + FRESH_START :]
    piece = jnp.concatenate(
        [lax.dynamic_slice_in_dim(kept, tensor_index * local, local, 1), fresh_piece]
    )
    old = compressed[0, 0, COMP_ROWS : COMP_ROWS + FRESH_START]
    m_rows = jnp.where(first, memory[0, 0], block_input[0, :SEG])

    saved = []
    weight_layers = []
    gains_by_layer = []
    c_rows = []
    for layer in range(2):
        if layer == 0:
            own = (w_query[0], w_key[0], w_value[0], w_out[0], w_up[0], w_down[0])
            result, *layers = forward_first(
                1, n, groups, m_rows, tokens, gains, docs, key_docs, own, old, piece,
                compressed[0, 0], memory[0, 0],
            )
            for *weights, layer_gains, rows in layers:
                weight_layers.append(weights)
                gains_by_layer.append(layer_gains)
                c_rows.append(rows)
        else:
            result = forward_last(
                2, n, c_rows[1], m_rows, tokens, weight_layers[1], gains_by_layer[1], docs,
                key_docs,
            )
        normed, queries, kv, log_total, attended, residual, two, hidden, active, out = result[:10]
        saved.append((tokens, m_rows, normed, queries, kv, log_total, attended, residual,
                      two, hidden, active))
        tokens = out.reshape(SEG, width)
        if layer == 0:
            m_rows = result[10].reshape(SEG, width)
        else:
            outputs = result[10].reshape(2 * SEG, width)

    handed = []
    for layer in (1, 0):
        (tokens, m_rows, normed, queries, kv, log_total, attended, residual, two, hidden,
         active) = saved[layer]
        block = fresh_block(n)
        fresh_rows = jnp.concatenate(
            [c_rows[layer][FRESH_START:], m_rows[: n * block - (CMEM - FRESH_START)]]
        ).reshape(1, n, block, width)
        result = backward_layer(
            4 + layer, n, groups, layer, grad_now, tokens, residual, hidden, fresh_rows,
            weight_layers[layer], gains_by_layer[layer], queries, kv, log_total, docs, key_docs,
            normed, two, active, attended, *handed,
        )
        dx, shipped, d_fresh, *grads = result
        grad_now = dx.reshape(SEG, width)
        handed = [grads[6:8], [padded], grads[:6] + [shipped, d_fresh]]

    grad_query, grad_key, grad_value, grad_out, grad_up, grad_down = grads[:6]
    gain_attn_grad, gain_ffn_grad, grad_compress = grads[6:]
    return (
        outputs[None, None],
        shipped.reshape(2 * SEG, width)[None, None],
        gain_attn_grad,
        grad_query[None],
        grad_key[None],
        grad_value[None],
        grad_out[None],
        gain_ffn_grad,
        grad_up[None],
        grad_down[None],
        grad_compress[None],
    )


def solution(mesh):
    return jax.shard_map(
        shards,
        mesh=mesh,
        in_specs=(
            P("dp", None, None),
            P("dp", None),
            P("section", "dp", None, None),
            P("section", "dp", None, None),
            P("section", None),
            P("section", None, "tensor"),
            P("section", None, "tensor"),
            P("section", None, "tensor"),
            P("section", "tensor", None),
            P("section", None),
            P("section", None, "tensor"),
            P("section", "tensor", None),
            P("section", None, None, "tensor"),
            P("dp", None, None),
        ),
        out_specs=(
            P("section", "dp", None, None),
            P("section", "dp", None, None),
            P("section", "dp"),
            P("section", "dp", "tensor"),
            P("section", "dp", "tensor"),
            P("section", "dp", "tensor"),
            P("section", "tensor", "dp"),
            P("section", "dp"),
            P("section", "dp", "tensor"),
            P("section", "tensor", "dp"),
            P("section", None, "dp", "tensor"),
        ),
        check_vma=False,
    )
```

```python
import functools

import jax
import jax.numpy as jnp
from jax import lax
from jax.experimental import pallas as pl
from jax.experimental.pallas import tpu as pltpu
from jax.sharding import PartitionSpec as P

HD = 128
SEG = 512
MEM = 512
CMEM = 512
RATE = 3
COMP_ROWS = 171
PAD = 1
OLD_ROWS = CMEM - COMP_ROWS
CHUNKS = 4
ROWS = SEG // CHUNKS
FRESH_START = OLD_ROWS // 16 * 16

epsilon = 1e-06
masked_value = -1000000000.0
MESH = pl.DeviceIdType.MESH
f32 = jnp.float32
bf16 = jnp.bfloat16
GELU_A = 0.7978845608028654
GELU_B = 0.044715


def inverse_rms(rows):
    return lax.rsqrt(jnp.mean(rows * rows, axis=-1, keepdims=True) + epsilon)


def rms_pull(grad, rows, gain):
    scale = inverse_rms(rows)
    scaled_grad = grad * gain
    inner = jnp.mean(scaled_grad * rows, axis=-1, keepdims=True)
    return scale * (scaled_grad - rows * (scale * scale * inner))


def gelu(x):
    return 0.5 * x * (1.0 + jnp.tanh(GELU_A * (x + GELU_B * x * x * x)))


def gelu_slope(x):
    square = x * x
    bend = jnp.tanh(GELU_A * (x + GELU_B * x * square))
    return 0.5 * (1.0 + bend) + 0.5 * x * (1.0 - bend * bend) * GELU_A * (
        1.0 + 3.0 * GELU_B * square
    )


def dot_nn(a, b):
    return lax.dot_general(a, b, (((1,), (0,)), ((), ())), preferred_element_type=f32)


def dot_nt(a, b):
    return lax.dot_general(a, b, (((1,), (1,)), ((), ())), preferred_element_type=f32)


def dot_tn(a, b):
    return lax.dot_general(a, b, (((0,), (0,)), ((), ())), preferred_element_type=f32)


def greet(n, with_peer=False, groups=0):
    me = lax.axis_index("tensor")
    barrier = pltpu.get_barrier_semaphore()
    for step in (-1, 1):
        other = me + step

        @pl.when((other >= 0) & (other < n))
        def _():
            pl.semaphore_signal(barrier, inc=1, device_id={"tensor": other}, device_id_type=MESH)

    extra = 0
    if with_peer:
        extra += 1
        peer = 1 - lax.axis_index("section")
        pl.semaphore_signal(barrier, inc=1, device_id={"section": peer}, device_id_type=MESH)
    if groups:
        mine = lax.axis_index("dp")
        others = [mine + 1 - 2 * (mine % 2)]
        others += [(mine + 2 * step) % groups for step in range(1, groups // 2)]
        for other in others:
            pl.semaphore_signal(barrier, inc=1, device_id={"dp": other}, device_id_type=MESH)
        extra += len(others)
    pl.semaphore_wait(barrier, jnp.where((me > 0) & (me < n - 1), 2 + extra, 1 + extra))
    return me


class GridSum:
    def __init__(self, groups, home, tiles, landings, sems, parts):
        self.groups, self.home, self.tiles, self.parts = groups, home, tiles, parts
        self.from_core, self.from_row, self.from_section = landings
        self.core_sems, self.row_sems, self.section_sems = sems
        self.dp = lax.axis_index("dp")
        self.section = lax.axis_index("section")
        self.core = self.dp % 2
        self.row = self.dp // 2
        self.rows = groups // 2

    def span(self, part):
        start, stop = self.parts[part]
        return pl.ds(start, stop - start)

    def core_copy(self, part, row):
        return pltpu.make_async_remote_copy(
            src_ref=self.tiles.at[row * 2 + 1 - self.core, self.span(part)],
            dst_ref=self.from_core.at[row, self.span(part)],
            send_sem=self.core_sems.at[0, part, row],
            recv_sem=self.core_sems.at[1, part, row],
            device_id={"dp": self.dp + 1 - 2 * self.core},
            device_id_type=MESH,
        )

    def row_copy(self, part, step):
        target = (self.row + step) % self.rows
        return pltpu.make_async_remote_copy(
            src_ref=self.tiles.at[target * 2 + self.core, self.span(part)],
            dst_ref=self.from_row.at[step - 1, self.span(part)],
            send_sem=self.row_sems.at[0, part, step - 1],
            recv_sem=self.row_sems.at[1, part, step - 1],
            device_id={"dp": target * 2 + self.core},
            device_id_type=MESH,
        )

    def section_copy(self, part):
        return pltpu.make_async_remote_copy(
            src_ref=self.tiles.at[self.dp, self.span(part)],
            dst_ref=self.from_section.at[self.span(part)],
            send_sem=self.section_sems.at[0, part],
            recv_sem=self.section_sems.at[1, part],
            device_id={"section": 1 - self.section},
            device_id_type=MESH,
        )

    def add(self, place, landing, part):
        start, stop = self.parts[part]

        def body(tile, carry):
            self.tiles[place, tile] = (
                self.tiles[place, tile].astype(f32) + landing[tile].astype(f32)
            ).astype(bf16)
            return carry

        lax.fori_loop(start, stop, body, 0)

    def send_core(self, part):
        for row in range(self.rows):
            self.core_copy(part, row).start()

    def send_rows(self, part):
        for row in range(self.rows):
            self.core_copy(part, row).wait_recv()
            self.add(row * 2 + self.core, self.from_core.at[row], part)
        for step in range(1, self.rows):
            self.row_copy(part, step).start()

    def send_section(self, part):
        for step in range(1, self.rows):
            self.row_copy(part, step).wait_recv()
            self.add(self.dp, self.from_row.at[step - 1], part)

        @pl.when(self.section != self.home)
        def _():
            self.section_copy(part).start()

    def close(self, part, write):
        @pl.when(self.section == self.home)
        def _():
            self.section_copy(part).wait_recv()
            for tile in range(*self.parts[part]):
                write(
                    tile,
                    self.tiles[self.dp, tile].astype(f32) + self.from_section[tile].astype(f32),
                )

    def close_rows(self, part, write):
        for step in range(1, self.rows):
            self.row_copy(part, step).wait_recv()
        for tile in range(*self.parts[part]):
            total = self.tiles[self.dp, tile].astype(f32)
            for step in range(1, self.rows):
                total = total + self.from_row[step - 1, tile].astype(f32)
            write(tile, total)

    def finish(self, shared):
        for part in range(len(self.parts)):
            for row in range(self.rows):
                self.core_copy(part, row).wait_send()
            for step in range(1, self.rows):
                self.row_copy(part, step).wait_send()
            if part < shared:

                @pl.when(self.section != self.home)
                def _():
                    self.section_copy(part).wait_send()


def grid_scratch(groups, tiles, size, parts):
    rows = groups // 2
    return [
        pltpu.VMEM((groups, tiles, size, size), bf16),
        pltpu.VMEM((rows, tiles, size, size), bf16),
        pltpu.VMEM((rows - 1, tiles, size, size), bf16),
        pltpu.VMEM((tiles, size, size), bf16),
        pltpu.SemaphoreType.DMA((2, parts, rows)),
        pltpu.SemaphoreType.DMA((2, parts, rows - 1)),
        pltpu.SemaphoreType.DMA((2, parts)),
    ]


class LineSum:
    def __init__(self, n, me, middle, part, out, held, sems):
        self.n, self.me, self.middle, self.part, self.out = n, me, middle, part, out
        self.from_left, self.from_right = held
        self.rs_send, self.rs_recv, self.ag_send, self.ag_recv = sems
        self.stages = 2 * n - 1

    def reduce_copy(self, src, landing, side, chunk, block, target):
        return pltpu.make_async_remote_copy(
            src_ref=src,
            dst_ref=landing.at[chunk, block],
            send_sem=self.rs_send.at[side, chunk, block],
            recv_sem=self.rs_recv.at[side, chunk, block],
            device_id={"tensor": target},
            device_id_type=MESH,
        )

    def gather_copy(self, side, chunk, block, target):
        return pltpu.make_async_remote_copy(
            src_ref=self.out.at[chunk, block],
            dst_ref=self.out.at[chunk, block],
            send_sem=self.ag_send.at[side, chunk, block],
            recv_sem=self.ag_recv.at[chunk, block],
            device_id={"tensor": target},
            device_id_type=MESH,
        )

    def put(self, chunk, rows):
        self.part[chunk] = rows.astype(bf16).reshape(self.part.shape[1:])

    def rows(self, chunk):
        whole = self.out[chunk]
        return whole.reshape(-1, whole.shape[-1])

    def stage(self, chunk, stage):
        n = self.n
        if stage == 0:
            self.first_sends(chunk)
        elif stage <= n - 2:
            self.hop(chunk, stage)
        elif stage == n - 1:
            self.own_rows(chunk)
        else:
            self.forward(chunk, stage - n + 1)

    def first_sends(self, chunk):
        n, part = self.n, self.part

        @pl.when(self.me == 0)
        def _():
            for block in range(n - 1, 0, -1):
                self.reduce_copy(
                    part.at[chunk, block], self.from_left, 0, chunk, block, 1
                ).start()

        @pl.when(self.me == n - 1)
        def _():
            for block in range(n - 1):
                self.reduce_copy(
                    part.at[chunk, block], self.from_right, 1, chunk, block, n - 2
                ).start()

    def hop(self, chunk, step):
        n, part = self.n, self.part

        @pl.when(self.me == step)
        def _():
            landing = self.from_left
            for block in range(n - 1, step, -1):
                self.reduce_copy(
                    part.at[chunk, block], landing, 0, chunk, block, step
                ).wait_recv()
                part[chunk, block] = (
                    landing[chunk, block].astype(f32) + part[chunk, block].astype(f32)
                ).astype(bf16)
                self.reduce_copy(
                    part.at[chunk, block], landing, 0, chunk, block, step + 1
                ).start()

        @pl.when(self.me == n - 1 - step)
        def _():
            landing = self.from_right
            mine = n - 1 - step
            for block in range(mine):
                self.reduce_copy(
                    part.at[chunk, block], landing, 1, chunk, block, mine
                ).wait_recv()
                part[chunk, block] = (
                    landing[chunk, block].astype(f32) + part[chunk, block].astype(f32)
                ).astype(bf16)
                self.reduce_copy(
                    part.at[chunk, block], landing, 1, chunk, block, mine - 1
                ).start()

    def own_rows(self, chunk):
        n, me, part = self.n, self.me, self.part

        @pl.when(me > 0)
        def _():
            self.reduce_copy(part.at[chunk, me], self.from_left, 0, chunk, me, me).wait_recv()

        @pl.when(me < n - 1)
        def _():
            self.reduce_copy(part.at[chunk, me], self.from_right, 1, chunk, me, me).wait_recv()

        total = part[chunk, me].astype(f32)
        total = total + jnp.where(me > 0, self.from_left[chunk, me].astype(f32), 0.0)
        total = total + jnp.where(me < n - 1, self.from_right[chunk, me].astype(f32), 0.0)
        self.out[chunk, me] = self.middle(chunk, me, total).astype(bf16)

        @pl.when(me < n - 1)
        def _():
            self.gather_copy(0, chunk, me, me + 1).start()

        @pl.when(me > 0)
        def _():
            self.gather_copy(1, chunk, me, me - 1).start()

    def forward(self, chunk, step):
        n, me = self.n, self.me
        left_block = me - step

        @pl.when(left_block >= 0)
        def _():
            self.gather_copy(0, chunk, left_block, me).wait_recv()

            @pl.when(me < n - 1)
            def _():
                self.gather_copy(0, chunk, left_block, me + 1).start()

        right_block = me + step

        @pl.when(right_block < n)
        def _():
            self.gather_copy(1, chunk, right_block, me).wait_recv()

            @pl.when(me > 0)
            def _():
                self.gather_copy(1, chunk, right_block, me - 1).start()

    def finish(self):
        n, me, part = self.n, self.me, self.part
        for chunk in range(part.shape[0]):
            for block in range(n):

                @pl.when((me < n - 1) & (block > me))
                def _():
                    self.reduce_copy(
                        part.at[chunk, block], self.from_left, 0, chunk, block, me
                    ).wait_send()

                @pl.when((me > 0) & (block < me))
                def _():
                    self.reduce_copy(
                        part.at[chunk, block], self.from_right, 1, chunk, block, me
                    ).wait_send()

                @pl.when((me < n - 1) & (block <= me))
                def _():
                    self.gather_copy(0, chunk, block, me).wait_send()

                @pl.when((me > 0) & (block >= me))
                def _():
                    self.gather_copy(1, chunk, block, me).wait_send()


def line_scratch(chunks, n, block, width):
    return [pltpu.VMEM((chunks, n, block, width), bf16)] * 3 + [
        pltpu.SemaphoreType.DMA((2, chunks, n)),
        pltpu.SemaphoreType.DMA((2, chunks, n)),
        pltpu.SemaphoreType.DMA((2, chunks, n)),
        pltpu.SemaphoreType.DMA((chunks, n)),
    ]


def make_line(n, me, middle, out, scratch):
    return LineSum(n, me, middle, scratch[0], out, scratch[1:3], scratch[3:7])


def run_two(order, first, second, produce, between, finished, extra):
    lag = first.stages - 1
    last = len(order) - 1
    for slot in range(2 * lag + last + 1):
        if slot <= last:
            produce(order[slot])
        extra(slot)
        for place, chunk in enumerate(order):
            stage = slot - lag - place
            if 1 <= stage <= lag:
                second.stage(chunk, stage)
            if stage == lag:
                finished(chunk)
        for place, chunk in enumerate(order):
            stage = slot - place
            if 0 <= stage <= lag:
                first.stage(chunk, stage)
        if 0 <= slot - lag <= last:
            chunk = order[slot - lag]
            between(chunk)
            second.stage(chunk, 0)


def run_chain(order, sums, works, finished, extra):
    lag = sums[0].stages - 1
    last = len(order) - 1
    for slot in range(len(sums) * lag + last + 1):
        if slot <= last:
            works[0](order[slot])
        extra(slot)
        for level in range(len(sums) - 1, -1, -1):
            for place, chunk in enumerate(order):
                stage = slot - level * lag - place
                if min(level, 1) <= stage <= lag:
                    sums[level].stage(chunk, stage)
                if stage == lag:
                    finished(level, chunk)
        for level in range(len(sums) - 1, 0, -1):
            if 0 <= slot - level * lag <= last:
                chunk = order[slot - level * lag]
                works[level](chunk)
                sums[level].stage(chunk, 0)


class WeightSwap:
    def __init__(self, groups, own, layers, sems):
        self.groups, self.own, self.layers = groups, own, layers
        self.x_sems, self.row_sems, self.core_sems, self.local_sems = sems
        self.dp = lax.axis_index("dp")
        self.section = lax.axis_index("section")
        self.core = self.dp % 2
        self.row = self.dp // 2
        self.rows = groups // 2

    def share(self, array, piece):
        rows = self.own[array][0].shape[0] // self.groups
        return pl.ds(pl.multiple_of(piece * rows, rows), rows)

    def block(self, layer, array, piece):
        ref, lanes = self.layers[layer][array]
        return ref.at[self.share(array, piece), lanes]

    def section_copy(self, layer, array):
        ref, lanes = self.own[array]
        return pltpu.make_async_remote_copy(
            src_ref=ref.at[self.share(array, self.dp), lanes],
            dst_ref=self.block(layer, array, self.dp),
            send_sem=self.x_sems.at[0, array],
            recv_sem=self.x_sems.at[1, array],
            device_id={"section": 1 - self.section},
            device_id_type=MESH,
        )

    def row_copy(self, layer, array, step, source, target):
        piece = source * 2 + self.core
        return pltpu.make_async_remote_copy(
            src_ref=self.block(layer, array, piece),
            dst_ref=self.block(layer, array, piece),
            send_sem=self.row_sems.at[0, array, step - 1],
            recv_sem=self.row_sems.at[1, array, step - 1],
            device_id={"dp": target * 2 + self.core},
            device_id_type=MESH,
        )

    def core_copy(self, layer, array, step, core):
        piece = (self.row - step) % self.rows * 2 + core
        return pltpu.make_async_remote_copy(
            src_ref=self.block(layer, array, piece),
            dst_ref=self.block(layer, array, piece),
            send_sem=self.core_sems.at[0, array, step],
            recv_sem=self.core_sems.at[1, array, step],
            device_id={"dp": self.dp + 1 - 2 * self.core},
            device_id_type=MESH,
        )

    def local_copy(self, layer, array):
        ref, lanes = self.own[array]
        to, to_lanes = self.layers[layer][array]
        return pltpu.make_async_copy(
            ref.at[:, lanes], to.at[:, to_lanes], self.local_sems.at[array]
        )

    def take(self, layer, arrays):
        for array in arrays:
            self.section_copy(layer, array).wait_recv()
            for step in range(1, self.rows):
                target = (self.row + step) % self.rows
                self.row_copy(layer, array, step, self.row, target).start()
            self.core_copy(layer, array, 0, self.core).start()

    def spread(self, layer, arrays):
        for array in arrays:
            for step in range(1, self.rows):
                source = (self.row - step) % self.rows
                self.row_copy(layer, array, step, source, self.row).wait_recv()
                self.core_copy(layer, array, step, self.core).start()

    def settle(self, layer, arrays):
        for array in arrays:
            for step in range(self.rows):
                self.core_copy(layer, array, step, 1 - self.core).wait_recv()

    def on_arrival(self, work, arrays):
        for layer in range(2):

            @pl.when(self.section != layer)
            def _():
                work(layer, arrays)

    def finish(self):
        for layer in range(2):
            for array in range(len(self.own)):

                @pl.when(self.section == layer)
                def _():
                    self.section_copy(layer, array).wait_send()

                @pl.when(self.section != layer)
                def _():
                    for step in range(1, self.rows):
                        target = (self.row + step) % self.rows
                        self.row_copy(layer, array, step, self.row, target).wait_send()
                    for step in range(self.rows):
                        self.core_copy(layer, array, step, self.core).wait_send()


class LineGather:
    def __init__(self, n, me, place, sems):
        self.n, self.me, self.place = n, me, place
        self.send, self.recv = sems

    def copy(self, side, block, target):
        return pltpu.make_async_remote_copy(
            src_ref=self.place(block),
            dst_ref=self.place(block),
            send_sem=self.send.at[side, block],
            recv_sem=self.recv.at[block],
            device_id={"tensor": target},
            device_id_type=MESH,
        )

    def start(self):
        n, me = self.n, self.me

        @pl.when(me < n - 1)
        def _():
            self.copy(0, me, me + 1).start()

        @pl.when(me > 0)
        def _():
            self.copy(1, me, me - 1).start()

    def forward(self, step):
        n, me = self.n, self.me
        left_block = me - step

        @pl.when(left_block >= 0)
        def _():
            self.copy(0, left_block, me).wait_recv()

            @pl.when(me < n - 1)
            def _():
                self.copy(0, left_block, me + 1).start()

        right_block = me + step

        @pl.when(right_block < n)
        def _():
            self.copy(1, right_block, me).wait_recv()

            @pl.when(me > 0)
            def _():
                self.copy(1, right_block, me - 1).start()

    def finish(self):
        n, me = self.n, self.me
        for block in range(n):

            @pl.when((me < n - 1) & (block <= me))
            def _():
                self.copy(0, block, me).wait_send()

            @pl.when((me > 0) & (block >= me))
            def _():
                self.copy(1, block, me).wait_send()


def columns_of(ref, lanes):
    def place(block):
        at = pl.ds(pl.multiple_of(block * lanes, lanes), lanes)
        return ref.at[FRESH_START:CMEM, at]

    return place


def score_columns(head, chunk, q_ref, kv_ref, docs, keys_docs):
    lanes = slice(head * HD, (head + 1) * HD)
    width = CMEM + MEM + (chunk + 1) * ROWS
    query = q_ref[chunk * ROWS : (chunk + 1) * ROWS, lanes]
    scores = dot_nt(kv_ref[:width, lanes], query) * HD ** (-0.5)
    own = docs[:, chunk * ROWS : (chunk + 1) * ROWS]
    same = keys_docs[: MEM + chunk * ROWS, :] == own
    tail_docs = keys_docs[MEM + chunk * ROWS : MEM + (chunk + 1) * ROWS, :]
    key_place = lax.broadcasted_iota(jnp.int32, (ROWS, ROWS), 0)
    query_place = lax.broadcasted_iota(jnp.int32, (ROWS, ROWS), 1)
    tail_same = (tail_docs == own) & (key_place <= query_place)
    middle_end = CMEM + MEM + chunk * ROWS
    return jnp.concatenate(
        [
            scores[:CMEM],
            jnp.where(same, scores[CMEM:middle_end], masked_value),
            jnp.where(tail_same, scores[middle_end:], masked_value),
        ],
        axis=0,
    )


class ForwardLayer:
    def __init__(self, n, me, weights, x_ref, saved, out, docs, keys_docs, scratch):
        self.wq, self.wkv, self.wo, self.wup, self.wdown, self.gains, self.c_ref = weights
        (self.normed, self.q_ref, self.kv_ref, self.log_sum, self.attended, self.residual,
         self.two, self.hidden, self.active) = saved
        self.x_ref, self.docs, self.keys_docs = x_ref, docs, keys_docs
        self.values_t, first_scratch, second_scratch = scratch[0], scratch[1:8], scratch[8:15]
        self.local = self.wq.shape[1]
        self.heads = self.local // HD
        self.first = make_line(n, me, self.attention_middle, self.two, first_scratch)
        self.second = make_line(n, me, self.output_middle, out, second_scratch)

    def project(self, wide, at):
        block = (wide * inverse_rms(wide) * self.gains[0:1, :]).astype(bf16)
        self.normed[at, :] = block
        self.kv_ref[at, :] = dot_nn(block, self.wkv[...]).astype(bf16)
        return block

    def flip_values(self, rows):
        for head in range(self.heads):
            lanes = slice(self.local + head * HD, self.local + (head + 1) * HD)
            self.values_t[head, :, rows] = self.kv_ref[rows, lanes].astype(f32).T.astype(bf16)

    def project_block(self, source, place):
        def body(step, carry):
            rows = pl.ds(pl.multiple_of(step * 256, 256), 256)
            at = pl.ds(pl.multiple_of(place * SEG + step * 256, 256), 256)
            self.project(source[rows, :].astype(f32), at)
            return carry

        lax.fori_loop(0, SEG // 256, body, 0)
        self.flip_values(slice(place * SEG, (place + 1) * SEG))

    def attention_middle(self, chunk, me, total):
        rows = self.x_ref[chunk, me].astype(f32) + total
        self.residual[chunk] = rows
        return rows * inverse_rms(rows) * self.gains[1:2, :]

    def output_middle(self, chunk, me, total):
        return self.residual[chunk] + total

    def attend(self, chunk):
        rows = slice(chunk * ROWS, (chunk + 1) * ROWS)
        at = slice(CMEM + MEM + chunk * ROWS, CMEM + MEM + (chunk + 1) * ROWS)
        source = self.x_ref[chunk]
        block = self.project(source.reshape(ROWS, source.shape[-1]).astype(f32), at)
        self.q_ref[rows, :] = dot_nn(block, self.wq[...]).astype(bf16)
        self.flip_values(at)
        for head in range(self.heads):
            lanes = slice(head * HD, (head + 1) * HD)
            scores = score_columns(
                head, chunk, self.q_ref, self.kv_ref, self.docs, self.keys_docs
            )
            top = jnp.max(scores, axis=0, keepdims=True)
            powers = jnp.exp(scores - top)
            total = jnp.sum(powers, axis=0, keepdims=True)
            self.log_sum[head : head + 1, rows] = top + jnp.log(total)
            weights = (powers * (1.0 / total)).astype(bf16)
            mixed = dot_nn(self.values_t[head, :, : weights.shape[0]], weights)
            self.attended[rows, lanes] = mixed.T.astype(bf16)
        self.first.put(chunk, dot_nn(self.attended[rows, :], self.wo[...]))

    def feed(self, chunk):
        rows = slice(chunk * ROWS, (chunk + 1) * ROWS)
        before = dot_nn(self.first.rows(chunk), self.wup[...])
        self.hidden[rows, :] = before
        after = gelu(before).astype(bf16)
        self.active[rows, :] = after
        self.second.put(chunk, dot_nn(after, self.wdown[...]))


def forward_kernel(n, groups, *refs):
    m_ref, x_ref, own_gains, docs, key_docs = refs[:5]
    own_refs, (old, piece, compressed, memory) = refs[5:11], refs[11:15]
    saved = [refs[15:24], refs[24:33]]
    middle_rows, shipped, outputs = refs[33:36]
    layer_refs = [refs[36:43], refs[43:50]]
    keys_docs, last_rows = refs[50:52]
    scratch = [refs[52:67], refs[67:82]]
    (ship_send, ship_recv, final_send, final_recv, keep, *swap_sems, item_sems, local_sems) = (
        refs[82:93]
    )
    gather_sems = refs[93:97]
    me = greet(n, True, groups)
    section = lax.axis_index("section")
    wq, wup = layer_refs[0][0], layer_refs[0][3]
    local, inner, width = wq.shape[1], wup.shape[1], wup.shape[0]
    whole = slice(None)
    front, back = slice(0, inner // 2), slice(inner // 2, inner)
    lead, trail = slice(0, width // 2), slice(width // 2, width)
    q_own, k_own, v_own, o_own, up_own, down_own = own_refs
    own = [(q_own, whole), (k_own, whole), (v_own, whole), (o_own, whole),
           (up_own, front), (up_own, back), (down_own, lead), (down_own, trail)]
    places = [
        [(w[0], whole), (w[1], slice(0, local)), (w[1], slice(local, 2 * local)),
         (w[2], whole), (w[3], front), (w[3], back), (w[4], lead), (w[4], trail)]
        for w in layer_refs
    ]
    swap = WeightSwap(groups, own, places, swap_sems)
    gathers = [
        LineGather(n, me, columns_of(layer_refs[layer][6], local),
                   gather_sems[2 * layer : 2 * layer + 2])
        for layer in range(2)
    ]
    items = [
        [(own_gains, layer_refs[0][5]), (piece, gathers[0].place(me)),
         (old, layer_refs[0][6].at[:FRESH_START, :])],
        [(own_gains, layer_refs[1][5]), (compressed, layer_refs[1][6]), (memory, shipped)],
    ]

    def peer_copy(src, dst, send, recv):
        return pltpu.make_async_remote_copy(
            src_ref=src,
            dst_ref=dst,
            send_sem=send,
            recv_sem=recv,
            device_id={"section": 1 - section},
            device_id_type=MESH,
        )

    def item_copy(layer, index):
        src, dst = items[layer][index]
        return peer_copy(src, dst, item_sems.at[0, index], item_sems.at[1, index])

    local_rows = [
        pltpu.make_async_copy(compressed, layer_refs[0][6], local_sems.at[0]),
        pltpu.make_async_copy(old, layer_refs[1][6].at[:FRESH_START, :], local_sems.at[0]),
        pltpu.make_async_copy(piece, gathers[1].place(me), local_sems.at[1]),
    ]
    keys_docs[...] = jnp.broadcast_to(key_docs[...], keys_docs.shape)
    layers = [
        ForwardLayer(n, me, layer_refs[0], x_ref, saved[0], middle_rows, docs, keys_docs,
                     scratch[0]),
        ForwardLayer(n, me, layer_refs[1], middle_rows, saved[1], last_rows, docs, keys_docs,
                     scratch[1]),
    ]

    @pl.when(section == 0)
    def _():
        item_copy(0, 0).start()
        item_copy(0, 1).start()
        for array in range(3):
            swap.section_copy(0, array).start()
        item_copy(0, 2).start()
        for array in range(3, 8):
            swap.section_copy(0, array).start()
        for array in range(3):
            swap.local_copy(0, array).start()
        local_rows[0].start()
        for array in range(3, 8):
            swap.local_copy(0, array).start()
        layer_refs[0][5][...] = own_gains[...]
        local_rows[0].wait()
        for array in range(8):
            swap.local_copy(0, array).wait()

    @pl.when(section == 1)
    def _():
        item_copy(1, 0).start()
        for array in range(3):
            swap.section_copy(1, array).start()
        item_copy(1, 1).start()
        item_copy(1, 2).start()
        for array in range(3, 8):
            swap.section_copy(1, array).start()
        local_rows[1].start()
        local_rows[2].start()
        for array in range(8):
            swap.local_copy(1, array).start()
        layer_refs[1][5][...] = own_gains[...]
        item_copy(0, 0).wait_recv()
        item_copy(0, 1).wait_recv()
        gathers[0].start()
        swap.take(0, range(3))
        gathers[0].forward(1)
        swap.spread(0, range(3))
        for step in range(2, n):
            gathers[0].forward(step)
        swap.settle(0, range(3))

    layers[0].project_block(m_ref, 1)

    @pl.when(section == 1)
    def _():
        item_copy(0, 2).wait_recv()

    layers[0].project_block(layer_refs[0][6], 0)

    @pl.when(section == 1)
    def _():
        swap.take(0, [3])
        swap.spread(0, [3])
        swap.settle(0, [3])

    lag = 2 * n - 2
    plans = [
        {
            1: [(swap.take, range(3))],
            2: [(swap.spread, range(3))],
            3: [(swap.settle, range(3))],
            10: [(swap.take, [3])],
            11: [(swap.spread, [3])],
            12: [(swap.settle, [3])],
            13: [(swap.take, [4])],
            14: [(swap.spread, [4]), (swap.take, [5])],
            15: [(swap.spread, [5]), (swap.take, [6])],
            16: [(swap.spread, [6]), (swap.take, [7])],
            17: [(swap.spread, [7]), (swap.settle, [4, 5])],
            18: [(swap.settle, [6, 7])],
        },
        {
            2: [(swap.take, [4])],
            3: [(swap.take, [5]), (swap.spread, [4])],
            4: [(swap.spread, [5]), (swap.take, [6])],
            5: [(swap.take, [7]), (swap.spread, [6]), (swap.settle, [4, 5])],
            6: [(swap.spread, [7]), (swap.settle, [6, 7])],
        },
    ]

    def ship_copy(chunk):
        return peer_copy(
            middle_rows.at[chunk], shipped.at[chunk], ship_send.at[chunk], ship_recv.at[chunk]
        )

    def final_copy(layer, chunk):
        rows = (middle_rows, last_rows)[layer]
        return peer_copy(
            rows.at[chunk], outputs.at[1 - layer, chunk], final_send.at[chunk],
            final_recv.at[chunk],
        )

    def keep_copy(layer, chunk):
        rows = (middle_rows, last_rows)[layer]
        return pltpu.make_async_copy(rows.at[chunk], outputs.at[layer, chunk], keep.at[chunk])

    def finished(level, chunk):
        if level == 1:

            @pl.when(section == 0)
            def _():
                ship_copy(chunk).start()
                keep_copy(0, chunk).start()

            @pl.when(section == 1)
            def _():
                final_copy(0, chunk).start()

        if level == 3:

            @pl.when(section == 0)
            def _():
                final_copy(1, chunk).start()

            @pl.when(section == 1)
            def _():
                keep_copy(1, chunk).start()

    def extra(slot):
        for place in range(2):
            if slot in plans[place]:

                @pl.when(section == place)
                def _():
                    for work, arrays in plans[place][slot]:
                        work(1 - place, arrays)

        if slot < n:

            @pl.when(section == 1)
            def _():
                if slot == 0:
                    local_rows[2].wait()
                    gathers[1].start()
                else:
                    gathers[1].forward(slot)

        if slot == lag + 2:

            @pl.when(section == 0)
            def _():
                item_copy(1, 0).wait_recv()
                item_copy(1, 1).wait_recv()

            @pl.when(section == 1)
            def _():
                local_rows[1].wait()
                for array in range(8):
                    swap.local_copy(1, array).wait()

            layers[1].project_block(layer_refs[1][6], 0)
        if slot == 2 * lag - 1:

            @pl.when(section == 0)
            def _():
                item_copy(1, 2).wait_recv()

            @pl.when(section == 1)
            def _():
                for chunk in range(CHUNKS):
                    ship_copy(chunk).wait_recv()

            layers[1].project_block(shipped.reshape(MEM, width), 1)

    sums = [layers[0].first, layers[0].second, layers[1].first, layers[1].second]
    works = [layers[0].attend, layers[0].feed, layers[1].attend, layers[1].feed]
    run_chain(list(range(CHUNKS)), sums, works, finished, extra)
    for line in sums:
        line.finish()
    swap.finish()

    @pl.when(section == 0)
    def _():
        for chunk in range(CHUNKS):
            ship_copy(chunk).wait_send()
            keep_copy(0, chunk).wait()
            final_copy(1, chunk).wait_send()
            final_copy(0, chunk).wait_recv()
        for index in range(3):
            item_copy(0, index).wait_send()

    @pl.when(section == 1)
    def _():
        for chunk in range(CHUNKS):
            keep_copy(1, chunk).wait()
            final_copy(0, chunk).wait_send()
            final_copy(1, chunk).wait_recv()
        for index in range(3):
            item_copy(1, index).wait_send()
        for gather in gathers:
            gather.finish()


def vmem_specs(count):
    return [pl.BlockSpec(memory_space=pltpu.VMEM)] * count


def forward(collective, n, groups, m_rows, x_rows, gains, docs, key_docs, own, old, piece,
            compressed, memory):
    width, local, inner = x_rows.shape[1], own[0].shape[1], own[4].shape[1]
    block = ROWS // n
    shape = jax.ShapeDtypeStruct
    rows = shape((CHUNKS, n, block, width), bf16)
    saved = [
        shape((CMEM + MEM + SEG, width), bf16),
        shape((SEG, local), bf16),
        shape((CMEM + MEM + SEG, 2 * local), bf16),
        shape((8, SEG), f32),
        shape((SEG, local), bf16),
        shape((CHUNKS, block, width), f32),
        rows,
        shape((SEG, inner), f32),
        shape((SEG, inner), bf16),
    ]
    layer = [
        shape((width, local), bf16),
        shape((width, 2 * local), bf16),
        shape((local, width), bf16),
        shape((width, inner), bf16),
        shape((inner, width), bf16),
        shape(gains.shape, f32),
        shape((CMEM, width), bf16),
    ]
    outs = saved + saved + [rows, rows, shape((2,) + rows.shape, bf16)] + layer + layer
    arrays, rows_y = 8, groups // 2
    dma = pltpu.SemaphoreType.DMA
    layer_scratch = (
        [pltpu.VMEM((local // HD, HD, CMEM + MEM + SEG), bf16)]
        + line_scratch(CHUNKS, n, block, width)
        + line_scratch(CHUNKS, n, block, width)
    )
    scratch = [
        pltpu.VMEM((MEM + SEG, HD), jnp.int32),
        pltpu.VMEM(rows.shape, bf16),
        *layer_scratch,
        *layer_scratch,
        dma((CHUNKS,)),
        dma((CHUNKS,)),
        dma((CHUNKS,)),
        dma((CHUNKS,)),
        dma((CHUNKS,)),
        dma((2, arrays)),
        dma((2, arrays, rows_y - 1)),
        dma((2, arrays, rows_y)),
        dma((arrays,)),
        dma((2, 3)),
        dma((2,)),
        dma((2, n)),
        dma((n,)),
        dma((2, n)),
        dma((n,)),
    ]
    any_space = pl.BlockSpec(memory_space=pl.ANY)
    result = pl.pallas_call(
        functools.partial(forward_kernel, n, groups),
        name="forward",
        out_shape=outs,
        in_specs=vmem_specs(5) + [any_space] * 10,
        out_specs=vmem_specs(20) + [any_space] + vmem_specs(14),
        scratch_shapes=scratch,
        compiler_params=pltpu.CompilerParams(
            collective_id=collective, has_side_effects=True, vmem_limit_bytes=65000 * 1024
        ),
    )(m_rows, x_rows.reshape(rows.shape), gains, docs, key_docs, *own, old, piece, compressed,
      memory.reshape(rows.shape))
    return result[:9], result[9:18], result[18:21], result[21:28], result[28:35]


def backward_kernel(n, groups, home, *refs):
    (g_ref, x_ref, residual, hidden, fresh, wq, wkv, wo, wup, wdown, gains, q_ref, kv_ref,
     log_sum, docs, key_docs, normed, two, active, attended) = refs[:20]
    last = home == 0
    rest = refs[20:]
    if last:
        earlier_gains, padded, earlier, rest = rest[:2], rest[2], rest[3:11], rest[11:]
    dx_ref, shipped, d_fresh = rest[:3]
    results, gain_results, rest = rest[3:9], rest[9:11], rest[11:]
    grad_query, grad_key, grad_value, grad_out, grad_up, grad_down = results
    if last:
        grad_compress, rest = rest[0], rest[1:]
    d_hidden, d_branch, dq_ref, dkv_ref, d_residual, keys_docs, keys_t, sums = rest[:8]
    rest = rest[8:]
    first_scratch, second_scratch, fresh_scratch = rest[:7], rest[7:14], rest[14:21]
    tiles, grid_rest = rest[21], rest[22:28]
    ship_send, ship_recv = rest[28:30]
    gain_sums, gain_blocks, gain_send, gain_recv = rest[30:34]
    if last:
        fresh_columns, keep, keep_rows, fresh_sems = rest[34:38]
    me = greet(n, True, groups)
    section = lax.axis_index("section")
    late = section == 1
    local = wq.shape[1]
    heads = local // HD
    gain_a = gains[0:1, :]
    gain_f = gains[1:2, :]
    scale = HD ** (-0.5)

    keys_docs[...] = jnp.broadcast_to(key_docs[...], keys_docs.shape)
    for head in range(heads):
        lanes = slice(head * HD, (head + 1) * HD)
        keys_t[head] = kv_ref[:, lanes].astype(f32).T.astype(bf16)

    def branch_middle(chunk, me, total):
        rows = g_ref[chunk, me].astype(f32) + rms_pull(total, residual[chunk], gain_f)
        d_residual[chunk] = rows
        return rows

    def input_middle(chunk, me, total):
        return d_residual[chunk] + rms_pull(total, x_ref[chunk, me].astype(f32), gain_a)

    def fresh_middle(chunk, me, total):
        return rms_pull(total, fresh[chunk, me].astype(f32), gain_a)

    first = make_line(n, me, branch_middle, d_branch, first_scratch)
    second = make_line(n, me, input_middle, dx_ref, second_scratch)
    third = make_line(n, me, fresh_middle, d_fresh, fresh_scratch)

    def produce(chunk):
        rows = slice(chunk * ROWS, (chunk + 1) * ROWS)
        grad = g_ref[chunk]
        d_active = dot_nt(grad.reshape(ROWS, grad.shape[-1]), wdown[...])
        block = (gelu_slope(hidden[rows, :]) * d_active).astype(bf16)
        d_hidden[rows, :] = block
        first.put(chunk, dot_nt(block, wup[...]))

    def attend_back(chunk):
        rows = slice(chunk * ROWS, (chunk + 1) * ROWS)
        d_attended = dot_nt(first.rows(chunk), wo[...]).astype(bf16)
        fresh_sum = chunk == CHUNKS - 1
        for head in range(heads):
            lanes = slice(head * HD, (head + 1) * HD)
            value_lanes = slice(local + head * HD, local + (head + 1) * HD)
            scores = score_columns(head, chunk, q_ref, kv_ref, docs, keys_docs)
            size = scores.shape[0]
            probs = jnp.exp(scores - log_sum[head : head + 1, rows])
            d_mixed = d_attended[:, lanes]
            d_values = dot_nn(probs.astype(bf16), d_mixed)
            d_probs = dot_nt(kv_ref[:size, value_lanes], d_mixed)
            inner = jnp.sum(d_probs * probs, axis=0, keepdims=True)
            d_scores = (probs * (d_probs - inner)).astype(bf16)
            d_keys = dot_nn(d_scores, q_ref[rows, lanes])
            d_queries = dot_nn(keys_t[head, :, :size], d_scores) * scale
            dq_ref[rows, lanes] = d_queries.T.astype(bf16)
            if fresh_sum:
                sums[:size, lanes] = d_keys
                sums[:size, value_lanes] = d_values
            else:
                sums[:size, lanes] += d_keys
                sums[:size, value_lanes] += d_values
        own = slice(CMEM + MEM + chunk * ROWS, CMEM + MEM + (chunk + 1) * ROWS)
        close_rows(own)
        second.put(
            chunk, dot_nt(dq_ref[rows, :], wq[...]) + dot_nt(dkv_ref[own, :], wkv[...])
        )
        if chunk == 0:
            close_rows(slice(0, CMEM + MEM))

            @pl.when(late)
            def _():
                count = third.part.shape[1] * third.part.shape[2]
                third.put(0, dot_nt(dkv_ref[FRESH_START : FRESH_START + count, :], wkv[...]))
                third.stage(0, 0)

    def close_rows(rows):
        dkv_ref[rows, :local] = (sums[rows, :local] * scale).astype(bf16)
        dkv_ref[rows, local:] = sums[rows, local:].astype(bf16)

    size = wq.shape[0] // groups
    wide = hidden.shape[1] // size
    up_at, down_at, fresh_at = 4, 4 + wide, 4 + 2 * wide
    parts = [(down_at, fresh_at), (up_at, down_at), (0, 2), (2, 4)]
    shared = len(parts)
    if last:
        parts.append((fresh_at, fresh_at + RATE))
    grid = GridSum(groups, home, tiles, grid_rest[:3], grid_rest[3:6], parts)
    half = groups // 2
    g_rows = g_ref.reshape(SEG, g_ref.shape[-1])
    two_rows = two.reshape(SEG, two.shape[-1])
    branch_rows = d_branch.reshape(SEG, d_branch.shape[-1])

    def each_block(start, stop, work):
        def body(block, carry):
            work(block, pl.ds(pl.multiple_of(block * size, size), size))
            return carry

        lax.fori_loop(start, stop, body, 0)

    def put_tiles(block, at, value):
        for tile in range(value.shape[1] // size):
            tiles[block, at + tile] = value[:, tile * size : (tile + 1) * size].astype(bf16)

    def down_block(block, lanes):
        put_tiles(block, down_at, dot_tn(g_rows[:, lanes], active[...]))

    def up_block(block, lanes):
        put_tiles(block, up_at, dot_tn(two_rows[:, lanes], d_hidden[...]))

    def small_block(block, lanes):
        put_tiles(block, 0, dot_tn(normed[CMEM + MEM :, lanes], dq_ref[...]))
        put_tiles(block, 1, dot_tn(branch_rows[:, lanes], attended[...]))

    def kv_block(block, lanes):
        put_tiles(block, 2, dot_tn(normed[:, lanes], dkv_ref[...]))

    share = pl.ds(pl.multiple_of(grid.dp * size, size), size)
    gain_sums[...] = jnp.zeros(gain_sums.shape, f32)

    def write(tile, value):
        if tile >= down_at:
            grad_down[(tile - down_at) * size : (tile - down_at + 1) * size, :] = value.T
        elif tile >= up_at:
            lanes = slice((tile - up_at) * size, (tile - up_at + 1) * size)
            grad_up[:, lanes] = value
            gain_sums[1] += wup[share, lanes].astype(f32) * value
        elif tile == 1:
            grad_out[...] = value.T
        elif tile == 0:
            grad_query[...] = value
            gain_sums[0] += wq[share, :].astype(f32) * value
        else:
            (grad_key, grad_value)[tile - 2][...] = value
            lanes = slice((tile - 2) * local, (tile - 1) * local)
            gain_sums[0] += wkv[share, lanes].astype(f32) * value

    gain_gather = LineGather(
        n, me, lambda block: gain_blocks.at[block], (gain_send, gain_recv)
    )

    first_slot = 2 * n - 2
    plan = {
        1: [lambda: each_block(0, half, down_block)],
        2: [lambda: each_block(half, groups, down_block), lambda: grid.send_core(0)],
        4: [lambda: each_block(0, half, up_block), lambda: grid.send_rows(0)],
        5: [lambda: each_block(half, groups, up_block), lambda: grid.send_core(1)],
        first_slot: [lambda: grid.send_rows(1)],
        first_slot + 1: [lambda: grid.send_section(0)],
        first_slot + 2: [lambda: grid.send_section(1)],
        first_slot + 3: [lambda: grid.close(0, write)],
        first_slot + 4: [
            lambda: each_block(0, groups, small_block), lambda: grid.send_core(2),
        ],
        first_slot + 5: [lambda: each_block(0, half, kv_block), lambda: grid.send_rows(2)],
        first_slot + 6: [
            lambda: each_block(half, groups, kv_block), lambda: grid.send_core(3),
            lambda: grid.send_section(2), lambda: grid.close(1, write),
        ],
        first_slot + 7: [lambda: grid.send_rows(3)],
        first_slot + 8: [lambda: grid.close(2, write)],
        first_slot + 9: [lambda: grid.send_section(3)],
    }

    def ship_copy(chunk):
        return pltpu.make_async_remote_copy(
            src_ref=dx_ref.at[chunk],
            dst_ref=shipped.at[1, chunk] if last else shipped.at[chunk],
            send_sem=ship_send.at[chunk],
            recv_sem=ship_recv.at[chunk],
            device_id={"section": 1 - section},
            device_id_type=MESH,
        )

    def finished(chunk):
        @pl.when(section != home)
        def _():
            ship_copy(chunk).start()

        if last:

            @pl.when(section == home)
            def _():
                keep_row(chunk).start()

    if last:
        earlier_shipped, earlier_fresh = earlier[6:]
        columns = pl.ds(pl.multiple_of(me * local, local), local)

        def keep_row(chunk):
            return pltpu.make_async_copy(
                dx_ref.at[chunk], shipped.at[0, chunk], keep_rows.at[chunk]
            )

        kept = [
            pltpu.make_async_copy(src, dst, keep.at[index])
            for index, (src, dst) in enumerate(zip(earlier[:6], results))
        ] + [
            pltpu.make_async_copy(earlier_shipped, shipped.at[0], keep.at[6]),
            pltpu.make_async_copy(g_ref, shipped.at[1], keep.at[7]),
            pltpu.make_async_copy(
                earlier_fresh.at[0, :, :, columns], fresh_columns, keep.at[8]
            ),
        ]
        fresh_copy = pltpu.make_async_remote_copy(
            src_ref=d_fresh.at[0, :, :, columns],
            dst_ref=fresh_columns,
            send_sem=fresh_sems.at[0],
            recv_sem=fresh_sems.at[1],
            device_id={"section": 1 - section},
            device_id_type=MESH,
        )

        @pl.when(late)
        def _():
            for copy in kept:
                copy.start()
            for index in range(2):
                gain_results[index][...] = earlier_gains[index][...]

    def compress_block(block, lanes):
        rows = fresh_columns.reshape(padded.shape[0], local)[...]
        for place in range(RATE):
            at = pl.ds(pl.multiple_of(place * wo.shape[1] + block * size, size), size)
            put_tiles(block, fresh_at + place, dot_tn(padded[:, at], rows))

    def write_compress(tile, value):
        grad_compress[tile - fresh_at] = value

    def extra(slot):
        for action in plan.get(slot, ()):
            action()
        step = slot - (first_slot + CHUNKS - 1)
        if 0 < step < third.stages:

            @pl.when(late)
            def _():
                third.stage(0, step)

    run_two(
        list(range(CHUNKS - 1, -1, -1)), first, second, produce, attend_back, finished, extra,
    )
    if last:

        @pl.when(late)
        def _():
            fresh_copy.start()
            for copy in kept:
                copy.wait()

        @pl.when(section == home)
        def _():
            fresh_copy.wait_recv()

        each_block(0, groups, compress_block)
        grid.send_core(4)
    grid.close(3, write)

    @pl.when(section == home)
    def _():
        gain_blocks[me] = jnp.zeros(gain_blocks.shape[1:], f32)
        for index in range(2):
            gain_blocks[me, index : index + 1, :] = jnp.sum(
                gain_sums[index].T, axis=0, keepdims=True
            )
        gain_gather.start()

    if last:
        grid.send_rows(4)

    @pl.when(section == home)
    def _():
        for step in range(1, n):
            gain_gather.forward(step)
        total = gain_blocks[0]
        for block in range(1, n):
            total = total + gain_blocks[block]
        for index in range(2):
            gain_results[index][...] = (
                total[index : index + 1, :] / gains[index : index + 1, share]
            )
        gain_gather.finish()

    first.finish()
    second.finish()
    if last:
        grid.close_rows(4, write_compress)
    grid.finish(shared)
    for chunk in range(CHUNKS):

        @pl.when(section != home)
        def _():
            ship_copy(chunk).wait_send()

        @pl.when(section == home)
        def _():
            ship_copy(chunk).wait_recv()
            if last:
                keep_row(chunk).wait()

    @pl.when(late)
    def _():
        third.finish()
        if last:
            fresh_copy.wait_send()


def fresh_block(n):
    return -(-(CMEM - FRESH_START) // (16 * n)) * 16


def backward_layer(collective, n, groups, home, grad, x_rows, residual, hidden, fresh, weights,
                   gains, q, kv, log_sum, docs, key_docs, normed, two, active, attended,
                   earlier_gains=(), padded=(), earlier=()):
    wq, wkv, wo, wup, wdown = weights
    width = wo.shape[1]
    local = wq.shape[1]
    block = ROWS // n
    size = width // groups
    inner = wup.shape[1]
    last = home == 0
    shape = jax.ShapeDtypeStruct
    any_space = pl.BlockSpec(memory_space=pl.ANY)
    rows = shape((CHUNKS, n, block, width), bf16)
    ship = shape((2,) + rows.shape, bf16) if last else rows
    fresh_shape = (n, fresh_block(n), width)
    outs = [rows, ship, shape((1,) + fresh_shape, bf16)]
    outs += [shape((size, local), f32)] * 3
    outs += [shape((local, size), f32), shape((size, inner), f32), shape((inner, size), f32)]
    outs += [shape((1, size), f32)] * 2
    out_specs = vmem_specs(1) + [any_space] + vmem_specs(9)
    tile_count = 4 + 2 * inner // size
    dma = pltpu.SemaphoreType.DMA
    if last:
        outs.append(shape((RATE, size, local), f32))
        out_specs += vmem_specs(1)
        tile_count += RATE
    return pl.pallas_call(
        functools.partial(backward_kernel, n, groups, home),
        name="backward_%d" % home,
        out_shape=outs,
        in_specs=vmem_specs(20 + (3 if last else 0)) + [any_space] * len(earlier),
        out_specs=out_specs,
        scratch_shapes=[
            pltpu.VMEM((SEG, inner), bf16),
            pltpu.VMEM(rows.shape, bf16),
            pltpu.VMEM((SEG, local), bf16),
            pltpu.VMEM((CMEM + MEM + SEG, 2 * local), bf16),
            pltpu.VMEM((CHUNKS, block, width), f32),
            pltpu.VMEM((MEM + SEG, HD), jnp.int32),
            pltpu.VMEM((local // HD, HD, CMEM + MEM + SEG), bf16),
            pltpu.VMEM((CMEM + MEM + SEG, 2 * local), f32),
        ]
        + line_scratch(CHUNKS, n, block, width)
        + line_scratch(CHUNKS, n, block, width)
        + line_scratch(1, n, fresh_block(n), width)
        + grid_scratch(groups, tile_count, size, 5 if last else 4)
        + [dma((CHUNKS,))] * 2
        + [pltpu.VMEM((2, size, size), f32), pltpu.VMEM((n, 8, size), f32), dma((2, n)), dma((n,))]
        + (
            [
                pltpu.VMEM((n, fresh_block(n), local), bf16),
                dma((9,)),
                dma((CHUNKS,)),
                dma((2,)),
            ]
            if last
            else []
        ),
        compiler_params=pltpu.CompilerParams(
            collective_id=collective, has_side_effects=True, vmem_limit_bytes=65000 * 1024
        ),
    )(grad.reshape(rows.shape), x_rows.reshape(rows.shape), residual, hidden, fresh,
      wq, wkv, wo, wup, wdown, gains, q, kv, log_sum, docs, key_docs, normed, two, active,
      attended, *earlier_gains, *padded, *earlier)


def project(rows, weight):
    return jnp.dot(rows, weight, preferred_element_type=f32).astype(bf16)


def shards(
    block_input,
    doc_ids,
    memory,
    compressed,
    gain_attn,
    w_query,
    w_key,
    w_value,
    w_out,
    gain_ffn,
    w_up,
    w_down,
    w_compress,
    cotangent,
):
    section = lax.axis_index("section")
    first = section == 0
    n = lax.axis_size("tensor")
    groups = lax.axis_size("dp")
    tensor_index = lax.axis_index("tensor")
    width = block_input.shape[2]
    local = w_query.shape[2]
    gains = jnp.stack([gain_attn[0], gain_ffn[0]])

    history = doc_ids[0]
    memory_docs = lax.dynamic_slice_in_dim(history, section * SEG, MEM, 0)
    token_docs = lax.dynamic_slice_in_dim(history, MEM + section * SEG, SEG, 0)
    docs = token_docs[None]
    key_docs = jnp.concatenate([memory_docs, token_docs])[:, None]
    tokens = lax.dynamic_slice_in_dim(block_input[0], section * SEG, SEG, 0)
    grad_now = lax.dynamic_slice_in_dim(cotangent[0], section * SEG, SEG, 0)

    fresh_count = n * fresh_block(n)
    lead = OLD_ROWS - FRESH_START
    trail = fresh_count - lead - COMP_ROWS
    padded = jnp.concatenate(
        [
            jnp.zeros((RATE * lead + PAD, width), bf16),
            memory[0, 0],
            jnp.zeros((RATE * trail, width), bf16),
        ]
    ).reshape(fresh_count, RATE * width)
    fresh_piece = project(padded, w_compress[0].reshape(RATE * width, local))
    fresh_piece = fresh_piece[lead : lead + COMP_ROWS]
    kept = compressed[0, 0, COMP_ROWS + FRESH_START :]
    piece = jnp.concatenate(
        [lax.dynamic_slice_in_dim(kept, tensor_index * local, local, 1), fresh_piece]
    )
    old = compressed[0, 0, COMP_ROWS : COMP_ROWS + FRESH_START]
    m_rows = jnp.where(first, memory[0, 0], block_input[0, :SEG])

    own = (w_query[0], w_key[0], w_value[0], w_out[0], w_up[0], w_down[0])
    low, high, (middle, shipped, outputs), *layers = forward(
        1, n, groups, m_rows, tokens, gains, docs, key_docs, own, old, piece, compressed[0, 0],
        memory[0, 0],
    )
    outputs = outputs.reshape(2 * SEG, width)
    saved = [
        (tokens, m_rows, *low),
        (middle.reshape(SEG, width), shipped.reshape(SEG, width), *high),
    ]
    weight_layers = [layer[:5] for layer in layers]
    gains_by_layer = [layer[5] for layer in layers]
    c_rows = [layer[6] for layer in layers]

    handed = []
    for layer in (1, 0):
        (tokens, m_rows, normed, queries, kv, log_total, attended, residual, two, hidden,
         active) = saved[layer]
        block = fresh_block(n)
        fresh_rows = jnp.concatenate(
            [c_rows[layer][FRESH_START:], m_rows[: n * block - (CMEM - FRESH_START)]]
        ).reshape(1, n, block, width)
        result = backward_layer(
            4 + layer, n, groups, layer, grad_now, tokens, residual, hidden, fresh_rows,
            weight_layers[layer], gains_by_layer[layer], queries, kv, log_total, docs, key_docs,
            normed, two, active, attended, *handed,
        )
        dx, shipped, d_fresh, *grads = result
        grad_now = dx.reshape(SEG, width)
        handed = [grads[6:8], [padded], grads[:6] + [shipped, d_fresh]]

    grad_query, grad_key, grad_value, grad_out, grad_up, grad_down = grads[:6]
    gain_attn_grad, gain_ffn_grad, grad_compress = grads[6:]
    return (
        outputs[None, None],
        shipped.reshape(2 * SEG, width)[None, None],
        gain_attn_grad,
        grad_query[None],
        grad_key[None],
        grad_value[None],
        grad_out[None],
        gain_ffn_grad,
        grad_up[None],
        grad_down[None],
        grad_compress[None],
    )


def solution(mesh):
    return jax.shard_map(
        shards,
        mesh=mesh,
        in_specs=(
            P("dp", None, None),
            P("dp", None),
            P("section", "dp", None, None),
            P("section", "dp", None, None),
            P("section", None),
            P("section", None, "tensor"),
            P("section", None, "tensor"),
            P("section", None, "tensor"),
            P("section", "tensor", None),
            P("section", None),
            P("section", None, "tensor"),
            P("section", "tensor", None),
            P("section", None, None, "tensor"),
            P("dp", None, None),
        ),
        out_specs=(
            P("section", "dp", None, None),
            P("section", "dp", None, None),
            P("section", "dp"),
            P("section", "dp", "tensor"),
            P("section", "dp", "tensor"),
            P("section", "dp", "tensor"),
            P("section", "tensor", "dp"),
            P("section", "dp"),
            P("section", "dp", "tensor"),
            P("section", "tensor", "dp"),
            P("section", None, "dp", "tensor"),
        ),
        check_vma=False,
    )
```

```python
import functools

import jax
import jax.numpy as jnp
from jax import lax
from jax.experimental import pallas as pl
from jax.experimental.pallas import tpu as pltpu
from jax.sharding import PartitionSpec as P

HD = 128
SEG = 512
MEM = 512
CMEM = 512
RATE = 3
COMP_ROWS = 171
PAD = 1
OLD_ROWS = CMEM - COMP_ROWS
CHUNKS = 4
ROWS = SEG // CHUNKS
FRESH_START = OLD_ROWS // 16 * 16

epsilon = 1e-06
masked_value = -1000000000.0
MESH = pl.DeviceIdType.MESH
f32 = jnp.float32
bf16 = jnp.bfloat16
GELU_A = 0.7978845608028654
GELU_B = 0.044715


def inverse_rms(rows):
    return lax.rsqrt(jnp.mean(rows * rows, axis=-1, keepdims=True) + epsilon)


def rms_pull(grad, rows, gain):
    scale = inverse_rms(rows)
    scaled_grad = grad * gain
    inner = jnp.mean(scaled_grad * rows, axis=-1, keepdims=True)
    return scale * (scaled_grad - rows * (scale * scale * inner))


def gelu(x):
    return 0.5 * x * (1.0 + jnp.tanh(GELU_A * (x + GELU_B * x * x * x)))


def gelu_slope(x):
    square = x * x
    bend = jnp.tanh(GELU_A * (x + GELU_B * x * square))
    return 0.5 * (1.0 + bend) + 0.5 * x * (1.0 - bend * bend) * GELU_A * (
        1.0 + 3.0 * GELU_B * square
    )


def dot_nn(a, b):
    return lax.dot_general(a, b, (((1,), (0,)), ((), ())), preferred_element_type=f32)


def dot_nt(a, b):
    return lax.dot_general(a, b, (((1,), (1,)), ((), ())), preferred_element_type=f32)


def dot_tn(a, b):
    return lax.dot_general(a, b, (((0,), (0,)), ((), ())), preferred_element_type=f32)


def greet(n, with_peer=False, groups=0, everyone=False):
    me = lax.axis_index("tensor")
    barrier = pltpu.get_barrier_semaphore()
    for step in (-1, 1):
        other = me + step

        @pl.when((other >= 0) & (other < n))
        def _():
            pl.semaphore_signal(barrier, inc=1, device_id={"tensor": other}, device_id_type=MESH)

    extra = 0
    if with_peer:
        extra += 1
        peer = 1 - lax.axis_index("section")
        pl.semaphore_signal(barrier, inc=1, device_id={"section": peer}, device_id_type=MESH)
    if groups:
        mine = lax.axis_index("dp")
        others = [mine + 1 - 2 * (mine % 2)]
        others += [(mine + 2 * step) % groups for step in range(1, groups // 2)]
        if everyone:
            others = [(mine + step) % groups for step in range(1, groups)]
        for other in others:
            pl.semaphore_signal(barrier, inc=1, device_id={"dp": other}, device_id_type=MESH)
        extra += len(others)
    pl.semaphore_wait(barrier, jnp.where((me > 0) & (me < n - 1), 2 + extra, 1 + extra))
    return me


class GridSum:
    def __init__(self, groups, home, tiles, landings, sems, parts):
        self.groups, self.home, self.tiles, self.parts = groups, home, tiles, parts
        self.from_core, self.from_row, self.from_section = landings
        self.core_sems, self.row_sems, self.section_sems = sems
        self.dp = lax.axis_index("dp")
        self.section = lax.axis_index("section")
        self.core = self.dp % 2
        self.row = self.dp // 2
        self.rows = groups // 2

    def span(self, part):
        start, stop = self.parts[part]
        return pl.ds(start, stop - start)

    def core_copy(self, part, row):
        return pltpu.make_async_remote_copy(
            src_ref=self.tiles.at[row * 2 + 1 - self.core, self.span(part)],
            dst_ref=self.from_core.at[row, self.span(part)],
            send_sem=self.core_sems.at[0, part, row],
            recv_sem=self.core_sems.at[1, part, row],
            device_id={"dp": self.dp + 1 - 2 * self.core},
            device_id_type=MESH,
        )

    def row_copy(self, part, step):
        target = (self.row + step) % self.rows
        return pltpu.make_async_remote_copy(
            src_ref=self.tiles.at[target * 2 + self.core, self.span(part)],
            dst_ref=self.from_row.at[step - 1, self.span(part)],
            send_sem=self.row_sems.at[0, part, step - 1],
            recv_sem=self.row_sems.at[1, part, step - 1],
            device_id={"dp": target * 2 + self.core},
            device_id_type=MESH,
        )

    def section_copy(self, part):
        return pltpu.make_async_remote_copy(
            src_ref=self.tiles.at[self.dp, self.span(part)],
            dst_ref=self.from_section.at[self.span(part)],
            send_sem=self.section_sems.at[0, part],
            recv_sem=self.section_sems.at[1, part],
            device_id={"section": 1 - self.section},
            device_id_type=MESH,
        )

    def add(self, place, landing, part):
        start, stop = self.parts[part]

        def body(tile, carry):
            self.tiles[place, tile] = (
                self.tiles[place, tile].astype(f32) + landing[tile].astype(f32)
            ).astype(bf16)
            return carry

        lax.fori_loop(start, stop, body, 0)

    def send_core(self, part):
        for row in range(self.rows):
            self.core_copy(part, row).start()

    def send_rows(self, part):
        for row in range(self.rows):
            self.core_copy(part, row).wait_recv()
            self.add(row * 2 + self.core, self.from_core.at[row], part)
        for step in range(1, self.rows):
            self.row_copy(part, step).start()

    def send_section(self, part):
        for step in range(1, self.rows):
            self.row_copy(part, step).wait_recv()
            self.add(self.dp, self.from_row.at[step - 1], part)

        @pl.when(self.section != self.home)
        def _():
            self.section_copy(part).start()

    def close(self, part, write):
        @pl.when(self.section == self.home)
        def _():
            self.section_copy(part).wait_recv()
            for tile in range(*self.parts[part]):
                write(
                    tile,
                    self.tiles[self.dp, tile].astype(f32) + self.from_section[tile].astype(f32),
                )

    def finish(self):
        for part in range(len(self.parts)):
            for row in range(self.rows):
                self.core_copy(part, row).wait_send()
            for step in range(1, self.rows):
                self.row_copy(part, step).wait_send()

            @pl.when(self.section != self.home)
            def _():
                self.section_copy(part).wait_send()


def grid_scratch(groups, tiles, size, parts):
    rows = groups // 2
    return [
        pltpu.VMEM((groups, tiles, size, size), bf16),
        pltpu.VMEM((rows, tiles, size, size), bf16),
        pltpu.VMEM((rows - 1, tiles, size, size), bf16),
        pltpu.VMEM((tiles, size, size), bf16),
        pltpu.SemaphoreType.DMA((2, parts, rows)),
        pltpu.SemaphoreType.DMA((2, parts, rows - 1)),
        pltpu.SemaphoreType.DMA((2, parts)),
    ]


class LineSum:
    def __init__(self, n, me, middle, part, out, held, sems):
        self.n, self.me, self.middle, self.part, self.out = n, me, middle, part, out
        self.from_left, self.from_right = held
        self.rs_send, self.rs_recv, self.ag_send, self.ag_recv = sems
        self.stages = 2 * n - 1

    def reduce_copy(self, src, landing, side, chunk, block, target):
        return pltpu.make_async_remote_copy(
            src_ref=src,
            dst_ref=landing.at[chunk, block],
            send_sem=self.rs_send.at[side, chunk, block],
            recv_sem=self.rs_recv.at[side, chunk, block],
            device_id={"tensor": target},
            device_id_type=MESH,
        )

    def gather_copy(self, side, chunk, block, target):
        return pltpu.make_async_remote_copy(
            src_ref=self.out.at[chunk, block],
            dst_ref=self.out.at[chunk, block],
            send_sem=self.ag_send.at[side, chunk, block],
            recv_sem=self.ag_recv.at[chunk, block],
            device_id={"tensor": target},
            device_id_type=MESH,
        )

    def put(self, chunk, rows):
        self.part[chunk] = rows.astype(bf16).reshape(self.part.shape[1:])

    def rows(self, chunk):
        whole = self.out[chunk]
        return whole.reshape(-1, whole.shape[-1])

    def stage(self, chunk, stage):
        n = self.n
        if stage == 0:
            self.first_sends(chunk)
        elif stage <= n - 2:
            self.hop(chunk, stage)
        elif stage == n - 1:
            self.own_rows(chunk)
        else:
            self.forward(chunk, stage - n + 1)

    def first_sends(self, chunk):
        n, part = self.n, self.part

        @pl.when(self.me == 0)
        def _():
            for block in range(n - 1, 0, -1):
                self.reduce_copy(
                    part.at[chunk, block], self.from_left, 0, chunk, block, 1
                ).start()

        @pl.when(self.me == n - 1)
        def _():
            for block in range(n - 1):
                self.reduce_copy(
                    part.at[chunk, block], self.from_right, 1, chunk, block, n - 2
                ).start()

    def hop(self, chunk, step):
        n, part = self.n, self.part

        @pl.when(self.me == step)
        def _():
            landing = self.from_left
            for block in range(n - 1, step, -1):
                self.reduce_copy(
                    part.at[chunk, block], landing, 0, chunk, block, step
                ).wait_recv()
                part[chunk, block] = (
                    landing[chunk, block].astype(f32) + part[chunk, block].astype(f32)
                ).astype(bf16)
                self.reduce_copy(
                    part.at[chunk, block], landing, 0, chunk, block, step + 1
                ).start()

        @pl.when(self.me == n - 1 - step)
        def _():
            landing = self.from_right
            mine = n - 1 - step
            for block in range(mine):
                self.reduce_copy(
                    part.at[chunk, block], landing, 1, chunk, block, mine
                ).wait_recv()
                part[chunk, block] = (
                    landing[chunk, block].astype(f32) + part[chunk, block].astype(f32)
                ).astype(bf16)
                self.reduce_copy(
                    part.at[chunk, block], landing, 1, chunk, block, mine - 1
                ).start()

    def own_rows(self, chunk):
        n, me, part = self.n, self.me, self.part

        @pl.when(me > 0)
        def _():
            self.reduce_copy(part.at[chunk, me], self.from_left, 0, chunk, me, me).wait_recv()

        @pl.when(me < n - 1)
        def _():
            self.reduce_copy(part.at[chunk, me], self.from_right, 1, chunk, me, me).wait_recv()

        total = part[chunk, me].astype(f32)
        total = total + jnp.where(me > 0, self.from_left[chunk, me].astype(f32), 0.0)
        total = total + jnp.where(me < n - 1, self.from_right[chunk, me].astype(f32), 0.0)
        self.out[chunk, me] = self.middle(chunk, me, total).astype(bf16)

        @pl.when(me < n - 1)
        def _():
            self.gather_copy(0, chunk, me, me + 1).start()

        @pl.when(me > 0)
        def _():
            self.gather_copy(1, chunk, me, me - 1).start()

    def forward(self, chunk, step):
        n, me = self.n, self.me
        left_block = me - step

        @pl.when(left_block >= 0)
        def _():
            self.gather_copy(0, chunk, left_block, me).wait_recv()

            @pl.when(me < n - 1)
            def _():
                self.gather_copy(0, chunk, left_block, me + 1).start()

        right_block = me + step

        @pl.when(right_block < n)
        def _():
            self.gather_copy(1, chunk, right_block, me).wait_recv()

            @pl.when(me > 0)
            def _():
                self.gather_copy(1, chunk, right_block, me - 1).start()

    def finish(self):
        n, me, part = self.n, self.me, self.part
        for chunk in range(part.shape[0]):
            for block in range(n):

                @pl.when((me < n - 1) & (block > me))
                def _():
                    self.reduce_copy(
                        part.at[chunk, block], self.from_left, 0, chunk, block, me
                    ).wait_send()

                @pl.when((me > 0) & (block < me))
                def _():
                    self.reduce_copy(
                        part.at[chunk, block], self.from_right, 1, chunk, block, me
                    ).wait_send()

                @pl.when((me < n - 1) & (block <= me))
                def _():
                    self.gather_copy(0, chunk, block, me).wait_send()

                @pl.when((me > 0) & (block >= me))
                def _():
                    self.gather_copy(1, chunk, block, me).wait_send()


def line_scratch(chunks, n, block, width):
    return [pltpu.VMEM((chunks, n, block, width), bf16)] * 3 + [
        pltpu.SemaphoreType.DMA((2, chunks, n)),
        pltpu.SemaphoreType.DMA((2, chunks, n)),
        pltpu.SemaphoreType.DMA((2, chunks, n)),
        pltpu.SemaphoreType.DMA((chunks, n)),
    ]


def make_line(n, me, middle, out, scratch):
    return LineSum(n, me, middle, scratch[0], out, scratch[1:3], scratch[3:7])


def run_two(order, first, second, produce, between, finished, extra):
    lag = first.stages - 1
    last = len(order) - 1
    for slot in range(2 * lag + last + 1):
        if slot <= last:
            produce(order[slot])
        extra(slot)
        for place, chunk in enumerate(order):
            stage = slot - lag - place
            if 1 <= stage <= lag:
                second.stage(chunk, stage)
            if stage == lag:
                finished(chunk)
        for place, chunk in enumerate(order):
            stage = slot - place
            if 0 <= stage <= lag:
                first.stage(chunk, stage)
        if 0 <= slot - lag <= last:
            chunk = order[slot - lag]
            between(chunk)
            second.stage(chunk, 0)


def run_chain(order, sums, works, finished, extra):
    lag = sums[0].stages - 1
    last = len(order) - 1
    for slot in range(len(sums) * lag + last + 1):
        if slot <= last:
            works[0](order[slot])
        extra(slot)
        for level in range(len(sums) - 1, -1, -1):
            for place, chunk in enumerate(order):
                stage = slot - level * lag - place
                if min(level, 1) <= stage <= lag:
                    sums[level].stage(chunk, stage)
                if stage == lag:
                    finished(level, chunk)
        for level in range(len(sums) - 1, 0, -1):
            if 0 <= slot - level * lag <= last:
                chunk = order[slot - level * lag]
                works[level](chunk)
                sums[level].stage(chunk, 0)


class WeightSwap:
    def __init__(self, groups, own, layers, sems):
        self.groups, self.own, self.layers = groups, own, layers
        self.x_sems, self.row_sems, self.core_sems, self.local_sems = sems
        self.dp = lax.axis_index("dp")
        self.section = lax.axis_index("section")
        self.core = self.dp % 2
        self.row = self.dp // 2
        self.rows = groups // 2

    def share(self, array, piece):
        rows = self.own[array][0].shape[0] // self.groups
        return pl.ds(pl.multiple_of(piece * rows, rows), rows)

    def block(self, layer, array, piece):
        ref, lanes = self.layers[layer][array]
        return ref.at[self.share(array, piece), lanes]

    def section_copy(self, layer, array):
        ref, lanes = self.own[array]
        return pltpu.make_async_remote_copy(
            src_ref=ref.at[self.share(array, self.dp), lanes],
            dst_ref=self.block(layer, array, self.dp),
            send_sem=self.x_sems.at[0, array],
            recv_sem=self.x_sems.at[1, array],
            device_id={"section": 1 - self.section},
            device_id_type=MESH,
        )

    def row_copy(self, layer, array, step, source, target):
        piece = source * 2 + self.core
        return pltpu.make_async_remote_copy(
            src_ref=self.block(layer, array, piece),
            dst_ref=self.block(layer, array, piece),
            send_sem=self.row_sems.at[0, array, step - 1],
            recv_sem=self.row_sems.at[1, array, step - 1],
            device_id={"dp": target * 2 + self.core},
            device_id_type=MESH,
        )

    def core_copy(self, layer, array, step, core):
        piece = (self.row - step) % self.rows * 2 + core
        return pltpu.make_async_remote_copy(
            src_ref=self.block(layer, array, piece),
            dst_ref=self.block(layer, array, piece),
            send_sem=self.core_sems.at[0, array, step],
            recv_sem=self.core_sems.at[1, array, step],
            device_id={"dp": self.dp + 1 - 2 * self.core},
            device_id_type=MESH,
        )

    def local_copy(self, layer, array):
        ref, lanes = self.own[array]
        to, to_lanes = self.layers[layer][array]
        return pltpu.make_async_copy(
            ref.at[:, lanes], to.at[:, to_lanes], self.local_sems.at[array]
        )

    def take(self, layer, arrays):
        for array in arrays:
            self.section_copy(layer, array).wait_recv()
            for step in range(1, self.rows):
                target = (self.row + step) % self.rows
                self.row_copy(layer, array, step, self.row, target).start()
            self.core_copy(layer, array, 0, self.core).start()

    def spread(self, layer, arrays):
        for array in arrays:
            for step in range(1, self.rows):
                source = (self.row - step) % self.rows
                self.row_copy(layer, array, step, source, self.row).wait_recv()
                self.core_copy(layer, array, step, self.core).start()

    def settle(self, layer, arrays):
        for array in arrays:
            for step in range(self.rows):
                self.core_copy(layer, array, step, 1 - self.core).wait_recv()

    def on_arrival(self, work, arrays):
        for layer in range(2):

            @pl.when(self.section != layer)
            def _():
                work(layer, arrays)

    def finish(self):
        for layer in range(2):
            for array in range(len(self.own)):

                @pl.when(self.section == layer)
                def _():
                    self.section_copy(layer, array).wait_send()

                @pl.when(self.section != layer)
                def _():
                    for step in range(1, self.rows):
                        target = (self.row + step) % self.rows
                        self.row_copy(layer, array, step, self.row, target).wait_send()
                    for step in range(self.rows):
                        self.core_copy(layer, array, step, self.core).wait_send()


class LineGather:
    def __init__(self, n, me, place, sems):
        self.n, self.me, self.place = n, me, place
        self.send, self.recv = sems

    def copy(self, side, block, target):
        return pltpu.make_async_remote_copy(
            src_ref=self.place(block),
            dst_ref=self.place(block),
            send_sem=self.send.at[side, block],
            recv_sem=self.recv.at[block],
            device_id={"tensor": target},
            device_id_type=MESH,
        )

    def start(self):
        n, me = self.n, self.me

        @pl.when(me < n - 1)
        def _():
            self.copy(0, me, me + 1).start()

        @pl.when(me > 0)
        def _():
            self.copy(1, me, me - 1).start()

    def forward(self, step):
        n, me = self.n, self.me
        left_block = me - step

        @pl.when(left_block >= 0)
        def _():
            self.copy(0, left_block, me).wait_recv()

            @pl.when(me < n - 1)
            def _():
                self.copy(0, left_block, me + 1).start()

        right_block = me + step

        @pl.when(right_block < n)
        def _():
            self.copy(1, right_block, me).wait_recv()

            @pl.when(me > 0)
            def _():
                self.copy(1, right_block, me - 1).start()

    def finish(self):
        n, me = self.n, self.me
        for block in range(n):

            @pl.when((me < n - 1) & (block <= me))
            def _():
                self.copy(0, block, me).wait_send()

            @pl.when((me > 0) & (block >= me))
            def _():
                self.copy(1, block, me).wait_send()


def columns_of(ref, lanes):
    def place(block):
        at = pl.ds(pl.multiple_of(block * lanes, lanes), lanes)
        return ref.at[FRESH_START:CMEM, at]

    return place


def score_columns(head, chunk, q_ref, kv_ref, docs, keys_docs):
    lanes = slice(head * HD, (head + 1) * HD)
    width = CMEM + MEM + (chunk + 1) * ROWS
    query = q_ref[chunk * ROWS : (chunk + 1) * ROWS, lanes]
    scores = dot_nt(kv_ref[:width, lanes], query) * HD ** (-0.5)
    own = docs[:, chunk * ROWS : (chunk + 1) * ROWS]
    same = keys_docs[: MEM + chunk * ROWS, :] == own
    tail_docs = keys_docs[MEM + chunk * ROWS : MEM + (chunk + 1) * ROWS, :]
    key_place = lax.broadcasted_iota(jnp.int32, (ROWS, ROWS), 0)
    query_place = lax.broadcasted_iota(jnp.int32, (ROWS, ROWS), 1)
    tail_same = (tail_docs == own) & (key_place <= query_place)
    middle_end = CMEM + MEM + chunk * ROWS
    return jnp.concatenate(
        [
            scores[:CMEM],
            jnp.where(same, scores[CMEM:middle_end], masked_value),
            jnp.where(tail_same, scores[middle_end:], masked_value),
        ],
        axis=0,
    )


class ForwardLayer:
    def __init__(self, n, me, weights, x_ref, saved, out, docs, keys_docs, scratch):
        self.wq, self.wkv, self.wo, self.wup, self.wdown, self.gains, self.c_ref = weights
        (self.normed, self.q_ref, self.kv_ref, self.log_sum, self.attended, self.residual,
         self.two, self.hidden, self.active) = saved
        self.x_ref, self.docs, self.keys_docs = x_ref, docs, keys_docs
        self.values_t, first_scratch, second_scratch = scratch[0], scratch[1:8], scratch[8:15]
        self.local = self.wq.shape[1]
        self.heads = self.local // HD
        self.first = make_line(n, me, self.attention_middle, self.two, first_scratch)
        self.second = make_line(n, me, self.output_middle, out, second_scratch)

    def project(self, wide, at):
        block = (wide * inverse_rms(wide) * self.gains[0:1, :]).astype(bf16)
        self.normed[at, :] = block
        self.kv_ref[at, :] = dot_nn(block, self.wkv[...]).astype(bf16)
        return block

    def flip_values(self, rows):
        for head in range(self.heads):
            lanes = slice(self.local + head * HD, self.local + (head + 1) * HD)
            self.values_t[head, :, rows] = self.kv_ref[rows, lanes].astype(f32).T.astype(bf16)

    def project_block(self, source, place):
        def body(step, carry):
            rows = pl.ds(pl.multiple_of(step * 256, 256), 256)
            at = pl.ds(pl.multiple_of(place * SEG + step * 256, 256), 256)
            self.project(source[rows, :].astype(f32), at)
            return carry

        lax.fori_loop(0, SEG // 256, body, 0)
        self.flip_values(slice(place * SEG, (place + 1) * SEG))

    def attention_middle(self, chunk, me, total):
        rows = self.x_ref[chunk, me].astype(f32) + total
        self.residual[chunk] = rows
        return rows * inverse_rms(rows) * self.gains[1:2, :]

    def output_middle(self, chunk, me, total):
        return self.residual[chunk] + total

    def attend(self, chunk):
        rows = slice(chunk * ROWS, (chunk + 1) * ROWS)
        at = slice(CMEM + MEM + chunk * ROWS, CMEM + MEM + (chunk + 1) * ROWS)
        source = self.x_ref[chunk]
        block = self.project(source.reshape(ROWS, source.shape[-1]).astype(f32), at)
        self.q_ref[rows, :] = dot_nn(block, self.wq[...]).astype(bf16)
        self.flip_values(at)
        for head in range(self.heads):
            lanes = slice(head * HD, (head + 1) * HD)
            scores = score_columns(
                head, chunk, self.q_ref, self.kv_ref, self.docs, self.keys_docs
            )
            top = jnp.max(scores, axis=0, keepdims=True)
            powers = jnp.exp(scores - top)
            total = jnp.sum(powers, axis=0, keepdims=True)
            self.log_sum[head : head + 1, rows] = top + jnp.log(total)
            weights = (powers * (1.0 / total)).astype(bf16)
            mixed = dot_nn(self.values_t[head, :, : weights.shape[0]], weights)
            self.attended[rows, lanes] = mixed.T.astype(bf16)
        self.first.put(chunk, dot_nn(self.attended[rows, :], self.wo[...]))

    def feed(self, chunk):
        rows = slice(chunk * ROWS, (chunk + 1) * ROWS)
        before = dot_nn(self.first.rows(chunk), self.wup[...])
        self.hidden[rows, :] = before
        after = gelu(before).astype(bf16)
        self.active[rows, :] = after
        self.second.put(chunk, dot_nn(after, self.wdown[...]))


def forward_kernel(n, groups, *refs):
    m_ref, x_ref, own_gains, docs, key_docs = refs[:5]
    own_refs, (old, piece, compressed, memory) = refs[5:11], refs[11:15]
    saved = [refs[15:24], refs[24:33]]
    middle_rows, shipped, outputs = refs[33:36]
    layer_refs = [refs[36:43], refs[43:50]]
    keys_docs, last_rows = refs[50:52]
    scratch = [refs[52:67], refs[67:82]]
    (ship_send, ship_recv, final_send, final_recv, keep, *swap_sems, item_sems, local_sems) = (
        refs[82:93]
    )
    gather_sems = refs[93:97]
    me = greet(n, True, groups)
    section = lax.axis_index("section")
    wq, wup = layer_refs[0][0], layer_refs[0][3]
    local, inner, width = wq.shape[1], wup.shape[1], wup.shape[0]
    whole = slice(None)
    front, back = slice(0, inner // 2), slice(inner // 2, inner)
    lead, trail = slice(0, width // 2), slice(width // 2, width)
    q_own, k_own, v_own, o_own, up_own, down_own = own_refs
    own = [(q_own, whole), (k_own, whole), (v_own, whole), (o_own, whole),
           (up_own, front), (up_own, back), (down_own, lead), (down_own, trail)]
    places = [
        [(w[0], whole), (w[1], slice(0, local)), (w[1], slice(local, 2 * local)),
         (w[2], whole), (w[3], front), (w[3], back), (w[4], lead), (w[4], trail)]
        for w in layer_refs
    ]
    swap = WeightSwap(groups, own, places, swap_sems)
    gathers = [
        LineGather(n, me, columns_of(layer_refs[layer][6], local),
                   gather_sems[2 * layer : 2 * layer + 2])
        for layer in range(2)
    ]
    items = [
        [(own_gains, layer_refs[0][5]), (piece, gathers[0].place(me)),
         (old, layer_refs[0][6].at[:FRESH_START, :])],
        [(own_gains, layer_refs[1][5]), (compressed, layer_refs[1][6]), (memory, shipped)],
    ]

    def peer_copy(src, dst, send, recv):
        return pltpu.make_async_remote_copy(
            src_ref=src,
            dst_ref=dst,
            send_sem=send,
            recv_sem=recv,
            device_id={"section": 1 - section},
            device_id_type=MESH,
        )

    def item_copy(layer, index):
        src, dst = items[layer][index]
        return peer_copy(src, dst, item_sems.at[0, index], item_sems.at[1, index])

    local_rows = [
        pltpu.make_async_copy(compressed, layer_refs[0][6], local_sems.at[0]),
        pltpu.make_async_copy(old, layer_refs[1][6].at[:FRESH_START, :], local_sems.at[0]),
        pltpu.make_async_copy(piece, gathers[1].place(me), local_sems.at[1]),
    ]
    keys_docs[...] = jnp.broadcast_to(key_docs[...], keys_docs.shape)
    layers = [
        ForwardLayer(n, me, layer_refs[0], x_ref, saved[0], middle_rows, docs, keys_docs,
                     scratch[0]),
        ForwardLayer(n, me, layer_refs[1], middle_rows, saved[1], last_rows, docs, keys_docs,
                     scratch[1]),
    ]

    @pl.when(section == 0)
    def _():
        item_copy(0, 0).start()
        item_copy(0, 1).start()
        for array in range(3):
            swap.section_copy(0, array).start()
        item_copy(0, 2).start()
        for array in range(3, 8):
            swap.section_copy(0, array).start()
        for array in range(3):
            swap.local_copy(0, array).start()
        local_rows[0].start()
        for array in range(3, 8):
            swap.local_copy(0, array).start()
        layer_refs[0][5][...] = own_gains[...]
        local_rows[0].wait()
        for array in range(8):
            swap.local_copy(0, array).wait()

    @pl.when(section == 1)
    def _():
        item_copy(1, 0).start()
        for array in range(3):
            swap.section_copy(1, array).start()
        item_copy(1, 1).start()
        item_copy(1, 2).start()
        for array in range(3, 8):
            swap.section_copy(1, array).start()
        local_rows[1].start()
        local_rows[2].start()
        for array in range(8):
            swap.local_copy(1, array).start()
        layer_refs[1][5][...] = own_gains[...]
        item_copy(0, 0).wait_recv()
        item_copy(0, 1).wait_recv()
        gathers[0].start()
        swap.take(0, range(3))
        gathers[0].forward(1)
        swap.spread(0, range(3))
        for step in range(2, n):
            gathers[0].forward(step)
        swap.settle(0, range(3))

    layers[0].project_block(m_ref, 1)

    @pl.when(section == 1)
    def _():
        item_copy(0, 2).wait_recv()

    layers[0].project_block(layer_refs[0][6], 0)

    @pl.when(section == 1)
    def _():
        swap.take(0, [3])
        swap.spread(0, [3])
        swap.settle(0, [3])

    lag = 2 * n - 2
    plans = [
        {
            1: [(swap.take, range(3))],
            2: [(swap.spread, range(3))],
            3: [(swap.settle, range(3))],
            10: [(swap.take, [3])],
            11: [(swap.spread, [3])],
            12: [(swap.settle, [3])],
            13: [(swap.take, [4])],
            14: [(swap.spread, [4]), (swap.take, [5])],
            15: [(swap.spread, [5]), (swap.take, [6])],
            16: [(swap.spread, [6]), (swap.take, [7])],
            17: [(swap.spread, [7]), (swap.settle, [4, 5])],
            18: [(swap.settle, [6, 7])],
        },
        {
            2: [(swap.take, [4])],
            3: [(swap.take, [5]), (swap.spread, [4])],
            4: [(swap.spread, [5]), (swap.take, [6])],
            5: [(swap.take, [7]), (swap.spread, [6]), (swap.settle, [4, 5])],
            6: [(swap.spread, [7]), (swap.settle, [6, 7])],
        },
    ]

    def ship_copy(chunk):
        return peer_copy(
            middle_rows.at[chunk], shipped.at[chunk], ship_send.at[chunk], ship_recv.at[chunk]
        )

    def final_copy(layer, chunk):
        rows = (middle_rows, last_rows)[layer]
        return peer_copy(
            rows.at[chunk], outputs.at[1 - layer, chunk], final_send.at[chunk],
            final_recv.at[chunk],
        )

    def keep_copy(layer, chunk):
        rows = (middle_rows, last_rows)[layer]
        return pltpu.make_async_copy(rows.at[chunk], outputs.at[layer, chunk], keep.at[chunk])

    def finished(level, chunk):
        if level == 1:

            @pl.when(section == 0)
            def _():
                ship_copy(chunk).start()
                keep_copy(0, chunk).start()

            @pl.when(section == 1)
            def _():
                final_copy(0, chunk).start()

        if level == 3:

            @pl.when(section == 0)
            def _():
                final_copy(1, chunk).start()

            @pl.when(section == 1)
            def _():
                keep_copy(1, chunk).start()

    def extra(slot):
        for place in range(2):
            if slot in plans[place]:

                @pl.when(section == place)
                def _():
                    for work, arrays in plans[place][slot]:
                        work(1 - place, arrays)

        if slot < n:

            @pl.when(section == 1)
            def _():
                if slot == 0:
                    local_rows[2].wait()
                    gathers[1].start()
                else:
                    gathers[1].forward(slot)

        if slot == lag + 2:

            @pl.when(section == 0)
            def _():
                item_copy(1, 0).wait_recv()
                item_copy(1, 1).wait_recv()

            @pl.when(section == 1)
            def _():
                local_rows[1].wait()
                for array in range(8):
                    swap.local_copy(1, array).wait()

            layers[1].project_block(layer_refs[1][6], 0)
        if slot == 2 * lag - 1:

            @pl.when(section == 0)
            def _():
                item_copy(1, 2).wait_recv()

            @pl.when(section == 1)
            def _():
                for chunk in range(CHUNKS):
                    ship_copy(chunk).wait_recv()

            layers[1].project_block(shipped.reshape(MEM, width), 1)

    sums = [layers[0].first, layers[0].second, layers[1].first, layers[1].second]
    works = [layers[0].attend, layers[0].feed, layers[1].attend, layers[1].feed]
    run_chain(list(range(CHUNKS)), sums, works, finished, extra)
    for line in sums:
        line.finish()
    swap.finish()

    @pl.when(section == 0)
    def _():
        for chunk in range(CHUNKS):
            ship_copy(chunk).wait_send()
            keep_copy(0, chunk).wait()
            final_copy(1, chunk).wait_send()
            final_copy(0, chunk).wait_recv()
        for index in range(3):
            item_copy(0, index).wait_send()

    @pl.when(section == 1)
    def _():
        for chunk in range(CHUNKS):
            keep_copy(1, chunk).wait()
            final_copy(0, chunk).wait_send()
            final_copy(1, chunk).wait_recv()
        for index in range(3):
            item_copy(1, index).wait_send()
        for gather in gathers:
            gather.finish()


def vmem_specs(count):
    return [pl.BlockSpec(memory_space=pltpu.VMEM)] * count


def forward(collective, n, groups, m_rows, x_rows, gains, docs, key_docs, own, old, piece,
            compressed, memory):
    width, local, inner = x_rows.shape[1], own[0].shape[1], own[4].shape[1]
    block = ROWS // n
    shape = jax.ShapeDtypeStruct
    rows = shape((CHUNKS, n, block, width), bf16)
    saved = [
        shape((CMEM + MEM + SEG, width), bf16),
        shape((SEG, local), bf16),
        shape((CMEM + MEM + SEG, 2 * local), bf16),
        shape((8, SEG), f32),
        shape((SEG, local), bf16),
        shape((CHUNKS, block, width), f32),
        rows,
        shape((SEG, inner), f32),
        shape((SEG, inner), bf16),
    ]
    layer = [
        shape((width, local), bf16),
        shape((width, 2 * local), bf16),
        shape((local, width), bf16),
        shape((width, inner), bf16),
        shape((inner, width), bf16),
        shape(gains.shape, f32),
        shape((CMEM, width), bf16),
    ]
    outs = saved + saved + [rows, rows, shape((2,) + rows.shape, bf16)] + layer + layer
    arrays, rows_y = 8, groups // 2
    dma = pltpu.SemaphoreType.DMA
    layer_scratch = (
        [pltpu.VMEM((local // HD, HD, CMEM + MEM + SEG), bf16)]
        + line_scratch(CHUNKS, n, block, width)
        + line_scratch(CHUNKS, n, block, width)
    )
    scratch = [
        pltpu.VMEM((MEM + SEG, HD), jnp.int32),
        pltpu.VMEM(rows.shape, bf16),
        *layer_scratch,
        *layer_scratch,
        dma((CHUNKS,)),
        dma((CHUNKS,)),
        dma((CHUNKS,)),
        dma((CHUNKS,)),
        dma((CHUNKS,)),
        dma((2, arrays)),
        dma((2, arrays, rows_y - 1)),
        dma((2, arrays, rows_y)),
        dma((arrays,)),
        dma((2, 3)),
        dma((2,)),
        dma((2, n)),
        dma((n,)),
        dma((2, n)),
        dma((n,)),
    ]
    any_space = pl.BlockSpec(memory_space=pl.ANY)
    result = pl.pallas_call(
        functools.partial(forward_kernel, n, groups),
        name="forward",
        out_shape=outs,
        in_specs=vmem_specs(5) + [any_space] * 10,
        out_specs=vmem_specs(20) + [any_space] + vmem_specs(14),
        scratch_shapes=scratch,
        compiler_params=pltpu.CompilerParams(
            collective_id=collective, has_side_effects=True, vmem_limit_bytes=65000 * 1024
        ),
    )(m_rows, x_rows.reshape(rows.shape), gains, docs, key_docs, *own, old, piece, compressed,
      memory.reshape(rows.shape))
    return result[:9], result[9:18], result[18:21], result[21:28], result[28:35]


def backward_kernel(n, groups, home, *refs):
    (g_ref, x_ref, residual, hidden, fresh, wq, wkv, wo, wup, wdown, gains, q_ref, kv_ref,
     log_sum, docs, key_docs, normed, two, active, attended) = refs[:20]
    last = home == 0
    rest = refs[20:]
    if last:
        earlier_gains, padded, earlier, rest = rest[:2], rest[2], rest[3:11], rest[11:]
    dx_ref, shipped, d_fresh = rest[:3]
    results, gain_results, rest = rest[3:9], rest[9:11], rest[11:]
    grad_query, grad_key, grad_value, grad_out, grad_up, grad_down = results
    if last:
        grad_compress, rest = rest[0], rest[1:]
    d_hidden, d_branch, dq_ref, dkv_ref, d_residual, keys_docs, keys_t, sums = rest[:8]
    rest = rest[8:]
    first_scratch, second_scratch, fresh_scratch = rest[:7], rest[7:14], rest[14:21]
    tiles, grid_rest = rest[21], rest[22:28]
    ship_send, ship_recv = rest[28:30]
    gain_sums, gain_blocks, gain_send, gain_recv = rest[30:34]
    if last:
        fresh_all, padded_all, keep, keep_rows, fresh_sems, pad_sems, column_sems = rest[34:41]
    me = greet(n, True, groups, last)
    section = lax.axis_index("section")
    late = section == 1
    local = wq.shape[1]
    heads = local // HD
    gain_a = gains[0:1, :]
    gain_f = gains[1:2, :]
    scale = HD ** (-0.5)

    keys_docs[...] = jnp.broadcast_to(key_docs[...], keys_docs.shape)
    for head in range(heads):
        lanes = slice(head * HD, (head + 1) * HD)
        keys_t[head] = kv_ref[:, lanes].astype(f32).T.astype(bf16)

    def branch_middle(chunk, me, total):
        rows = g_ref[chunk, me].astype(f32) + rms_pull(total, residual[chunk], gain_f)
        d_residual[chunk] = rows
        return rows

    def input_middle(chunk, me, total):
        return d_residual[chunk] + rms_pull(total, x_ref[chunk, me].astype(f32), gain_a)

    def fresh_middle(chunk, me, total):
        return rms_pull(total, fresh[chunk, me].astype(f32), gain_a)

    first = make_line(n, me, branch_middle, d_branch, first_scratch)
    second = make_line(n, me, input_middle, dx_ref, second_scratch)
    third = make_line(n, me, fresh_middle, d_fresh, fresh_scratch)

    def produce(chunk):
        rows = slice(chunk * ROWS, (chunk + 1) * ROWS)
        grad = g_ref[chunk]
        d_active = dot_nt(grad.reshape(ROWS, grad.shape[-1]), wdown[...])
        block = (gelu_slope(hidden[rows, :]) * d_active).astype(bf16)
        d_hidden[rows, :] = block
        first.put(chunk, dot_nt(block, wup[...]))

    def attend_back(chunk):
        rows = slice(chunk * ROWS, (chunk + 1) * ROWS)
        d_attended = dot_nt(first.rows(chunk), wo[...]).astype(bf16)
        fresh_sum = chunk == CHUNKS - 1
        for head in range(heads):
            lanes = slice(head * HD, (head + 1) * HD)
            value_lanes = slice(local + head * HD, local + (head + 1) * HD)
            scores = score_columns(head, chunk, q_ref, kv_ref, docs, keys_docs)
            size = scores.shape[0]
            probs = jnp.exp(scores - log_sum[head : head + 1, rows])
            d_mixed = d_attended[:, lanes]
            d_values = dot_nn(probs.astype(bf16), d_mixed)
            d_probs = dot_nt(kv_ref[:size, value_lanes], d_mixed)
            inner = jnp.sum(d_probs * probs, axis=0, keepdims=True)
            d_scores = (probs * (d_probs - inner)).astype(bf16)
            d_keys = dot_nn(d_scores, q_ref[rows, lanes])
            d_queries = dot_nn(keys_t[head, :, :size], d_scores) * scale
            dq_ref[rows, lanes] = d_queries.T.astype(bf16)
            if fresh_sum:
                sums[:size, lanes] = d_keys
                sums[:size, value_lanes] = d_values
            else:
                sums[:size, lanes] += d_keys
                sums[:size, value_lanes] += d_values
        own = slice(CMEM + MEM + chunk * ROWS, CMEM + MEM + (chunk + 1) * ROWS)
        close_rows(own)
        second.put(
            chunk, dot_nt(dq_ref[rows, :], wq[...]) + dot_nt(dkv_ref[own, :], wkv[...])
        )
        if chunk == 0:
            close_rows(slice(0, CMEM + MEM))

            @pl.when(late)
            def _():
                count = third.part.shape[1] * third.part.shape[2]
                third.put(0, dot_nt(dkv_ref[FRESH_START : FRESH_START + count, :], wkv[...]))
                third.stage(0, 0)

    def close_rows(rows):
        dkv_ref[rows, :local] = (sums[rows, :local] * scale).astype(bf16)
        dkv_ref[rows, local:] = sums[rows, local:].astype(bf16)

    size = wq.shape[0] // groups
    wide = hidden.shape[1] // size
    up_at, down_at = 4, 4 + wide
    parts = [(down_at, down_at + wide), (up_at, down_at), (0, 2), (2, 4)]
    grid = GridSum(groups, home, tiles, grid_rest[:3], grid_rest[3:6], parts)
    half = groups // 2
    g_rows = g_ref.reshape(SEG, g_ref.shape[-1])
    two_rows = two.reshape(SEG, two.shape[-1])
    branch_rows = d_branch.reshape(SEG, d_branch.shape[-1])

    def each_block(start, stop, work):
        def body(block, carry):
            work(block, pl.ds(pl.multiple_of(block * size, size), size))
            return carry

        lax.fori_loop(start, stop, body, 0)

    def put_tiles(block, at, value):
        for tile in range(value.shape[1] // size):
            tiles[block, at + tile] = value[:, tile * size : (tile + 1) * size].astype(bf16)

    def down_block(block, lanes):
        put_tiles(block, down_at, dot_tn(g_rows[:, lanes], active[...]))

    def up_block(block, lanes):
        put_tiles(block, up_at, dot_tn(two_rows[:, lanes], d_hidden[...]))

    def small_block(block, lanes):
        put_tiles(block, 0, dot_tn(normed[CMEM + MEM :, lanes], dq_ref[...]))
        put_tiles(block, 1, dot_tn(branch_rows[:, lanes], attended[...]))

    def kv_block(block, lanes):
        put_tiles(block, 2, dot_tn(normed[:, lanes], dkv_ref[...]))

    share = pl.ds(pl.multiple_of(grid.dp * size, size), size)
    gain_sums[...] = jnp.zeros(gain_sums.shape, f32)

    def write(tile, value):
        if tile >= down_at:
            grad_down[(tile - down_at) * size : (tile - down_at + 1) * size, :] = value.T
        elif tile >= up_at:
            lanes = slice((tile - up_at) * size, (tile - up_at + 1) * size)
            grad_up[:, lanes] = value
            gain_sums[1] += wup[share, lanes].astype(f32) * value
        elif tile == 1:
            grad_out[...] = value.T
        elif tile == 0:
            grad_query[...] = value
            gain_sums[0] += wq[share, :].astype(f32) * value
        else:
            (grad_key, grad_value)[tile - 2][...] = value
            lanes = slice((tile - 2) * local, (tile - 1) * local)
            gain_sums[0] += wkv[share, lanes].astype(f32) * value

    gain_gather = LineGather(
        n, me, lambda block: gain_blocks.at[block], (gain_send, gain_recv)
    )

    first_slot = 2 * n - 2
    plan = {
        1: [lambda: each_block(0, half, down_block)],
        2: [lambda: each_block(half, groups, down_block), lambda: grid.send_core(0)],
        4: [lambda: each_block(0, half, up_block), lambda: grid.send_rows(0)],
        5: [lambda: each_block(half, groups, up_block), lambda: grid.send_core(1)],
        first_slot: [lambda: grid.send_rows(1)],
        first_slot + 1: [lambda: grid.send_section(0)],
        first_slot + 2: [lambda: grid.send_section(1)],
        first_slot + 3: [lambda: grid.close(0, write)],
        first_slot + 4: [lambda: each_block(0, groups, kv_block), lambda: grid.send_core(3)],
        first_slot + 5: [
            lambda: each_block(0, groups, small_block), lambda: grid.send_core(2),
            lambda: grid.send_rows(3),
        ],
        first_slot + 6: [lambda: grid.send_rows(2), lambda: grid.close(1, write)],
        first_slot + 7: [lambda: grid.send_section(3)],
        first_slot + 8: [lambda: grid.send_section(2)],
        first_slot + 9: [lambda: grid.close(3, write)],
    }

    def ship_copy(chunk):
        return pltpu.make_async_remote_copy(
            src_ref=dx_ref.at[chunk],
            dst_ref=shipped.at[1, chunk] if last else shipped.at[chunk],
            send_sem=ship_send.at[chunk],
            recv_sem=ship_recv.at[chunk],
            device_id={"section": 1 - section},
            device_id_type=MESH,
        )

    def finished(chunk):
        @pl.when(section != home)
        def _():
            ship_copy(chunk).start()

        if last:

            @pl.when(section == home)
            def _():
                keep_row(chunk).start()

    if last:
        earlier_shipped, earlier_fresh = earlier[6:]
        columns = pl.ds(pl.multiple_of(me * local, local), local)

        def keep_row(chunk):
            return pltpu.make_async_copy(
                dx_ref.at[chunk], shipped.at[0, chunk], keep_rows.at[chunk]
            )

        kept = [
            pltpu.make_async_copy(src, dst, keep.at[index])
            for index, (src, dst) in enumerate(zip(earlier[:6], results))
        ] + [
            pltpu.make_async_copy(earlier_shipped, shipped.at[0], keep.at[6]),
            pltpu.make_async_copy(g_ref, shipped.at[1], keep.at[7]),
            pltpu.make_async_copy(
                earlier_fresh.at[0, :, :, columns], fresh_all.at[grid.dp], keep.at[8]
            ),
        ]
        fresh_copy = pltpu.make_async_remote_copy(
            src_ref=d_fresh.at[0, :, :, columns],
            dst_ref=fresh_all.at[grid.dp],
            send_sem=fresh_sems.at[0],
            recv_sem=fresh_sems.at[1],
            device_id={"section": 1 - section},
            device_id_type=MESH,
        )

        @pl.when(late)
        def _():
            for copy in kept:
                copy.start()
            for index in range(2):
                gain_results[index][...] = earlier_gains[index][...]

        def pad_source(place, target):
            return padded.at[
                :, pl.ds(pl.multiple_of(place * wo.shape[1] + target * size, size), size)
            ]

        def pad_place(place, source):
            return padded_all.at[source, :, place * size : (place + 1) * size]

        def pad_copy(step, place, source):
            target = (grid.dp + step) % groups
            return pltpu.make_async_remote_copy(
                src_ref=pad_source(place, target),
                dst_ref=pad_place(place, source),
                send_sem=pad_sems.at[0, step - 1, place],
                recv_sem=pad_sems.at[1, step - 1, place],
                device_id={"dp": target},
                device_id_type=MESH,
            )

        def column_copy(step, source):
            return pltpu.make_async_remote_copy(
                src_ref=fresh_all.at[source],
                dst_ref=fresh_all.at[source],
                send_sem=column_sems.at[0, step - 1],
                recv_sem=column_sems.at[1, step - 1],
                device_id={"dp": (grid.dp + step) % groups},
                device_id_type=MESH,
            )

        pad_own = [
            pltpu.make_async_copy(
                pad_source(place, grid.dp), pad_place(place, grid.dp), keep.at[9 + place]
            )
            for place in range(RATE)
        ]
        for place in range(RATE):
            pad_own[place].start()
            for step in range(1, groups):
                pad_copy(step, place, grid.dp).start()

    def extra(slot):
        for action in plan.get(slot, ()):
            action()
        step = slot - (first_slot + CHUNKS - 1)
        if 0 < step < third.stages:

            @pl.when(late)
            def _():
                third.stage(0, step)

    run_two(
        list(range(CHUNKS - 1, -1, -1)), first, second, produce, attend_back, finished, extra,
    )
    if last:

        @pl.when(late)
        def _():
            fresh_copy.start()
            for copy in kept:
                copy.wait()

        @pl.when(section == home)
        def _():
            fresh_copy.wait_recv()

        for step in range(1, groups):
            column_copy(step, grid.dp).start()
    grid.close(2, write)

    @pl.when(section == home)
    def _():
        gain_blocks[me] = jnp.zeros(gain_blocks.shape[1:], f32)
        for index in range(2):
            gain_blocks[me, index : index + 1, :] = jnp.sum(
                gain_sums[index].T, axis=0, keepdims=True
            )
        gain_gather.start()

    @pl.when(section == home)
    def _():
        for step in range(1, n):
            gain_gather.forward(step)
        total = gain_blocks[0]
        for block in range(1, n):
            total = total + gain_blocks[block]
        for index in range(2):
            gain_results[index][...] = (
                total[index : index + 1, :] / gains[index : index + 1, share]
            )
        gain_gather.finish()

    if last:
        for step in range(1, groups):
            source = (grid.dp - step) % groups
            column_copy(step, source).wait_recv()
            for place in range(RATE):
                pad_copy(step, place, source).wait_recv()
        for copy in pad_own:
            copy.wait()
        count = padded.shape[0]
        for place in range(RATE):
            total = jnp.zeros(grad_compress.shape[1:], f32)
            for source in range(groups):
                total = total + dot_tn(
                    padded_all[source, :, place * size : (place + 1) * size],
                    fresh_all[source].reshape(count, local),
                )
            grad_compress[place] = total

    first.finish()
    second.finish()
    if last:
        for step in range(1, groups):
            column_copy(step, grid.dp).wait_send()
            for place in range(RATE):
                pad_copy(step, place, grid.dp).wait_send()
    grid.finish()
    for chunk in range(CHUNKS):

        @pl.when(section != home)
        def _():
            ship_copy(chunk).wait_send()

        @pl.when(section == home)
        def _():
            ship_copy(chunk).wait_recv()
            if last:
                keep_row(chunk).wait()

    @pl.when(late)
    def _():
        third.finish()
        if last:
            fresh_copy.wait_send()


def fresh_block(n):
    return -(-(CMEM - FRESH_START) // (16 * n)) * 16


def backward_layer(collective, n, groups, home, grad, x_rows, residual, hidden, fresh, weights,
                   gains, q, kv, log_sum, docs, key_docs, normed, two, active, attended,
                   earlier_gains=(), padded=[], earlier=[]):
    wq, wkv, wo, wup, wdown = weights
    width = wo.shape[1]
    local = wq.shape[1]
    block = ROWS // n
    size = width // groups
    inner = wup.shape[1]
    last = home == 0
    shape = jax.ShapeDtypeStruct
    any_space = pl.BlockSpec(memory_space=pl.ANY)
    rows = shape((CHUNKS, n, block, width), bf16)
    ship = shape((2,) + rows.shape, bf16) if last else rows
    fresh_shape = (n, fresh_block(n), width)
    outs = [rows, ship, shape((1,) + fresh_shape, bf16)]
    outs += [shape((size, local), f32)] * 3
    outs += [shape((local, size), f32), shape((size, inner), f32), shape((inner, size), f32)]
    outs += [shape((1, size), f32)] * 2
    out_specs = vmem_specs(1) + [any_space] + vmem_specs(9)
    tile_count = 4 + 2 * inner // size
    dma = pltpu.SemaphoreType.DMA
    if last:
        outs.append(shape((RATE, size, local), f32))
        out_specs += vmem_specs(1)
    return pl.pallas_call(
        functools.partial(backward_kernel, n, groups, home),
        name="backward_%d" % home,
        out_shape=outs,
        in_specs=vmem_specs(20 + len(earlier_gains)) + [any_space] * len(padded + earlier),
        out_specs=out_specs,
        scratch_shapes=[
            pltpu.VMEM((SEG, inner), bf16),
            pltpu.VMEM(rows.shape, bf16),
            pltpu.VMEM((SEG, local), bf16),
            pltpu.VMEM((CMEM + MEM + SEG, 2 * local), bf16),
            pltpu.VMEM((CHUNKS, block, width), f32),
            pltpu.VMEM((MEM + SEG, HD), jnp.int32),
            pltpu.VMEM((local // HD, HD, CMEM + MEM + SEG), bf16),
            pltpu.VMEM((CMEM + MEM + SEG, 2 * local), f32),
        ]
        + line_scratch(CHUNKS, n, block, width)
        + line_scratch(CHUNKS, n, block, width)
        + line_scratch(1, n, fresh_block(n), width)
        + grid_scratch(groups, tile_count, size, 4)
        + [dma((CHUNKS,))] * 2
        + [pltpu.VMEM((2, size, size), f32), pltpu.VMEM((n, 8, size), f32), dma((2, n)), dma((n,))]
        + (
            [
                pltpu.VMEM((groups, n, fresh_block(n), local), bf16),
                pltpu.VMEM((groups, n * fresh_block(n), RATE * size), bf16),
                dma((9 + RATE,)),
                dma((CHUNKS,)),
                dma((2,)),
                dma((2, groups - 1, RATE)),
                dma((2, groups - 1)),
            ]
            if last
            else []
        ),
        compiler_params=pltpu.CompilerParams(
            collective_id=collective, has_side_effects=True, vmem_limit_bytes=65000 * 1024
        ),
    )(grad.reshape(rows.shape), x_rows.reshape(rows.shape), residual, hidden, fresh,
      wq, wkv, wo, wup, wdown, gains, q, kv, log_sum, docs, key_docs, normed, two, active,
      attended, *earlier_gains, *padded, *earlier)


def keep_kernel(count, *refs):
    small_in, big_in, refs = refs[:2], refs[2 : 2 + count], refs[2 + count :]
    small_out, big_out, refs = refs[:2], refs[2 : 2 + count], refs[2 + count :]
    held, sems = refs[:count], refs[count]
    taken = [
        pltpu.make_async_copy(big_in[i], held[i], sems.at[0, i]) for i in range(count)
    ]
    given = [
        pltpu.make_async_copy(held[i], big_out[i], sems.at[1, i]) for i in range(count)
    ]
    for copy in taken:
        copy.start()
    for i in range(2):
        small_out[i][...] = small_in[i][...]
    for i in range(count):
        taken[i].wait()
        given[i].start()
    for copy in given:
        copy.wait()


def keep_results(small, big):
    any_space = pl.BlockSpec(memory_space=pl.ANY)
    count = len(big)
    arrays = small + big
    return pl.pallas_call(
        functools.partial(keep_kernel, count),
        name="keep_results",
        out_shape=[jax.ShapeDtypeStruct(x.shape, x.dtype) for x in arrays],
        in_specs=vmem_specs(2) + [any_space] * count,
        out_specs=vmem_specs(2) + [any_space] * count,
        scratch_shapes=[pltpu.VMEM(x.shape, x.dtype) for x in big]
        + [pltpu.SemaphoreType.DMA((2, count))],
        compiler_params=pltpu.CompilerParams(vmem_limit_bytes=65000 * 1024),
    )(*arrays)


def project(rows, weight):
    return jnp.dot(rows, weight, preferred_element_type=f32).astype(bf16)


def shards(
    block_input,
    doc_ids,
    memory,
    compressed,
    gain_attn,
    w_query,
    w_key,
    w_value,
    w_out,
    gain_ffn,
    w_up,
    w_down,
    w_compress,
    cotangent,
):
    section = lax.axis_index("section")
    first = section == 0
    n = lax.axis_size("tensor")
    groups = lax.axis_size("dp")
    tensor_index = lax.axis_index("tensor")
    width = block_input.shape[2]
    local = w_query.shape[2]
    gains = jnp.stack([gain_attn[0], gain_ffn[0]])

    history = doc_ids[0]
    memory_docs = lax.dynamic_slice_in_dim(history, section * SEG, MEM, 0)
    token_docs = lax.dynamic_slice_in_dim(history, MEM + section * SEG, SEG, 0)
    docs = token_docs[None]
    key_docs = jnp.concatenate([memory_docs, token_docs])[:, None]
    tokens = lax.dynamic_slice_in_dim(block_input[0], section * SEG, SEG, 0)
    grad_now = lax.dynamic_slice_in_dim(cotangent[0], section * SEG, SEG, 0)

    fresh_count = n * fresh_block(n)
    lead = OLD_ROWS - FRESH_START
    trail = fresh_count - lead - COMP_ROWS
    padded = jnp.concatenate(
        [
            jnp.zeros((RATE * lead + PAD, width), bf16),
            memory[0, 0],
            jnp.zeros((RATE * trail, width), bf16),
        ]
    ).reshape(fresh_count, RATE * width)
    fresh_piece = project(padded, w_compress[0].reshape(RATE * width, local))
    fresh_piece = fresh_piece[lead : lead + COMP_ROWS]
    kept = compressed[0, 0, COMP_ROWS + FRESH_START :]
    piece = jnp.concatenate(
        [lax.dynamic_slice_in_dim(kept, tensor_index * local, local, 1), fresh_piece]
    )
    old = compressed[0, 0, COMP_ROWS : COMP_ROWS + FRESH_START]
    m_rows = jnp.where(first, memory[0, 0], block_input[0, :SEG])

    own = (w_query[0], w_key[0], w_value[0], w_out[0], w_up[0], w_down[0])
    low, high, (middle, shipped, outputs), *layers = forward(
        1, n, groups, m_rows, tokens, gains, docs, key_docs, own, old, piece, compressed[0, 0],
        memory[0, 0],
    )
    outputs = outputs.reshape(2 * SEG, width)
    saved = [
        (tokens, m_rows, *low),
        (middle.reshape(SEG, width), shipped.reshape(SEG, width), *high),
    ]
    weight_layers = [layer[:5] for layer in layers]
    gains_by_layer = [layer[5] for layer in layers]
    c_rows = [layer[6] for layer in layers]

    handed = []
    for layer in (1, 0):
        (tokens, m_rows, normed, queries, kv, log_total, attended, residual, two, hidden,
         active) = saved[layer]
        block = fresh_block(n)
        fresh_rows = jnp.concatenate(
            [c_rows[layer][FRESH_START:], m_rows[: n * block - (CMEM - FRESH_START)]]
        ).reshape(1, n, block, width)
        result = backward_layer(
            4 + layer, n, groups, layer, grad_now, tokens, residual, hidden, fresh_rows,
            weight_layers[layer], gains_by_layer[layer], queries, kv, log_total, docs, key_docs,
            normed, two, active, attended, *handed,
        )
        dx, shipped, d_fresh, *grads = result
        grad_now = dx.reshape(SEG, width)
        handed = [grads[6:8], [padded], grads[:6] + [shipped, d_fresh]]

    gain_attn_grad, gain_ffn_grad, *kept = keep_results(
        grads[6:8], [outputs, shipped.reshape(2 * SEG, width), *grads[:6], grads[8]]
    )
    outputs, input_grads, grad_query, grad_key, grad_value, grad_out, grad_up, grad_down = kept[:8]
    return (
        outputs[None, None],
        input_grads[None, None],
        gain_attn_grad,
        grad_query[None],
        grad_key[None],
        grad_value[None],
        grad_out[None],
        gain_ffn_grad,
        grad_up[None],
        grad_down[None],
        kept[8][None],
    )


def solution(mesh):
    return jax.shard_map(
        shards,
        mesh=mesh,
        in_specs=(
            P("dp", None, None),
            P("dp", None),
            P("section", "dp", None, None),
            P("section", "dp", None, None),
            P("section", None),
            P("section", None, "tensor"),
            P("section", None, "tensor"),
            P("section", None, "tensor"),
            P("section", "tensor", None),
            P("section", None),
            P("section", None, "tensor"),
            P("section", "tensor", None),
            P("section", None, None, "tensor"),
            P("dp", None, None),
        ),
        out_specs=(
            P("section", "dp", None, None),
            P("section", "dp", None, None),
            P("section", "dp"),
            P("section", "dp", "tensor"),
            P("section", "dp", "tensor"),
            P("section", "dp", "tensor"),
            P("section", "tensor", "dp"),
            P("section", "dp"),
            P("section", "dp", "tensor"),
            P("section", "tensor", "dp"),
            P("section", None, "dp", "tensor"),
        ),
        check_vma=False,
    )
```

```python
import functools

import jax
import jax.numpy as jnp
from jax import lax
from jax.experimental import pallas as pl
from jax.experimental.pallas import tpu as pltpu
from jax.sharding import PartitionSpec as P

HD = 128
SEG = 512
MEM = 512
CMEM = 512
RATE = 3
COMP_ROWS = 171
PAD = 1
OLD_ROWS = CMEM - COMP_ROWS
CHUNKS = 4
ROWS = SEG // CHUNKS
FRESH_START = OLD_ROWS // 16 * 16
SPLIT_START = FRESH_START // 32 * 16 + 16

epsilon = 1e-06
masked_value = -1000000000.0
MESH = pl.DeviceIdType.MESH
f32 = jnp.float32
bf16 = jnp.bfloat16
GELU_A = 0.7978845608028654
GELU_B = 0.044715


def inverse_rms(rows):
    return lax.rsqrt(jnp.mean(rows * rows, axis=-1, keepdims=True) + epsilon)


def rms_pull(grad, rows, gain):
    scale = inverse_rms(rows)
    scaled_grad = grad * gain
    inner = jnp.mean(scaled_grad * rows, axis=-1, keepdims=True)
    return scale * (scaled_grad - rows * (scale * scale * inner))


def gelu(x):
    return 0.5 * x * (1.0 + jnp.tanh(GELU_A * (x + GELU_B * x * x * x)))


def gelu_slope(x):
    square = x * x
    bend = jnp.tanh(GELU_A * (x + GELU_B * x * square))
    return 0.5 * (1.0 + bend) + 0.5 * x * (1.0 - bend * bend) * GELU_A * (
        1.0 + 3.0 * GELU_B * square
    )


def dot_nn(a, b):
    return lax.dot_general(a, b, (((1,), (0,)), ((), ())), preferred_element_type=f32)


def dot_nt(a, b):
    return lax.dot_general(a, b, (((1,), (1,)), ((), ())), preferred_element_type=f32)


def dot_tn(a, b):
    return lax.dot_general(a, b, (((0,), (0,)), ((), ())), preferred_element_type=f32)


def greet(n, with_peer=False, groups=0, everyone=False):
    me = lax.axis_index("tensor")
    barrier = pltpu.get_barrier_semaphore()
    for step in (-1, 1):
        other = me + step

        @pl.when((other >= 0) & (other < n))
        def _():
            pl.semaphore_signal(barrier, inc=1, device_id={"tensor": other}, device_id_type=MESH)

    extra = 0
    if with_peer:
        extra += 1
        peer = 1 - lax.axis_index("section")
        pl.semaphore_signal(barrier, inc=1, device_id={"section": peer}, device_id_type=MESH)
    if groups:
        mine = lax.axis_index("dp")
        others = [mine + 1 - 2 * (mine % 2)]
        others += [(mine + 2 * step) % groups for step in range(1, groups // 2)]
        if everyone:
            others = [(mine + step) % groups for step in range(1, groups)]
        for other in others:
            pl.semaphore_signal(barrier, inc=1, device_id={"dp": other}, device_id_type=MESH)
        extra += len(others)
    pl.semaphore_wait(barrier, jnp.where((me > 0) & (me < n - 1), 2 + extra, 1 + extra))
    return me


class GridSum:
    def __init__(self, groups, home, tiles, landings, sems, parts):
        self.groups, self.home, self.tiles, self.parts = groups, home, tiles, parts
        self.from_core, self.from_row, self.from_section = landings
        self.core_sems, self.row_sems, self.section_sems = sems
        self.dp = lax.axis_index("dp")
        self.section = lax.axis_index("section")
        self.core = self.dp % 2
        self.row = self.dp // 2
        self.rows = groups // 2

    def span(self, part):
        start, stop = self.parts[part]
        return pl.ds(start, stop - start)

    def core_copy(self, part, row):
        return pltpu.make_async_remote_copy(
            src_ref=self.tiles.at[row * 2 + 1 - self.core, self.span(part)],
            dst_ref=self.from_core.at[row, self.span(part)],
            send_sem=self.core_sems.at[0, part, row],
            recv_sem=self.core_sems.at[1, part, row],
            device_id={"dp": self.dp + 1 - 2 * self.core},
            device_id_type=MESH,
        )

    def row_copy(self, part, step):
        target = (self.row + step) % self.rows
        return pltpu.make_async_remote_copy(
            src_ref=self.tiles.at[target * 2 + self.core, self.span(part)],
            dst_ref=self.from_row.at[step - 1, self.span(part)],
            send_sem=self.row_sems.at[0, part, step - 1],
            recv_sem=self.row_sems.at[1, part, step - 1],
            device_id={"dp": target * 2 + self.core},
            device_id_type=MESH,
        )

    def section_copy(self, part):
        return pltpu.make_async_remote_copy(
            src_ref=self.tiles.at[self.dp, self.span(part)],
            dst_ref=self.from_section.at[self.span(part)],
            send_sem=self.section_sems.at[0, part],
            recv_sem=self.section_sems.at[1, part],
            device_id={"section": 1 - self.section},
            device_id_type=MESH,
        )

    def add(self, place, landing, part):
        start, stop = self.parts[part]

        def body(tile, carry):
            self.tiles[place, tile] = (
                self.tiles[place, tile].astype(f32) + landing[tile].astype(f32)
            ).astype(bf16)
            return carry

        lax.fori_loop(start, stop, body, 0)

    def send_core(self, part):
        for row in range(self.rows):
            self.core_copy(part, row).start()

    def send_rows(self, part):
        for row in range(self.rows):
            self.core_copy(part, row).wait_recv()
            self.add(row * 2 + self.core, self.from_core.at[row], part)
        for step in range(1, self.rows):
            self.row_copy(part, step).start()

    def send_section(self, part):
        for step in range(1, self.rows):
            self.row_copy(part, step).wait_recv()
            self.add(self.dp, self.from_row.at[step - 1], part)

        @pl.when(self.section != self.home)
        def _():
            self.section_copy(part).start()

    def close(self, part, write):
        @pl.when(self.section == self.home)
        def _():
            self.section_copy(part).wait_recv()
            for tile in range(*self.parts[part]):
                write(
                    tile,
                    self.tiles[self.dp, tile].astype(f32) + self.from_section[tile].astype(f32),
                )

    def finish(self):
        for part in range(len(self.parts)):
            for row in range(self.rows):
                self.core_copy(part, row).wait_send()
            for step in range(1, self.rows):
                self.row_copy(part, step).wait_send()

            @pl.when(self.section != self.home)
            def _():
                self.section_copy(part).wait_send()


def grid_scratch(groups, tiles, size, parts):
    rows = groups // 2
    return [
        pltpu.VMEM((groups, tiles, size, size), bf16),
        pltpu.VMEM((rows, tiles, size, size), bf16),
        pltpu.VMEM((rows - 1, tiles, size, size), bf16),
        pltpu.VMEM((tiles, size, size), bf16),
        pltpu.SemaphoreType.DMA((2, parts, rows)),
        pltpu.SemaphoreType.DMA((2, parts, rows - 1)),
        pltpu.SemaphoreType.DMA((2, parts)),
    ]


class LineSum:
    def __init__(self, n, me, middle, part, out, held, sems):
        self.n, self.me, self.middle, self.part, self.out = n, me, middle, part, out
        self.from_left, self.from_right = held
        self.rs_send, self.rs_recv, self.ag_send, self.ag_recv = sems
        self.stages = 2 * n - 1

    def reduce_copy(self, src, landing, side, chunk, block, target):
        return pltpu.make_async_remote_copy(
            src_ref=src,
            dst_ref=landing.at[chunk, block],
            send_sem=self.rs_send.at[side, chunk, block],
            recv_sem=self.rs_recv.at[side, chunk, block],
            device_id={"tensor": target},
            device_id_type=MESH,
        )

    def gather_copy(self, side, chunk, block, target):
        return pltpu.make_async_remote_copy(
            src_ref=self.out.at[chunk, block],
            dst_ref=self.out.at[chunk, block],
            send_sem=self.ag_send.at[side, chunk, block],
            recv_sem=self.ag_recv.at[chunk, block],
            device_id={"tensor": target},
            device_id_type=MESH,
        )

    def put(self, chunk, rows):
        self.part[chunk] = rows.astype(bf16).reshape(self.part.shape[1:])

    def rows(self, chunk):
        whole = self.out[chunk]
        return whole.reshape(-1, whole.shape[-1])

    def stage(self, chunk, stage):
        n = self.n
        if stage == 0:
            self.first_sends(chunk)
        elif stage <= n - 2:
            self.hop(chunk, stage)
        elif stage == n - 1:
            self.own_rows(chunk)
        else:
            self.forward(chunk, stage - n + 1)

    def first_sends(self, chunk):
        n, part = self.n, self.part

        @pl.when(self.me == 0)
        def _():
            for block in range(n - 1, 0, -1):
                self.reduce_copy(
                    part.at[chunk, block], self.from_left, 0, chunk, block, 1
                ).start()

        @pl.when(self.me == n - 1)
        def _():
            for block in range(n - 1):
                self.reduce_copy(
                    part.at[chunk, block], self.from_right, 1, chunk, block, n - 2
                ).start()

    def hop(self, chunk, step):
        n, part = self.n, self.part

        @pl.when(self.me == step)
        def _():
            landing = self.from_left
            for block in range(n - 1, step, -1):
                self.reduce_copy(
                    part.at[chunk, block], landing, 0, chunk, block, step
                ).wait_recv()
                part[chunk, block] = (
                    landing[chunk, block].astype(f32) + part[chunk, block].astype(f32)
                ).astype(bf16)
                self.reduce_copy(
                    part.at[chunk, block], landing, 0, chunk, block, step + 1
                ).start()

        @pl.when(self.me == n - 1 - step)
        def _():
            landing = self.from_right
            mine = n - 1 - step
            for block in range(mine):
                self.reduce_copy(
                    part.at[chunk, block], landing, 1, chunk, block, mine
                ).wait_recv()
                part[chunk, block] = (
                    landing[chunk, block].astype(f32) + part[chunk, block].astype(f32)
                ).astype(bf16)
                self.reduce_copy(
                    part.at[chunk, block], landing, 1, chunk, block, mine - 1
                ).start()

    def own_rows(self, chunk):
        n, me, part = self.n, self.me, self.part

        @pl.when(me > 0)
        def _():
            self.reduce_copy(part.at[chunk, me], self.from_left, 0, chunk, me, me).wait_recv()

        @pl.when(me < n - 1)
        def _():
            self.reduce_copy(part.at[chunk, me], self.from_right, 1, chunk, me, me).wait_recv()

        total = part[chunk, me].astype(f32)
        total = total + jnp.where(me > 0, self.from_left[chunk, me].astype(f32), 0.0)
        total = total + jnp.where(me < n - 1, self.from_right[chunk, me].astype(f32), 0.0)
        self.out[chunk, me] = self.middle(chunk, me, total).astype(bf16)

        @pl.when(me < n - 1)
        def _():
            self.gather_copy(0, chunk, me, me + 1).start()

        @pl.when(me > 0)
        def _():
            self.gather_copy(1, chunk, me, me - 1).start()

    def forward(self, chunk, step):
        n, me = self.n, self.me
        left_block = me - step

        @pl.when(left_block >= 0)
        def _():
            self.gather_copy(0, chunk, left_block, me).wait_recv()

            @pl.when(me < n - 1)
            def _():
                self.gather_copy(0, chunk, left_block, me + 1).start()

        right_block = me + step

        @pl.when(right_block < n)
        def _():
            self.gather_copy(1, chunk, right_block, me).wait_recv()

            @pl.when(me > 0)
            def _():
                self.gather_copy(1, chunk, right_block, me - 1).start()

    def finish(self):
        n, me, part = self.n, self.me, self.part
        for chunk in range(part.shape[0]):
            for block in range(n):

                @pl.when((me < n - 1) & (block > me))
                def _():
                    self.reduce_copy(
                        part.at[chunk, block], self.from_left, 0, chunk, block, me
                    ).wait_send()

                @pl.when((me > 0) & (block < me))
                def _():
                    self.reduce_copy(
                        part.at[chunk, block], self.from_right, 1, chunk, block, me
                    ).wait_send()

                @pl.when((me < n - 1) & (block <= me))
                def _():
                    self.gather_copy(0, chunk, block, me).wait_send()

                @pl.when((me > 0) & (block >= me))
                def _():
                    self.gather_copy(1, chunk, block, me).wait_send()


def line_scratch(chunks, n, block, width):
    return [pltpu.VMEM((chunks, n, block, width), bf16)] * 3 + [
        pltpu.SemaphoreType.DMA((2, chunks, n)),
        pltpu.SemaphoreType.DMA((2, chunks, n)),
        pltpu.SemaphoreType.DMA((2, chunks, n)),
        pltpu.SemaphoreType.DMA((chunks, n)),
    ]


def make_line(n, me, middle, out, scratch):
    return LineSum(n, me, middle, scratch[0], out, scratch[1:3], scratch[3:7])


def run_two(order, first, second, produce, between, finished, extra):
    lag = first.stages - 1
    last = len(order) - 1
    for slot in range(2 * lag + last + 1):
        if slot <= last:
            produce(order[slot])
        extra(slot)
        for place, chunk in enumerate(order):
            stage = slot - lag - place
            if 1 <= stage <= lag:
                second.stage(chunk, stage)
            if stage == lag:
                finished(chunk)
        for place, chunk in enumerate(order):
            stage = slot - place
            if 0 <= stage <= lag:
                first.stage(chunk, stage)
        if 0 <= slot - lag <= last:
            chunk = order[slot - lag]
            between(chunk)
            second.stage(chunk, 0)


def run_chain(order, sums, works, finished, extra):
    lag = sums[0].stages - 1
    last = len(order) - 1
    for slot in range(len(sums) * lag + last + 1):
        if slot <= last:
            works[0](order[slot])
        extra(slot)
        for level in range(len(sums) - 1, -1, -1):
            for place, chunk in enumerate(order):
                stage = slot - level * lag - place
                if min(level, 1) <= stage <= lag:
                    sums[level].stage(chunk, stage)
                if stage == lag:
                    finished(level, chunk)
        for level in range(len(sums) - 1, 0, -1):
            if 0 <= slot - level * lag <= last:
                chunk = order[slot - level * lag]
                works[level](chunk)
                sums[level].stage(chunk, 0)


class WeightSwap:
    def __init__(self, groups, own, layers, sems):
        self.groups, self.own, self.layers = groups, own, layers
        self.x_sems, self.row_sems, self.core_sems, self.local_sems = sems
        self.dp = lax.axis_index("dp")
        self.section = lax.axis_index("section")
        self.core = self.dp % 2
        self.row = self.dp // 2
        self.rows = groups // 2

    def share(self, array, piece):
        rows = self.own[array][0].shape[0] // self.groups
        return pl.ds(pl.multiple_of(piece * rows, rows), rows)

    def block(self, layer, array, piece):
        ref, lanes = self.layers[layer][array]
        return ref.at[self.share(array, piece), lanes]

    def section_copy(self, layer, array):
        ref, lanes = self.own[array]
        return pltpu.make_async_remote_copy(
            src_ref=ref.at[self.share(array, self.dp), lanes],
            dst_ref=self.block(layer, array, self.dp),
            send_sem=self.x_sems.at[0, array],
            recv_sem=self.x_sems.at[1, array],
            device_id={"section": 1 - self.section},
            device_id_type=MESH,
        )

    def row_copy(self, layer, array, step, source, target):
        piece = source * 2 + self.core
        return pltpu.make_async_remote_copy(
            src_ref=self.block(layer, array, piece),
            dst_ref=self.block(layer, array, piece),
            send_sem=self.row_sems.at[0, array, step - 1],
            recv_sem=self.row_sems.at[1, array, step - 1],
            device_id={"dp": target * 2 + self.core},
            device_id_type=MESH,
        )

    def core_copy(self, layer, array, step, core):
        piece = (self.row - step) % self.rows * 2 + core
        return pltpu.make_async_remote_copy(
            src_ref=self.block(layer, array, piece),
            dst_ref=self.block(layer, array, piece),
            send_sem=self.core_sems.at[0, array, step],
            recv_sem=self.core_sems.at[1, array, step],
            device_id={"dp": self.dp + 1 - 2 * self.core},
            device_id_type=MESH,
        )

    def local_copy(self, layer, array):
        ref, lanes = self.own[array]
        to, to_lanes = self.layers[layer][array]
        return pltpu.make_async_copy(
            ref.at[:, lanes], to.at[:, to_lanes], self.local_sems.at[array]
        )

    def take(self, layer, arrays):
        for array in arrays:
            self.section_copy(layer, array).wait_recv()
            for step in range(1, self.rows):
                target = (self.row + step) % self.rows
                self.row_copy(layer, array, step, self.row, target).start()
            self.core_copy(layer, array, 0, self.core).start()

    def spread(self, layer, arrays):
        for array in arrays:
            for step in range(1, self.rows):
                source = (self.row - step) % self.rows
                self.row_copy(layer, array, step, source, self.row).wait_recv()
                self.core_copy(layer, array, step, self.core).start()

    def settle(self, layer, arrays):
        for array in arrays:
            for step in range(self.rows):
                self.core_copy(layer, array, step, 1 - self.core).wait_recv()

    def on_arrival(self, work, arrays):
        for layer in range(2):

            @pl.when(self.section != layer)
            def _():
                work(layer, arrays)

    def finish(self):
        for layer in range(2):
            for array in range(len(self.own)):

                @pl.when(self.section == layer)
                def _():
                    self.section_copy(layer, array).wait_send()

                @pl.when(self.section != layer)
                def _():
                    for step in range(1, self.rows):
                        target = (self.row + step) % self.rows
                        self.row_copy(layer, array, step, self.row, target).wait_send()
                    for step in range(self.rows):
                        self.core_copy(layer, array, step, self.core).wait_send()


class LineGather:
    def __init__(self, n, me, place, sems):
        self.n, self.me, self.place = n, me, place
        self.send, self.recv = sems

    def copy(self, side, block, target):
        return pltpu.make_async_remote_copy(
            src_ref=self.place(block),
            dst_ref=self.place(block),
            send_sem=self.send.at[side, block],
            recv_sem=self.recv.at[block],
            device_id={"tensor": target},
            device_id_type=MESH,
        )

    def start(self):
        n, me = self.n, self.me

        @pl.when(me < n - 1)
        def _():
            self.copy(0, me, me + 1).start()

        @pl.when(me > 0)
        def _():
            self.copy(1, me, me - 1).start()

    def forward(self, step):
        n, me = self.n, self.me
        left_block = me - step

        @pl.when(left_block >= 0)
        def _():
            self.copy(0, left_block, me).wait_recv()

            @pl.when(me < n - 1)
            def _():
                self.copy(0, left_block, me + 1).start()

        right_block = me + step

        @pl.when(right_block < n)
        def _():
            self.copy(1, right_block, me).wait_recv()

            @pl.when(me > 0)
            def _():
                self.copy(1, right_block, me - 1).start()

    def finish(self):
        n, me = self.n, self.me
        for block in range(n):

            @pl.when((me < n - 1) & (block <= me))
            def _():
                self.copy(0, block, me).wait_send()

            @pl.when((me > 0) & (block >= me))
            def _():
                self.copy(1, block, me).wait_send()


def columns_of(ref, lanes, start):
    def place(block):
        at = pl.ds(pl.multiple_of(block * lanes, lanes), lanes)
        return ref.at[start:CMEM, at]

    return place


def score_columns(head, chunk, q_ref, kv_ref, docs, keys_docs):
    lanes = slice(head * HD, (head + 1) * HD)
    width = CMEM + MEM + (chunk + 1) * ROWS
    query = q_ref[chunk * ROWS : (chunk + 1) * ROWS, lanes]
    scores = dot_nt(kv_ref[:width, lanes], query) * HD ** (-0.5)
    own = docs[:, chunk * ROWS : (chunk + 1) * ROWS]
    same = keys_docs[: MEM + chunk * ROWS, :] == own
    tail_docs = keys_docs[MEM + chunk * ROWS : MEM + (chunk + 1) * ROWS, :]
    key_place = lax.broadcasted_iota(jnp.int32, (ROWS, ROWS), 0)
    query_place = lax.broadcasted_iota(jnp.int32, (ROWS, ROWS), 1)
    tail_same = (tail_docs == own) & (key_place <= query_place)
    middle_end = CMEM + MEM + chunk * ROWS
    return jnp.concatenate(
        [
            scores[:CMEM],
            jnp.where(same, scores[CMEM:middle_end], masked_value),
            jnp.where(tail_same, scores[middle_end:], masked_value),
        ],
        axis=0,
    )


class ForwardLayer:
    def __init__(self, n, me, weights, x_ref, saved, out, docs, keys_docs, scratch):
        self.wq, self.wkv, self.wo, self.wup, self.wdown, self.gains, self.c_ref = weights
        (self.normed, self.q_ref, self.kv_ref, self.log_sum, self.attended, self.residual,
         self.two, self.hidden, self.active) = saved
        self.x_ref, self.docs, self.keys_docs = x_ref, docs, keys_docs
        self.values_t, first_scratch, second_scratch = scratch[0], scratch[1:8], scratch[8:15]
        self.local = self.wq.shape[1]
        self.heads = self.local // HD
        self.first = make_line(n, me, self.attention_middle, self.two, first_scratch)
        self.second = make_line(n, me, self.output_middle, out, second_scratch)

    def project(self, wide, at):
        block = (wide * inverse_rms(wide) * self.gains[0:1, :]).astype(bf16)
        self.normed[at, :] = block
        self.kv_ref[at, :] = dot_nn(block, self.wkv[...]).astype(bf16)
        return block

    def flip_values(self, rows):
        for head in range(self.heads):
            lanes = slice(self.local + head * HD, self.local + (head + 1) * HD)
            self.values_t[head, :, rows] = self.kv_ref[rows, lanes].astype(f32).T.astype(bf16)

    def project_block(self, source, place):
        def body(step, carry):
            rows = pl.ds(pl.multiple_of(step * 256, 256), 256)
            at = pl.ds(pl.multiple_of(place * SEG + step * 256, 256), 256)
            self.project(source[rows, :].astype(f32), at)
            return carry

        lax.fori_loop(0, SEG // 256, body, 0)
        self.flip_values(slice(place * SEG, (place + 1) * SEG))

    def attention_middle(self, chunk, me, total):
        rows = self.x_ref[chunk, me].astype(f32) + total
        self.residual[chunk] = rows
        return rows * inverse_rms(rows) * self.gains[1:2, :]

    def output_middle(self, chunk, me, total):
        return self.residual[chunk] + total

    def attend(self, chunk):
        rows = slice(chunk * ROWS, (chunk + 1) * ROWS)
        at = slice(CMEM + MEM + chunk * ROWS, CMEM + MEM + (chunk + 1) * ROWS)
        source = self.x_ref[chunk]
        block = self.project(source.reshape(ROWS, source.shape[-1]).astype(f32), at)
        self.q_ref[rows, :] = dot_nn(block, self.wq[...]).astype(bf16)
        self.flip_values(at)
        for head in range(self.heads):
            lanes = slice(head * HD, (head + 1) * HD)
            scores = score_columns(
                head, chunk, self.q_ref, self.kv_ref, self.docs, self.keys_docs
            )
            top = jnp.max(scores, axis=0, keepdims=True)
            powers = jnp.exp(scores - top)
            total = jnp.sum(powers, axis=0, keepdims=True)
            self.log_sum[head : head + 1, rows] = top + jnp.log(total)
            weights = (powers * (1.0 / total)).astype(bf16)
            mixed = dot_nn(self.values_t[head, :, : weights.shape[0]], weights)
            self.attended[rows, lanes] = mixed.T.astype(bf16)
        self.first.put(chunk, dot_nn(self.attended[rows, :], self.wo[...]))

    def feed(self, chunk):
        rows = slice(chunk * ROWS, (chunk + 1) * ROWS)
        before = dot_nn(self.first.rows(chunk), self.wup[...])
        self.hidden[rows, :] = before
        after = gelu(before).astype(bf16)
        self.active[rows, :] = after
        self.second.put(chunk, dot_nn(after, self.wdown[...]))


def forward_kernel(n, groups, *refs):
    m_ref, x_ref, own_gains, docs, key_docs = refs[:5]
    own_refs, (old, piece, compressed, memory) = refs[5:11], refs[11:15]
    saved = [refs[15:24], refs[24:33]]
    middle_rows, shipped, outputs = refs[33:36]
    layer_refs = [refs[36:43], refs[43:50]]
    fresh_rows, refs = refs[50:52], refs[52:]
    keys_docs, last_rows = refs[:2]
    scratch = [refs[2:17], refs[17:32]]
    (ship_send, ship_recv, final_send, final_recv, keep, *swap_sems, item_sems, local_sems) = (
        refs[32:43]
    )
    gather_sems = refs[43:47]
    me = greet(n, True, groups)
    section = lax.axis_index("section")
    wq, wup = layer_refs[0][0], layer_refs[0][3]
    local, inner, width = wq.shape[1], wup.shape[1], wup.shape[0]
    whole = slice(None)
    front, back = slice(0, inner // 2), slice(inner // 2, inner)
    lead, trail = slice(0, width // 2), slice(width // 2, width)
    q_own, k_own, v_own, o_own, up_own, down_own = own_refs
    own = [(q_own, whole), (k_own, whole), (v_own, whole), (o_own, whole),
           (up_own, front), (up_own, back), (down_own, lead), (down_own, trail)]
    places = [
        [(w[0], whole), (w[1], slice(0, local)), (w[1], slice(local, 2 * local)),
         (w[2], whole), (w[3], front), (w[3], back), (w[4], lead), (w[4], trail)]
        for w in layer_refs
    ]
    swap = WeightSwap(groups, own, places, swap_sems)
    gathers = [
        LineGather(n, me, columns_of(layer_refs[layer][6], local, (SPLIT_START, FRESH_START)[layer]),
                   gather_sems[2 * layer : 2 * layer + 2])
        for layer in range(2)
    ]
    items = [
        [(own_gains, layer_refs[0][5]), (piece, gathers[0].place(me)),
         (old.at[:SPLIT_START, :], layer_refs[0][6].at[:SPLIT_START, :])],
        [(own_gains, layer_refs[1][5]), (compressed, layer_refs[1][6]), (memory, shipped)],
    ]

    def peer_copy(src, dst, send, recv):
        return pltpu.make_async_remote_copy(
            src_ref=src,
            dst_ref=dst,
            send_sem=send,
            recv_sem=recv,
            device_id={"section": 1 - section},
            device_id_type=MESH,
        )

    def item_copy(layer, index):
        src, dst = items[layer][index]
        return peer_copy(src, dst, item_sems.at[0, index], item_sems.at[1, index])

    local_rows = [
        pltpu.make_async_copy(compressed, layer_refs[0][6], local_sems.at[0]),
        pltpu.make_async_copy(old, layer_refs[1][6].at[:FRESH_START, :], local_sems.at[0]),
        pltpu.make_async_copy(
            piece.at[FRESH_START - SPLIT_START :, :], gathers[1].place(me), local_sems.at[1]
        ),
    ]
    keys_docs[...] = jnp.broadcast_to(key_docs[...], keys_docs.shape)
    layers = [
        ForwardLayer(n, me, layer_refs[0], x_ref, saved[0], middle_rows, docs, keys_docs,
                     scratch[0]),
        ForwardLayer(n, me, layer_refs[1], middle_rows, saved[1], last_rows, docs, keys_docs,
                     scratch[1]),
    ]

    @pl.when(section == 0)
    def _():
        item_copy(0, 0).start()
        item_copy(0, 1).start()
        for array in range(3):
            swap.section_copy(0, array).start()
        item_copy(0, 2).start()
        for array in range(3, 8):
            swap.section_copy(0, array).start()
        for array in range(3):
            swap.local_copy(0, array).start()
        local_rows[0].start()
        for array in range(3, 8):
            swap.local_copy(0, array).start()
        layer_refs[0][5][...] = own_gains[...]
        local_rows[0].wait()
        for array in range(8):
            swap.local_copy(0, array).wait()

    @pl.when(section == 1)
    def _():
        item_copy(1, 0).start()
        for array in range(3):
            swap.section_copy(1, array).start()
        item_copy(1, 1).start()
        item_copy(1, 2).start()
        for array in range(3, 8):
            swap.section_copy(1, array).start()
        local_rows[1].start()
        local_rows[2].start()
        for array in range(8):
            swap.local_copy(1, array).start()
        layer_refs[1][5][...] = own_gains[...]
        item_copy(0, 0).wait_recv()
        item_copy(0, 1).wait_recv()
        gathers[0].start()
        swap.take(0, range(3))
        gathers[0].forward(1)
        swap.spread(0, range(3))
        for step in range(2, n):
            gathers[0].forward(step)
        swap.settle(0, range(3))

    layers[0].project_block(m_ref, 1)

    @pl.when(section == 1)
    def _():
        item_copy(0, 2).wait_recv()

    layers[0].project_block(layer_refs[0][6], 0)

    def keep_fresh(layer, memory_rows):
        shape = fresh_rows[layer].shape
        count = shape[1] * shape[2] - (CMEM - FRESH_START)
        rows = [layer_refs[layer][6][FRESH_START:, :], memory_rows[:count, :]]
        fresh_rows[layer][...] = jnp.concatenate(rows, axis=0).reshape(shape)

    @pl.when(section == 1)
    def _():
        swap.take(0, [3])
        swap.spread(0, [3])
        swap.settle(0, [3])

    lag = 2 * n - 2
    plans = [
        {
            1: [(swap.take, range(3))],
            2: [(swap.spread, range(3))],
            3: [(swap.settle, range(3))],
            10: [(swap.take, [3])],
            11: [(swap.spread, [3])],
            12: [(swap.settle, [3])],
            13: [(swap.take, [4])],
            14: [(swap.spread, [4]), (swap.take, [5])],
            15: [(swap.spread, [5]), (swap.take, [6])],
            16: [(swap.spread, [6]), (swap.take, [7])],
            17: [(swap.spread, [7]), (swap.settle, [4, 5])],
            18: [(swap.settle, [6, 7])],
        },
        {
            2: [(swap.take, [4])],
            3: [(swap.take, [5]), (swap.spread, [4])],
            4: [(swap.spread, [5]), (swap.take, [6])],
            5: [(swap.take, [7]), (swap.spread, [6]), (swap.settle, [4, 5])],
            6: [(swap.spread, [7]), (swap.settle, [6, 7])],
        },
    ]

    def ship_copy(chunk):
        return peer_copy(
            middle_rows.at[chunk], shipped.at[chunk], ship_send.at[chunk], ship_recv.at[chunk]
        )

    def final_copy(layer, chunk):
        rows = (middle_rows, last_rows)[layer]
        return peer_copy(
            rows.at[chunk], outputs.at[1 - layer, chunk], final_send.at[chunk],
            final_recv.at[chunk],
        )

    def keep_copy(layer, chunk):
        rows = (middle_rows, last_rows)[layer]
        return pltpu.make_async_copy(rows.at[chunk], outputs.at[layer, chunk], keep.at[chunk])

    def finished(level, chunk):
        if level == 1:

            @pl.when(section == 0)
            def _():
                ship_copy(chunk).start()
                keep_copy(0, chunk).start()

            @pl.when(section == 1)
            def _():
                final_copy(0, chunk).start()

        if level == 3:

            @pl.when(section == 0)
            def _():
                final_copy(1, chunk).start()

            @pl.when(section == 1)
            def _():
                keep_copy(1, chunk).start()

    def extra(slot):
        for place in range(2):
            if slot in plans[place]:

                @pl.when(section == place)
                def _():
                    for work, arrays in plans[place][slot]:
                        work(1 - place, arrays)

        if slot < n:

            @pl.when(section == 1)
            def _():
                if slot == 0:
                    local_rows[2].wait()
                    gathers[1].start()
                else:
                    gathers[1].forward(slot)

        if slot == lag + 2:

            @pl.when(section == 0)
            def _():
                item_copy(1, 0).wait_recv()
                item_copy(1, 1).wait_recv()

            @pl.when(section == 1)
            def _():
                local_rows[1].wait()
                for array in range(8):
                    swap.local_copy(1, array).wait()

            layers[1].project_block(layer_refs[1][6], 0)
        if slot == 2 * lag - 1:

            @pl.when(section == 0)
            def _():
                item_copy(1, 2).wait_recv()

            @pl.when(section == 1)
            def _():
                for chunk in range(CHUNKS):
                    ship_copy(chunk).wait_recv()

            layers[1].project_block(shipped.reshape(MEM, width), 1)
        if slot == 2:
            keep_fresh(0, m_ref)
        if slot == 2 * lag:
            keep_fresh(1, shipped.reshape(MEM, width))

    sums = [layers[0].first, layers[0].second, layers[1].first, layers[1].second]
    works = [layers[0].attend, layers[0].feed, layers[1].attend, layers[1].feed]
    run_chain(list(range(CHUNKS)), sums, works, finished, extra)
    for line in sums:
        line.finish()
    swap.finish()

    @pl.when(section == 0)
    def _():
        for chunk in range(CHUNKS):
            ship_copy(chunk).wait_send()
            keep_copy(0, chunk).wait()
            final_copy(1, chunk).wait_send()
            final_copy(0, chunk).wait_recv()
        for index in range(3):
            item_copy(0, index).wait_send()

    @pl.when(section == 1)
    def _():
        for chunk in range(CHUNKS):
            keep_copy(1, chunk).wait()
            final_copy(0, chunk).wait_send()
            final_copy(1, chunk).wait_recv()
        for index in range(3):
            item_copy(1, index).wait_send()
        for gather in gathers:
            gather.finish()


def vmem_specs(count):
    return [pl.BlockSpec(memory_space=pltpu.VMEM)] * count


def forward(collective, n, groups, m_rows, x_rows, gains, docs, key_docs, own, old, piece,
            compressed, memory):
    width, local, inner = x_rows.shape[1], own[0].shape[1], own[4].shape[1]
    block = ROWS // n
    shape = jax.ShapeDtypeStruct
    rows = shape((CHUNKS, n, block, width), bf16)
    saved = [
        shape((CMEM + MEM + SEG, width), bf16),
        shape((SEG, local), bf16),
        shape((CMEM + MEM + SEG, 2 * local), bf16),
        shape((8, SEG), f32),
        shape((SEG, local), bf16),
        shape((CHUNKS, block, width), f32),
        rows,
        shape((SEG, inner), f32),
        shape((SEG, inner), bf16),
    ]
    layer = [
        shape((width, local), bf16),
        shape((width, 2 * local), bf16),
        shape((local, width), bf16),
        shape((width, inner), bf16),
        shape((inner, width), bf16),
        shape(gains.shape, f32),
        shape((CMEM, width), bf16),
    ]
    outs = saved + saved + [rows, rows, shape((2,) + rows.shape, bf16)] + layer + layer
    outs += [shape((1, n, fresh_block(n), width), bf16)] * 2
    arrays, rows_y = 8, groups // 2
    dma = pltpu.SemaphoreType.DMA
    layer_scratch = (
        [pltpu.VMEM((local // HD, HD, CMEM + MEM + SEG), bf16)]
        + line_scratch(CHUNKS, n, block, width)
        + line_scratch(CHUNKS, n, block, width)
    )
    scratch = [
        pltpu.VMEM((MEM + SEG, HD), jnp.int32),
        pltpu.VMEM(rows.shape, bf16),
        *layer_scratch,
        *layer_scratch,
        dma((CHUNKS,)),
        dma((CHUNKS,)),
        dma((CHUNKS,)),
        dma((CHUNKS,)),
        dma((CHUNKS,)),
        dma((2, arrays)),
        dma((2, arrays, rows_y - 1)),
        dma((2, arrays, rows_y)),
        dma((arrays,)),
        dma((2, 3)),
        dma((2,)),
        dma((2, n)),
        dma((n,)),
        dma((2, n)),
        dma((n,)),
    ]
    any_space = pl.BlockSpec(memory_space=pl.ANY)
    result = pl.pallas_call(
        functools.partial(forward_kernel, n, groups),
        name="forward",
        out_shape=outs,
        in_specs=vmem_specs(5) + [any_space] * 10,
        out_specs=vmem_specs(20) + [any_space] + vmem_specs(16),
        scratch_shapes=scratch,
        compiler_params=pltpu.CompilerParams(
            collective_id=collective, has_side_effects=True, vmem_limit_bytes=65000 * 1024
        ),
    )(m_rows, x_rows.reshape(rows.shape), gains, docs, key_docs, *own, old, piece, compressed,
      memory.reshape(rows.shape))
    return result[:9], result[9:18], result[18:21], result[35:], result[21:28], result[28:35]


def backward_kernel(n, groups, home, *refs):
    (g_ref, x_ref, residual, hidden, fresh, wq, wkv, wo, wup, wdown, gains, q_ref, kv_ref,
     log_sum, docs, key_docs, normed, two, active, attended) = refs[:20]
    last = home == 0
    rest = refs[20:]
    if last:
        earlier_gains, padded, earlier, rest = rest[:2], rest[2], rest[3:11], rest[11:]
    dx_ref, shipped, d_fresh = rest[:3]
    results, gain_results, rest = rest[3:9], rest[9:11], rest[11:]
    grad_query, grad_key, grad_value, grad_out, grad_up, grad_down = results
    if last:
        grad_compress, rest = rest[0], rest[1:]
    d_hidden, d_branch, dq_ref, dkv_ref, d_residual, keys_docs, keys_t, sums = rest[:8]
    rest = rest[8:]
    first_scratch, second_scratch, fresh_scratch = rest[:7], rest[7:14], rest[14:21]
    tiles, grid_rest = rest[21], rest[22:28]
    ship_send, ship_recv = rest[28:30]
    gain_sums, gain_blocks, gain_send, gain_recv = rest[30:34]
    if last:
        fresh_all, padded_all, keep, keep_rows, fresh_sems, pad_sems, column_sems = rest[34:41]
    me = greet(n, True, groups, last)
    section = lax.axis_index("section")
    late = section == 1
    local = wq.shape[1]
    heads = local // HD
    gain_a = gains[0:1, :]
    gain_f = gains[1:2, :]
    scale = HD ** (-0.5)

    keys_docs[...] = jnp.broadcast_to(key_docs[...], keys_docs.shape)
    for head in range(heads):
        lanes = slice(head * HD, (head + 1) * HD)
        keys_t[head] = kv_ref[:, lanes].astype(f32).T.astype(bf16)

    def branch_middle(chunk, me, total):
        rows = g_ref[chunk, me].astype(f32) + rms_pull(total, residual[chunk], gain_f)
        d_residual[chunk] = rows
        return rows

    def input_middle(chunk, me, total):
        return d_residual[chunk] + rms_pull(total, x_ref[chunk, me].astype(f32), gain_a)

    def fresh_middle(chunk, me, total):
        return rms_pull(total, fresh[chunk, me].astype(f32), gain_a)

    first = make_line(n, me, branch_middle, d_branch, first_scratch)
    second = make_line(n, me, input_middle, dx_ref, second_scratch)
    third = make_line(n, me, fresh_middle, d_fresh, fresh_scratch)

    def produce(chunk):
        rows = slice(chunk * ROWS, (chunk + 1) * ROWS)
        grad = g_ref[chunk]
        d_active = dot_nt(grad.reshape(ROWS, grad.shape[-1]), wdown[...])
        block = (gelu_slope(hidden[rows, :]) * d_active).astype(bf16)
        d_hidden[rows, :] = block
        first.put(chunk, dot_nt(block, wup[...]))

    def attend_back(chunk):
        rows = slice(chunk * ROWS, (chunk + 1) * ROWS)
        d_attended = dot_nt(first.rows(chunk), wo[...]).astype(bf16)
        fresh_sum = chunk == CHUNKS - 1
        for head in range(heads):
            lanes = slice(head * HD, (head + 1) * HD)
            value_lanes = slice(local + head * HD, local + (head + 1) * HD)
            scores = score_columns(head, chunk, q_ref, kv_ref, docs, keys_docs)
            size = scores.shape[0]
            probs = jnp.exp(scores - log_sum[head : head + 1, rows])
            d_mixed = d_attended[:, lanes]
            d_values = dot_nn(probs.astype(bf16), d_mixed)
            d_probs = dot_nt(kv_ref[:size, value_lanes], d_mixed)
            inner = jnp.sum(d_probs * probs, axis=0, keepdims=True)
            d_scores = (probs * (d_probs - inner)).astype(bf16)
            d_keys = dot_nn(d_scores, q_ref[rows, lanes])
            d_queries = dot_nn(keys_t[head, :, :size], d_scores) * scale
            dq_ref[rows, lanes] = d_queries.T.astype(bf16)
            if fresh_sum:
                sums[:size, lanes] = d_keys
                sums[:size, value_lanes] = d_values
            else:
                sums[:size, lanes] += d_keys
                sums[:size, value_lanes] += d_values
        own = slice(CMEM + MEM + chunk * ROWS, CMEM + MEM + (chunk + 1) * ROWS)
        close_rows(own)
        second.put(
            chunk, dot_nt(dq_ref[rows, :], wq[...]) + dot_nt(dkv_ref[own, :], wkv[...])
        )
        if chunk == 0:
            close_rows(slice(0, CMEM + MEM))

            @pl.when(late)
            def _():
                count = third.part.shape[1] * third.part.shape[2]
                third.put(0, dot_nt(dkv_ref[FRESH_START : FRESH_START + count, :], wkv[...]))
                third.stage(0, 0)

    def close_rows(rows):
        dkv_ref[rows, :local] = (sums[rows, :local] * scale).astype(bf16)
        dkv_ref[rows, local:] = sums[rows, local:].astype(bf16)

    size = wq.shape[0] // groups
    wide = hidden.shape[1] // size
    up_at, down_at = 4, 4 + wide
    parts = [(down_at, down_at + wide), (up_at, down_at), (0, 2), (2, 4)]
    grid = GridSum(groups, home, tiles, grid_rest[:3], grid_rest[3:6], parts)
    half = groups // 2
    g_rows = g_ref.reshape(SEG, g_ref.shape[-1])
    two_rows = two.reshape(SEG, two.shape[-1])
    branch_rows = d_branch.reshape(SEG, d_branch.shape[-1])

    def each_block(start, stop, work):
        def body(block, carry):
            work(block, pl.ds(pl.multiple_of(block * size, size), size))
            return carry

        lax.fori_loop(start, stop, body, 0)

    def put_tiles(block, at, value):
        for tile in range(value.shape[1] // size):
            tiles[block, at + tile] = value[:, tile * size : (tile + 1) * size].astype(bf16)

    def down_block(block, lanes):
        put_tiles(block, down_at, dot_tn(g_rows[:, lanes], active[...]))

    def up_block(block, lanes):
        put_tiles(block, up_at, dot_tn(two_rows[:, lanes], d_hidden[...]))

    def small_block(block, lanes):
        put_tiles(block, 0, dot_tn(normed[CMEM + MEM :, lanes], dq_ref[...]))
        put_tiles(block, 1, dot_tn(branch_rows[:, lanes], attended[...]))

    def kv_block(block, lanes):
        put_tiles(block, 2, dot_tn(normed[:, lanes], dkv_ref[...]))

    share = pl.ds(pl.multiple_of(grid.dp * size, size), size)
    gain_sums[...] = jnp.zeros(gain_sums.shape, f32)

    def write(tile, value):
        if tile >= down_at:
            grad_down[(tile - down_at) * size : (tile - down_at + 1) * size, :] = value.T
        elif tile >= up_at:
            lanes = slice((tile - up_at) * size, (tile - up_at + 1) * size)
            grad_up[:, lanes] = value
            gain_sums[1] += wup[share, lanes].astype(f32) * value
        elif tile == 1:
            grad_out[...] = value.T
        elif tile == 0:
            grad_query[...] = value
            gain_sums[0] += wq[share, :].astype(f32) * value
        else:
            (grad_key, grad_value)[tile - 2][...] = value
            lanes = slice((tile - 2) * local, (tile - 1) * local)
            gain_sums[0] += wkv[share, lanes].astype(f32) * value

    gain_gather = LineGather(
        n, me, lambda block: gain_blocks.at[block], (gain_send, gain_recv)
    )

    first_slot = 2 * n - 2
    plan = {
        1: [lambda: each_block(0, half, down_block)],
        2: [lambda: each_block(half, groups, down_block), lambda: grid.send_core(0)],
        4: [lambda: each_block(0, half, up_block), lambda: grid.send_rows(0)],
        5: [lambda: each_block(half, groups, up_block), lambda: grid.send_core(1)],
        first_slot: [lambda: grid.send_rows(1)],
        first_slot + 1: [lambda: grid.send_section(0)],
        first_slot + 2: [lambda: grid.send_section(1)],
        first_slot + 3: [lambda: grid.close(0, write)],
        first_slot + 4: [lambda: each_block(0, groups, kv_block), lambda: grid.send_core(3)],
        first_slot + 5: [
            lambda: each_block(0, groups, small_block), lambda: grid.send_core(2),
            lambda: grid.send_rows(3),
        ],
        first_slot + 6: [lambda: grid.send_rows(2), lambda: grid.close(1, write)],
        first_slot + 7: [lambda: grid.send_section(3)],
        first_slot + 8: [lambda: grid.send_section(2)],
        first_slot + 9: [lambda: grid.close(3, write)],
    }

    def ship_copy(chunk):
        return pltpu.make_async_remote_copy(
            src_ref=dx_ref.at[chunk],
            dst_ref=shipped.at[1, chunk] if last else shipped.at[chunk],
            send_sem=ship_send.at[chunk],
            recv_sem=ship_recv.at[chunk],
            device_id={"section": 1 - section},
            device_id_type=MESH,
        )

    def finished(chunk):
        @pl.when(section != home)
        def _():
            ship_copy(chunk).start()

        if last:

            @pl.when(section == home)
            def _():
                keep_row(chunk).start()

    if last:
        earlier_shipped, earlier_fresh = earlier[6:]
        columns = pl.ds(pl.multiple_of(me * local, local), local)

        def keep_row(chunk):
            return pltpu.make_async_copy(
                dx_ref.at[chunk], shipped.at[0, chunk], keep_rows.at[chunk]
            )

        kept = [
            pltpu.make_async_copy(src, dst, keep.at[index])
            for index, (src, dst) in enumerate(zip(earlier[:6], results))
        ] + [
            pltpu.make_async_copy(earlier_shipped, shipped.at[0], keep.at[6]),
            pltpu.make_async_copy(g_ref, shipped.at[1], keep.at[7]),
            pltpu.make_async_copy(
                earlier_fresh.at[0, :, :, columns], fresh_all.at[grid.dp], keep.at[8]
            ),
        ]
        fresh_copy = pltpu.make_async_remote_copy(
            src_ref=d_fresh.at[0, :, :, columns],
            dst_ref=fresh_all.at[grid.dp],
            send_sem=fresh_sems.at[0],
            recv_sem=fresh_sems.at[1],
            device_id={"section": 1 - section},
            device_id_type=MESH,
        )

        @pl.when(late)
        def _():
            for copy in kept:
                copy.start()
            for index in range(2):
                gain_results[index][...] = earlier_gains[index][...]

        def pad_source(place, target):
            return padded.at[
                :, pl.ds(pl.multiple_of(place * wo.shape[1] + target * size, size), size)
            ]

        def pad_place(place, source):
            return padded_all.at[source, :, place * size : (place + 1) * size]

        def pad_copy(step, place, source):
            target = (grid.dp + step) % groups
            return pltpu.make_async_remote_copy(
                src_ref=pad_source(place, target),
                dst_ref=pad_place(place, source),
                send_sem=pad_sems.at[0, step - 1, place],
                recv_sem=pad_sems.at[1, step - 1, place],
                device_id={"dp": target},
                device_id_type=MESH,
            )

        def column_copy(step, source):
            return pltpu.make_async_remote_copy(
                src_ref=fresh_all.at[source],
                dst_ref=fresh_all.at[source],
                send_sem=column_sems.at[0, step - 1],
                recv_sem=column_sems.at[1, step - 1],
                device_id={"dp": (grid.dp + step) % groups},
                device_id_type=MESH,
            )

        pad_own = [
            pltpu.make_async_copy(
                pad_source(place, grid.dp), pad_place(place, grid.dp), keep.at[9 + place]
            )
            for place in range(RATE)
        ]
        for place in range(RATE):
            pad_own[place].start()
            for step in range(1, groups):
                pad_copy(step, place, grid.dp).start()

    def extra(slot):
        for action in plan.get(slot, ()):
            action()
        step = slot - (first_slot + CHUNKS - 1)
        if 0 < step < third.stages:

            @pl.when(late)
            def _():
                third.stage(0, step)

    run_two(
        list(range(CHUNKS - 1, -1, -1)), first, second, produce, attend_back, finished, extra,
    )
    if last:

        @pl.when(late)
        def _():
            fresh_copy.start()
            for copy in kept:
                copy.wait()

        @pl.when(section == home)
        def _():
            fresh_copy.wait_recv()

        for step in range(1, groups):
            column_copy(step, grid.dp).start()
    grid.close(2, write)

    @pl.when(section == home)
    def _():
        gain_blocks[me] = jnp.zeros(gain_blocks.shape[1:], f32)
        for index in range(2):
            gain_blocks[me, index : index + 1, :] = jnp.sum(
                gain_sums[index].T, axis=0, keepdims=True
            )
        gain_gather.start()

    @pl.when(section == home)
    def _():
        for step in range(1, n):
            gain_gather.forward(step)
        total = gain_blocks[0]
        for block in range(1, n):
            total = total + gain_blocks[block]
        for index in range(2):
            gain_results[index][...] = (
                total[index : index + 1, :] / gains[index : index + 1, share]
            )
        gain_gather.finish()

    if last:
        for step in range(1, groups):
            source = (grid.dp - step) % groups
            column_copy(step, source).wait_recv()
            for place in range(RATE):
                pad_copy(step, place, source).wait_recv()
        for copy in pad_own:
            copy.wait()
        count = padded.shape[0]
        for place in range(RATE):
            total = jnp.zeros(grad_compress.shape[1:], f32)
            for source in range(groups):
                total = total + dot_tn(
                    padded_all[source, :, place * size : (place + 1) * size],
                    fresh_all[source].reshape(count, local),
                )
            grad_compress[place] = total

    first.finish()
    second.finish()
    if last:
        for step in range(1, groups):
            column_copy(step, grid.dp).wait_send()
            for place in range(RATE):
                pad_copy(step, place, grid.dp).wait_send()
    grid.finish()
    for chunk in range(CHUNKS):

        @pl.when(section != home)
        def _():
            ship_copy(chunk).wait_send()

        @pl.when(section == home)
        def _():
            ship_copy(chunk).wait_recv()
            if last:
                keep_row(chunk).wait()

    @pl.when(late)
    def _():
        third.finish()
        if last:
            fresh_copy.wait_send()


def fresh_block(n):
    return -(-(CMEM - FRESH_START) // (16 * n)) * 16


def backward_layer(collective, n, groups, home, grad, x_rows, residual, hidden, fresh, weights,
                   gains, q, kv, log_sum, docs, key_docs, normed, two, active, attended,
                   earlier_gains=(), padded=[], earlier=[]):
    wq, wkv, wo, wup, wdown = weights
    width = wo.shape[1]
    local = wq.shape[1]
    block = ROWS // n
    size = width // groups
    inner = wup.shape[1]
    last = home == 0
    shape = jax.ShapeDtypeStruct
    any_space = pl.BlockSpec(memory_space=pl.ANY)
    rows = shape((CHUNKS, n, block, width), bf16)
    ship = shape((2,) + rows.shape, bf16) if last else rows
    fresh_shape = (n, fresh_block(n), width)
    outs = [rows, ship, shape((1,) + fresh_shape, bf16)]
    outs += [shape((size, local), f32)] * 3
    outs += [shape((local, size), f32), shape((size, inner), f32), shape((inner, size), f32)]
    outs += [shape((1, size), f32)] * 2
    out_specs = vmem_specs(1) + [any_space] + vmem_specs(9)
    tile_count = 4 + 2 * inner // size
    dma = pltpu.SemaphoreType.DMA
    if last:
        outs.append(shape((RATE, size, local), f32))
        out_specs += vmem_specs(1)
    return pl.pallas_call(
        functools.partial(backward_kernel, n, groups, home),
        name="backward_%d" % home,
        out_shape=outs,
        in_specs=vmem_specs(20 + len(earlier_gains)) + [any_space] * len(padded + earlier),
        out_specs=out_specs,
        scratch_shapes=[
            pltpu.VMEM((SEG, inner), bf16),
            pltpu.VMEM(rows.shape, bf16),
            pltpu.VMEM((SEG, local), bf16),
            pltpu.VMEM((CMEM + MEM + SEG, 2 * local), bf16),
            pltpu.VMEM((CHUNKS, block, width), f32),
            pltpu.VMEM((MEM + SEG, HD), jnp.int32),
            pltpu.VMEM((local // HD, HD, CMEM + MEM + SEG), bf16),
            pltpu.VMEM((CMEM + MEM + SEG, 2 * local), f32),
        ]
        + line_scratch(CHUNKS, n, block, width)
        + line_scratch(CHUNKS, n, block, width)
        + line_scratch(1, n, fresh_block(n), width)
        + grid_scratch(groups, tile_count, size, 4)
        + [dma((CHUNKS,))] * 2
        + [pltpu.VMEM((2, size, size), f32), pltpu.VMEM((n, 8, size), f32), dma((2, n)), dma((n,))]
        + (
            [
                pltpu.VMEM((groups, n, fresh_block(n), local), bf16),
                pltpu.VMEM((groups, n * fresh_block(n), RATE * size), bf16),
                dma((9 + RATE,)),
                dma((CHUNKS,)),
                dma((2,)),
                dma((2, groups - 1, RATE)),
                dma((2, groups - 1)),
            ]
            if last
            else []
        ),
        compiler_params=pltpu.CompilerParams(
            collective_id=collective, has_side_effects=True, vmem_limit_bytes=65000 * 1024
        ),
    )(grad.reshape(rows.shape), x_rows.reshape(rows.shape), residual, hidden, fresh,
      wq, wkv, wo, wup, wdown, gains, q, kv, log_sum, docs, key_docs, normed, two, active,
      attended, *earlier_gains, *padded, *earlier)


def keep_kernel(count, *refs):
    small_in, big_in, refs = refs[:2], refs[2 : 2 + count], refs[2 + count :]
    small_out, big_out, refs = refs[:2], refs[2 : 2 + count], refs[2 + count :]
    held, sems = refs[:count], refs[count]
    taken = [
        pltpu.make_async_copy(big_in[i], held[i], sems.at[0, i]) for i in range(count)
    ]
    given = [
        pltpu.make_async_copy(held[i], big_out[i], sems.at[1, i]) for i in range(count)
    ]
    for copy in taken:
        copy.start()
    for i in range(2):
        small_out[i][...] = small_in[i][...]
    for i in range(count):
        taken[i].wait()
        given[i].start()
    for copy in given:
        copy.wait()


def keep_results(small, big):
    any_space = pl.BlockSpec(memory_space=pl.ANY)
    count = len(big)
    arrays = small + big
    return pl.pallas_call(
        functools.partial(keep_kernel, count),
        name="keep_results",
        out_shape=[jax.ShapeDtypeStruct(x.shape, x.dtype) for x in arrays],
        in_specs=vmem_specs(2) + [any_space] * count,
        out_specs=vmem_specs(2) + [any_space] * count,
        scratch_shapes=[pltpu.VMEM(x.shape, x.dtype) for x in big]
        + [pltpu.SemaphoreType.DMA((2, count))],
        compiler_params=pltpu.CompilerParams(vmem_limit_bytes=65000 * 1024),
    )(*arrays)


def project(rows, weight):
    return jnp.dot(rows, weight, preferred_element_type=f32).astype(bf16)


def shards(
    block_input,
    doc_ids,
    memory,
    compressed,
    gain_attn,
    w_query,
    w_key,
    w_value,
    w_out,
    gain_ffn,
    w_up,
    w_down,
    w_compress,
    cotangent,
):
    section = lax.axis_index("section")
    first = section == 0
    n = lax.axis_size("tensor")
    groups = lax.axis_size("dp")
    tensor_index = lax.axis_index("tensor")
    width = block_input.shape[2]
    local = w_query.shape[2]
    gains = jnp.stack([gain_attn[0], gain_ffn[0]])

    history = doc_ids[0]
    memory_docs = lax.dynamic_slice_in_dim(history, section * SEG, MEM, 0)
    token_docs = lax.dynamic_slice_in_dim(history, MEM + section * SEG, SEG, 0)
    docs = token_docs[None]
    key_docs = jnp.concatenate([memory_docs, token_docs])[:, None]
    tokens = lax.dynamic_slice_in_dim(block_input[0], section * SEG, SEG, 0)
    grad_now = lax.dynamic_slice_in_dim(cotangent[0], section * SEG, SEG, 0)

    fresh_count = n * fresh_block(n)
    lead = OLD_ROWS - FRESH_START
    trail = fresh_count - lead - COMP_ROWS
    padded = jnp.concatenate(
        [
            jnp.zeros((RATE * lead + PAD, width), bf16),
            memory[0, 0],
            jnp.zeros((RATE * trail, width), bf16),
        ]
    ).reshape(fresh_count, RATE * width)
    fresh_piece = project(padded, w_compress[0].reshape(RATE * width, local))
    fresh_piece = fresh_piece[lead : lead + COMP_ROWS]
    kept = compressed[0, 0, COMP_ROWS + SPLIT_START :]
    piece = jnp.concatenate(
        [lax.dynamic_slice_in_dim(kept, tensor_index * local, local, 1), fresh_piece]
    )
    old = compressed[0, 0, COMP_ROWS : COMP_ROWS + FRESH_START]
    m_rows = jnp.where(first, memory[0, 0], block_input[0, :SEG])

    own = (w_query[0], w_key[0], w_value[0], w_out[0], w_up[0], w_down[0])
    low, high, (middle, _, outputs), fresh_rows, *layers = forward(
        1, n, groups, m_rows, tokens, gains, docs, key_docs, own, old, piece, compressed[0, 0],
        memory[0, 0],
    )
    outputs = outputs.reshape(2 * SEG, width)
    saved = [
        (tokens, *low),
        (middle.reshape(SEG, width), *high),
    ]
    weight_layers = [layer[:5] for layer in layers]
    gains_by_layer = [layer[5] for layer in layers]

    handed = []
    for layer in (1, 0):
        (tokens, normed, queries, kv, log_total, attended, residual, two, hidden,
         active) = saved[layer]
        result = backward_layer(
            4 + layer, n, groups, layer, grad_now, tokens, residual, hidden,
            fresh_rows[layer],
            weight_layers[layer], gains_by_layer[layer], queries, kv, log_total, docs, key_docs,
            normed, two, active, attended, *handed,
        )
        dx, shipped, d_fresh, *grads = result
        grad_now = dx.reshape(SEG, width)
        handed = [grads[6:8], [padded], grads[:6] + [shipped, d_fresh]]

    gain_attn_grad, gain_ffn_grad, *kept = keep_results(
        grads[6:8], [outputs, shipped.reshape(2 * SEG, width), *grads[:6], grads[8]]
    )
    outputs, input_grads, grad_query, grad_key, grad_value, grad_out, grad_up, grad_down = kept[:8]
    return (
        outputs[None, None],
        input_grads[None, None],
        gain_attn_grad,
        grad_query[None],
        grad_key[None],
        grad_value[None],
        grad_out[None],
        gain_ffn_grad,
        grad_up[None],
        grad_down[None],
        kept[8][None],
    )


def solution(mesh):
    return jax.shard_map(
        shards,
        mesh=mesh,
        in_specs=(
            P("dp", None, None),
            P("dp", None),
            P("section", "dp", None, None),
            P("section", "dp", None, None),
            P("section", None),
            P("section", None, "tensor"),
            P("section", None, "tensor"),
            P("section", None, "tensor"),
            P("section", "tensor", None),
            P("section", None),
            P("section", None, "tensor"),
            P("section", "tensor", None),
            P("section", None, None, "tensor"),
            P("dp", None, None),
        ),
        out_specs=(
            P("section", "dp", None, None),
            P("section", "dp", None, None),
            P("section", "dp"),
            P("section", "dp", "tensor"),
            P("section", "dp", "tensor"),
            P("section", "dp", "tensor"),
            P("section", "tensor", "dp"),
            P("section", "dp"),
            P("section", "dp", "tensor"),
            P("section", "tensor", "dp"),
            P("section", None, "dp", "tensor"),
        ),
        check_vma=False,
    )
```
